256 devices in a mesh: tm: 32 (over x, y, core), sky: 8 (over z).
Axes of the slice: x: 4, y: 4, z: 8, core: 2. Of those that a mesh axis runs over, the one named last changes fastest.
Arguments:
- residuals: bfloat16 [128, 512, 2048], P('tm', None, 'sky')
- seg_counts: int32 [128], P('tm'), may hold values from 256 to 512, as said below
- attitude: bfloat16 [128, 512, 512], P('tm', 'sky')
- sched_seg: int32 [2048, 256], P(('tm', 'sky')), may hold values from 0 to 127, as said below
- sched_slot: int32 [2048, 256], P(('tm', 'sky')), may hold values from 0 to 511, as said below
- periods: int32 [1024], replicated, may hold values from 16 to 16383
Outputs:
- cleaned: float32 [128, 512, 2048], P('tm', None, 'sky')
- log_evidence: float32 [2048, 128], P(('tm', 'sky'))
The draws below stay inside these ranges and needn't reach their ends.
Inputs may be any that keep to these rules, and one draw needn't show every extreme that they name: `seg_counts`: every segment has between 256 and 512 observed slots; some segment has all 512. `sched_seg`: in each aligned block of 8 rows (the plans of one device) at most 128 entries fall in the segments of one index of tm, and in every block some index receives exactly 128. `sched_slot`: each slot is below the observed count of its segment.
All inputs are finite; a program needn't handle non-finite values.
Results may differ from the reference program's by a relative error of at most 0.035.
Values may be sent and summed in bfloat16 or wider, within the bound.
A program may use at most 128 MiB of HBM per device.

```python
import jax
import jax.numpy as jnp
from jax import lax

SLOTS = 512
NPER = 1024
OBS = 256
SRC_GROUP = 128
NCB = 2
ITERS = 2
SEG_DEV = 4
SCHED_DEV = 8
SEGMENTS = 128
COLS = 2048
PLANS = 2048
N_SKY = 8


def count_table(key):
    first, second = jax.random.split(key)
    values = jax.random.randint(first, (SEGMENTS,), SLOTS // 2, SLOTS + 1)
    spot = jax.random.randint(second, (), 0, SEGMENTS)
    return jnp.where(jnp.arange(SEGMENTS) == spot, SLOTS, values).astype(jnp.int32)


def period_table(key):
    return jax.random.randint(key, (NPER,), 16, 16384).astype(jnp.int32)


def plan_table(key):
    counts = count_table(jax.random.fold_in(key, 11))
    owners = SEGMENTS // SEG_DEV
    blocks = PLANS // SCHED_DEV
    wanted = SCHED_DEV * OBS
    mean = wanted // owners
    rank = jnp.arange(owners)
    profile = jnp.where(rank < owners // 4, 2 * mean, jnp.where(rank < owners // 2, mean, mean // 2))

    def single(block_key):
        key_a, key_b, key_c, key_d = jax.random.split(block_key, 4)
        loads = profile[jax.random.permutation(key_a, owners)]
        bounds = jnp.cumsum(loads)
        target = jnp.searchsorted(bounds, jnp.arange(wanted), side='right').astype(jnp.int32)
        target = jax.random.permutation(key_b, target)
        segment = target * SEG_DEV + jax.random.randint(key_c, (wanted,), 0, SEG_DEV)
        raw = jax.random.randint(key_d, (wanted,), 0, 1 << 20)
        slot = raw * counts[segment] // (1 << 20)
        return (segment.reshape(SCHED_DEV, OBS), slot.reshape(SCHED_DEV, OBS))
    segs, slots = jax.vmap(single)(jax.random.split(jax.random.fold_in(key, 23), blocks))
    return (segs.reshape(PLANS, OBS).astype(jnp.int32), slots.reshape(PLANS, OBS).astype(jnp.int32))


def draw_seg_counts(key, part):
    return count_table(jax.random.fold_in(key, 11))


def draw_periods(key, part):
    return period_table(jax.random.fold_in(key, 31))


def draw_sched_seg(key, part):
    return plan_table(key)[0]


def draw_sched_slot(key, part):
    return plan_table(key)[1]


def draw_attitude(key, part):
    first = jax.random.fold_in(jax.random.fold_in(key, 53), 0)
    ident = (jnp.arange(SLOTS)[:, None] == jnp.arange(SLOTS)[None, :]).astype(jnp.float32)
    noise = 0.5 * jax.random.normal(first, (SEGMENTS, SLOTS, SLOTS)) / SLOTS ** 0.5
    return (ident[None] + noise).astype(jnp.bfloat16)


def draw_residuals(key, part):
    base = jax.random.normal(jax.random.fold_in(key, 41), (SEGMENTS, SLOTS, COLS))
    return base.astype(jnp.bfloat16)


def setup_inputs(seed: int = 0) -> dict:
    splits = jax.random.split(jax.random.key(seed), 7)
    residuals = draw_residuals(jax.random.fold_in(splits[6], 71), 0)
    seg_counts = draw_seg_counts(jax.random.fold_in(splits[6], 71), 0)
    attitude = draw_attitude(jax.random.fold_in(splits[6], 71), 0)
    sched_seg = draw_sched_seg(jax.random.fold_in(splits[6], 71), 0)
    sched_slot = draw_sched_slot(jax.random.fold_in(splits[6], 71), 0)
    periods = draw_periods(jax.random.fold_in(splits[6], 71), 0)
    return {"residuals": residuals, "seg_counts": seg_counts, "attitude": attitude, "sched_seg": sched_seg, "sched_slot": sched_slot, "periods": periods}


TWO_PI = 6.283185307179586
BETA = 2.0
RIDGE = 1.0


def make_basis(times, periods):
    period_float = periods.astype(jnp.float32)
    phase = (times[:, None] % periods[None, :]).astype(jnp.float32) * (TWO_PI / period_float)[None, :]
    return jnp.concatenate([jnp.cos(phase), jnp.sin(phase)], axis=1).astype(jnp.bfloat16)


def fit_group(basis, observed):
    squares = basis.astype(jnp.float32) ** 2
    norm_cos = jnp.sum(squares[:, :NPER], axis=0) + RIDGE
    norm_sin = jnp.sum(squares[:, NPER:], axis=0) + RIDGE
    corr = jnp.dot(basis.T, observed, preferred_element_type=jnp.float32)
    cosine = corr[:NPER]
    sine = corr[NPER:]
    amp_c = cosine / norm_cos[:, None]
    amp_s = sine / norm_sin[:, None]
    power = cosine * amp_c + sine * amp_s
    logits = BETA * power
    highest = jnp.max(logits, axis=0)
    expo = jnp.exp(logits - highest[None, :])
    total = jnp.sum(expo, axis=0)
    share = expo / total[None, :]
    coeff = jnp.concatenate([share * amp_c, share * amp_s], axis=0).astype(jnp.bfloat16)
    model = jnp.dot(basis, coeff, preferred_element_type=jnp.float32)
    return model, highest + jnp.log(total)


def reference(residuals, seg_counts, attitude, sched_seg, sched_slot, periods):
    valid = jnp.arange(SLOTS, dtype=jnp.int32)[None, :] < seg_counts[:, None]
    index = jnp.arange(PLANS, dtype=jnp.int32)
    region = (index // SCHED_DEV) % N_SKY
    block = (index % SCHED_DEV) % NCB
    first = ((region * NCB + block) * SRC_GROUP).astype(jnp.int32)
    columns = jnp.arange(SRC_GROUP, dtype=jnp.int32)
    current = residuals.astype(jnp.float32)
    evidence = jnp.zeros((PLANS, SRC_GROUP), jnp.float32)
    for iteration in range(ITERS):
        masked = jnp.where(valid[:, :, None], current, 0.0).astype(jnp.bfloat16)
        white = lax.map(lambda pair: jnp.dot(pair[0], pair[1], preferred_element_type=jnp.float32).astype(jnp.bfloat16), (attitude, masked))

        def visit(placed, item):
            seg_row, slot_row, start = item
            cols = start + columns
            observed = white[seg_row[:, None], slot_row[:, None], cols[None, :]]
            basis = make_basis(seg_row * SLOTS + slot_row, periods)
            model, score = fit_group(basis, observed)
            placed = placed.at[seg_row[:, None], slot_row[:, None], cols[None, :]].add(model.astype(jnp.float32))
            return placed, score

        placed, evidence = lax.scan(visit, jnp.zeros(current.shape, jnp.float32), (sched_seg, sched_slot, first))
        current = current - placed
    return current, evidence
```

```python
import jax
import jax.numpy as jnp
from jax import lax
from jax.experimental import pallas as pl
from jax.sharding import PartitionSpec as P

SRC_GROUP = 128
ITERS = 2


TWO_PI = 6.283185307179586
BETA = 2.0
RIDGE = 1.0


PIO2_1 = 1.5703125
PIO2_2 = 4.837512969970703125e-4
PIO2_3 = 7.549789954891e-8
ROWS = 16
LANES = 128


def basis_kernel(t_ref, p_ref, w_ref, inv_ref, basis_ref, nc_ref, ns_ref):
    obs = t_ref.shape[0]
    nper = p_ref.shape[1]

    def lane_block(j, carry):
        c0 = pl.multiple_of(j * LANES, LANES)
        pf = p_ref[:, pl.ds(c0, LANES)]
        w = w_ref[:, pl.ds(c0, LANES)]
        inv = inv_ref[:, pl.ds(c0, LANES)]

        def row_block(i, acc):
            acc_c, acc_s = acc
            r0 = pl.multiple_of(i * ROWS, ROWS)
            tf = jnp.broadcast_to(t_ref[pl.ds(r0, ROWS), :], (ROWS, LANES))
            q = jnp.floor(tf * inv)
            r = tf - q * pf
            r = jnp.where(r < 0.0, r + pf, r)
            r = jnp.where(r >= pf, r - pf, r)
            phase = r * w
            k = jnp.floor(phase * 0.6366197723675814 + 0.5)
            y = ((phase - k * PIO2_1) - k * PIO2_2) - k * PIO2_3
            z = y * y
            s = y + y * z * (-1.6666654611e-1 + z * (8.3321608736e-3 + z * -1.9515295891e-4))
            c = 1.0 - 0.5 * z + z * z * (4.166664568298827e-2 + z * (-1.388731625493765e-3 + z * 2.443315711809948e-5))
            odd = (k == 1.0) | (k == 3.0)
            cs = jnp.where(odd, s, c)
            sn = jnp.where(odd, c, s)
            cos_v = jnp.where((k == 1.0) | (k == 2.0), -cs, cs).astype(jnp.bfloat16)
            sin_v = jnp.where((k == 2.0) | (k == 3.0), -sn, sn).astype(jnp.bfloat16)
            basis_ref[pl.ds(r0, ROWS), pl.ds(c0, LANES)] = cos_v
            basis_ref[pl.ds(r0, ROWS), pl.ds(nper + c0, LANES)] = sin_v
            cf = cos_v.astype(jnp.float32)
            sf = sin_v.astype(jnp.float32)
            return acc_c + cf * cf, acc_s + sf * sf

        zero = jnp.zeros((ROWS, LANES), jnp.float32)
        acc_c, acc_s = lax.fori_loop(0, obs // ROWS, row_block, (zero, zero))
        nc_ref[:, pl.ds(c0, LANES)] = jnp.sum(acc_c, axis=0, keepdims=True) + RIDGE
        ns_ref[:, pl.ds(c0, LANES)] = jnp.sum(acc_s, axis=0, keepdims=True) + RIDGE
        return carry

    lax.fori_loop(0, nper // LANES, lane_block, 0)


def basis_and_norms(times, periods):
    plans, obs = times.shape
    nper = periods.shape[0]
    pf = periods.astype(jnp.float32)
    w = (TWO_PI / pf).reshape(1, nper)
    inv = (1.0 / pf).reshape(1, nper)
    pf = pf.reshape(1, nper)
    tf = times.astype(jnp.float32).reshape(plans, obs, 1)
    row = pl.BlockSpec((1, nper), lambda g: (0, 0))
    basis, nc, ns = pl.pallas_call(
        basis_kernel,
        grid=(plans,),
        in_specs=[pl.BlockSpec((None, obs, 1), lambda g: (g, 0, 0)), row, row, row],
        out_specs=[
            pl.BlockSpec((None, obs, 2 * nper), lambda g: (g, 0, 0)),
            pl.BlockSpec((None, 1, nper), lambda g: (g, 0, 0)),
            pl.BlockSpec((None, 1, nper), lambda g: (g, 0, 0)),
        ],
        out_shape=[
            jax.ShapeDtypeStruct((plans, obs, 2 * nper), jnp.bfloat16),
            jax.ShapeDtypeStruct((plans, 1, nper), jnp.float32),
            jax.ShapeDtypeStruct((plans, 1, nper), jnp.float32),
        ],
        cost_estimate=pl.CostEstimate(
            flops=60 * plans * obs * nper, transcendentals=0,
            bytes_accessed=plans * obs * 2 * nper * 2),
    )(tf, pf, w, inv)
    return basis, nc.reshape(plans, nper), ns.reshape(plans, nper)


def fit_groups(basis, observed, norm_cos, norm_sin, nper):
    corr = jnp.einsum("fio,fic->foc", basis, observed, preferred_element_type=jnp.float32)
    cosine = corr[:, :nper]
    sine = corr[:, nper:]
    amp_c = cosine / norm_cos[:, :, None]
    amp_s = sine / norm_sin[:, :, None]
    power = cosine * amp_c + sine * amp_s
    logits = BETA * power
    highest = jnp.max(logits, axis=1)
    expo = jnp.exp(logits - highest[:, None, :])
    total = jnp.sum(expo, axis=1)
    share = expo / total[:, None, :]
    coeff = jnp.concatenate([share * amp_c, share * amp_s], axis=1).astype(jnp.bfloat16)
    model = jnp.einsum("fio,foc->fic", basis, coeff, preferred_element_type=jnp.float32)
    return (model, highest + jnp.log(total))


def on_device(residuals, seg_counts, attitude, sched_seg, sched_slot, periods):
    tm_count = lax.axis_size("tm")
    sched_dev, obs = sched_seg.shape
    seg_dev, slots, width = residuals.shape
    nper = periods.shape[0]
    column_blocks = width // SRC_GROUP
    capacity = 2 * sched_dev * obs // tm_count
    requests = sched_dev * obs
    seg_flat = sched_seg.reshape(-1)
    slot_flat = sched_slot.reshape(-1)
    block_of = jnp.repeat(jnp.arange(sched_dev, dtype=jnp.int32) % column_blocks, obs)
    target = seg_flat // seg_dev
    local_row = (seg_flat % seg_dev * slots + slot_flat) * column_blocks + block_of
    onehot = (target[:, None] == jnp.arange(tm_count, dtype=jnp.int32)[None, :]).astype(jnp.int32)
    position = jnp.sum(jnp.cumsum(onehot, axis=0) * onehot, axis=1) - 1
    empty_row = seg_dev * slots * column_blocks
    wanted = (
        jnp.full((tm_count, capacity), empty_row, jnp.int32).at[target, position].set(local_row)
    )
    asked = lax.all_to_all(wanted, "tm", split_axis=0, concat_axis=0, tiled=True)
    basis, norm_cos, norm_sin = basis_and_norms(sched_seg * slots + sched_slot, periods)
    valid = jnp.arange(slots, dtype=jnp.int32)[None, :] < seg_counts[:, None]
    current = residuals.astype(jnp.float32)
    evidence = jnp.zeros((sched_dev, SRC_GROUP), jnp.float32)
    for iteration in range(ITERS):
        masked = jnp.where(valid[:, :, None], current, 0.0).astype(jnp.bfloat16)
        white = jnp.einsum(
            "sij,sjc->sic",
            lax.all_gather(attitude, "sky", axis=1, tiled=True),
            masked,
            preferred_element_type=jnp.float32,
        ).astype(jnp.bfloat16)
        flat = white.reshape(-1, SRC_GROUP)
        picked = jnp.take(flat, asked, axis=0, mode="fill", fill_value=0)
        arrived = lax.all_to_all(picked, "tm", split_axis=0, concat_axis=0, tiled=True)
        observed = arrived[target, position].reshape(sched_dev, obs, SRC_GROUP)
        model, evidence = fit_groups(basis, observed, norm_cos, norm_sin, nper)
        outgoing = (
            jnp.zeros((tm_count, capacity, SRC_GROUP), jnp.float32)
            .at[target, position]
            .set(model.reshape(requests, SRC_GROUP))
        )
        returned = lax.all_to_all(outgoing, "tm", split_axis=0, concat_axis=0, tiled=True)
        placed = (
            jnp.zeros((empty_row, SRC_GROUP), jnp.float32)
            .at[asked.reshape(-1)]
            .add(returned.reshape(-1, SRC_GROUP), mode="drop")
        )
        current = current - placed.reshape(seg_dev, slots, width)
    return (current, evidence)


def solution(mesh):
    in_specs = (
        P("tm", None, "sky"),
        P("tm"),
        P("tm", "sky", None),
        P(("tm", "sky"), None),
        P(("tm", "sky"), None),
        P(),
    )
    out_specs = (P("tm", None, "sky"), P(("tm", "sky"), None))
    return jax.shard_map(
        on_device, mesh=mesh, in_specs=in_specs, out_specs=out_specs, check_vma=False
    )
```

```python
import jax
import jax.numpy as jnp
from jax import lax
from jax.experimental import pallas as pl
from jax.sharding import PartitionSpec as P

SRC_GROUP = 128
ITERS = 2


TWO_PI = 6.283185307179586
BETA = 2.0
RIDGE = 1.0


PIO2_1 = 1.5703125
PIO2_2 = 4.837512969970703125e-4
PIO2_3 = 7.549789954891e-8
ROWS = 16
LANES = 512
UNROLL = 2


def basis_kernel(t_ref, p_ref, w_ref, inv_ref, basis_ref, nc_ref, ns_ref):
    obs = t_ref.shape[0]
    nper = p_ref.shape[1]

    def lane_block(j, carry):
        c0 = pl.multiple_of(j * LANES, LANES)
        pf = p_ref[:, pl.ds(c0, LANES)]
        w = w_ref[:, pl.ds(c0, LANES)]
        inv = inv_ref[:, pl.ds(c0, LANES)]

        def row_block(i, acc):
            acc_c, acc_s = acc
            r0 = pl.multiple_of(i * ROWS, ROWS)
            tf = jnp.broadcast_to(t_ref[pl.ds(r0, ROWS), :], (ROWS, LANES))
            q = jnp.floor(tf * inv)
            r = tf - q * pf
            r = jnp.where(r < 0.0, r + pf, r)
            r = jnp.where(r >= pf, r - pf, r)
            phase = r * w
            k = jnp.floor(phase * 0.6366197723675814 + 0.5)
            y = ((phase - k * PIO2_1) - k * PIO2_2) - k * PIO2_3
            z = y * y
            s = y + y * z * (-1.6666654611e-1 + z * (8.3321608736e-3 + z * -1.9515295891e-4))
            c = 1.0 - 0.5 * z + z * z * (4.166664568298827e-2 + z * (-1.388731625493765e-3 + z * 2.443315711809948e-5))
            odd = (k == 1.0) | (k == 3.0)
            cs = jnp.where(odd, s, c)
            sn = jnp.where(odd, c, s)
            cos_v = jnp.where((k == 1.0) | (k == 2.0), -cs, cs).astype(jnp.bfloat16)
            sin_v = jnp.where((k == 2.0) | (k == 3.0), -sn, sn).astype(jnp.bfloat16)
            basis_ref[pl.ds(r0, ROWS), pl.ds(c0, LANES)] = cos_v
            basis_ref[pl.ds(r0, ROWS), pl.ds(nper + c0, LANES)] = sin_v
            cf = cos_v.astype(jnp.float32)
            sf = sin_v.astype(jnp.float32)
            return acc_c + cf * cf, acc_s + sf * sf

        zero = jnp.zeros((ROWS, LANES), jnp.float32)
        acc_c, acc_s = lax.fori_loop(0, obs // ROWS, row_block, (zero, zero), unroll=UNROLL)
        nc_ref[:, pl.ds(c0, LANES)] = jnp.sum(acc_c, axis=0, keepdims=True) + RIDGE
        ns_ref[:, pl.ds(c0, LANES)] = jnp.sum(acc_s, axis=0, keepdims=True) + RIDGE
        return carry

    lax.fori_loop(0, nper // LANES, lane_block, 0)


def basis_and_norms(times, periods):
    plans, obs = times.shape
    nper = periods.shape[0]
    pf = periods.astype(jnp.float32)
    w = (TWO_PI / pf).reshape(1, nper)
    inv = (1.0 / pf).reshape(1, nper)
    pf = pf.reshape(1, nper)
    tf = times.astype(jnp.float32).reshape(plans, obs, 1)
    row = pl.BlockSpec((1, nper), lambda g: (0, 0))
    basis, nc, ns = pl.pallas_call(
        basis_kernel,
        grid=(plans,),
        in_specs=[pl.BlockSpec((None, obs, 1), lambda g: (g, 0, 0)), row, row, row],
        out_specs=[
            pl.BlockSpec((None, obs, 2 * nper), lambda g: (g, 0, 0)),
            pl.BlockSpec((None, 1, nper), lambda g: (g, 0, 0)),
            pl.BlockSpec((None, 1, nper), lambda g: (g, 0, 0)),
        ],
        out_shape=[
            jax.ShapeDtypeStruct((plans, obs, 2 * nper), jnp.bfloat16),
            jax.ShapeDtypeStruct((plans, 1, nper), jnp.float32),
            jax.ShapeDtypeStruct((plans, 1, nper), jnp.float32),
        ],
        cost_estimate=pl.CostEstimate(
            flops=60 * plans * obs * nper, transcendentals=0,
            bytes_accessed=plans * obs * 2 * nper * 2),
    )(tf, pf, w, inv)
    return basis, nc.reshape(plans, nper), ns.reshape(plans, nper)


def fit_groups(basis, observed, norm_cos, norm_sin, nper):
    corr = jnp.einsum("fio,fic->foc", basis, observed, preferred_element_type=jnp.float32)
    cosine = corr[:, :nper]
    sine = corr[:, nper:]
    amp_c = cosine / norm_cos[:, :, None]
    amp_s = sine / norm_sin[:, :, None]
    power = cosine * amp_c + sine * amp_s
    logits = BETA * power
    highest = jnp.max(logits, axis=1)
    expo = jnp.exp(logits - highest[:, None, :])
    total = jnp.sum(expo, axis=1)
    share = expo / total[:, None, :]
    coeff = jnp.concatenate([share * amp_c, share * amp_s], axis=1).astype(jnp.bfloat16)
    model = jnp.einsum("fio,foc->fic", basis, coeff, preferred_element_type=jnp.float32)
    return (model, highest + jnp.log(total))


def on_device(residuals, seg_counts, attitude, sched_seg, sched_slot, periods):
    tm_count = lax.axis_size("tm")
    sched_dev, obs = sched_seg.shape
    seg_dev, slots, width = residuals.shape
    nper = periods.shape[0]
    column_blocks = width // SRC_GROUP
    capacity = 2 * sched_dev * obs // tm_count
    requests = sched_dev * obs
    seg_flat = sched_seg.reshape(-1)
    slot_flat = sched_slot.reshape(-1)
    block_of = jnp.repeat(jnp.arange(sched_dev, dtype=jnp.int32) % column_blocks, obs)
    target = seg_flat // seg_dev
    local_row = (seg_flat % seg_dev * slots + slot_flat) * column_blocks + block_of
    onehot = (target[:, None] == jnp.arange(tm_count, dtype=jnp.int32)[None, :]).astype(jnp.int32)
    position = jnp.sum(jnp.cumsum(onehot, axis=0) * onehot, axis=1) - 1
    empty_row = seg_dev * slots * column_blocks
    wanted = (
        jnp.full((tm_count, capacity), empty_row, jnp.int32).at[target, position].set(local_row)
    )
    asked = lax.all_to_all(wanted, "tm", split_axis=0, concat_axis=0, tiled=True)
    basis, norm_cos, norm_sin = basis_and_norms(sched_seg * slots + sched_slot, periods)
    valid = jnp.arange(slots, dtype=jnp.int32)[None, :] < seg_counts[:, None]
    current = residuals.astype(jnp.float32)
    evidence = jnp.zeros((sched_dev, SRC_GROUP), jnp.float32)
    for iteration in range(ITERS):
        masked = jnp.where(valid[:, :, None], current, 0.0).astype(jnp.bfloat16)
        white = jnp.einsum(
            "sij,sjc->sic",
            lax.all_gather(attitude, "sky", axis=1, tiled=True),
            masked,
            preferred_element_type=jnp.float32,
        ).astype(jnp.bfloat16)
        flat = white.reshape(-1, SRC_GROUP)
        picked = jnp.take(flat, asked, axis=0, mode="fill", fill_value=0)
        arrived = lax.all_to_all(picked, "tm", split_axis=0, concat_axis=0, tiled=True)
        observed = arrived[target, position].reshape(sched_dev, obs, SRC_GROUP)
        model, evidence = fit_groups(basis, observed, norm_cos, norm_sin, nper)
        outgoing = (
            jnp.zeros((tm_count, capacity, SRC_GROUP), jnp.bfloat16)
            .at[target, position]
            .set(model.reshape(requests, SRC_GROUP).astype(jnp.bfloat16))
        )
        returned = lax.all_to_all(outgoing, "tm", split_axis=0, concat_axis=0, tiled=True)
        placed = (
            jnp.zeros((empty_row, SRC_GROUP), jnp.float32)
            .at[asked.reshape(-1)]
            .add(returned.reshape(-1, SRC_GROUP).astype(jnp.float32), mode="drop")
        )
        current = current - placed.reshape(seg_dev, slots, width)
    return (current, evidence)


def solution(mesh):
    in_specs = (
        P("tm", None, "sky"),
        P("tm"),
        P("tm", "sky", None),
        P(("tm", "sky"), None),
        P(("tm", "sky"), None),
        P(),
    )
    out_specs = (P("tm", None, "sky"), P(("tm", "sky"), None))
    return jax.shard_map(
        on_device, mesh=mesh, in_specs=in_specs, out_specs=out_specs, check_vma=False
    )
```

```python
import jax
import jax.numpy as jnp
from jax import lax
from jax.experimental import pallas as pl
from jax.experimental.pallas import tpu as pltpu
from jax.sharding import PartitionSpec as P

SRC_GROUP = 128
ITERS = 2


TWO_PI = 6.283185307179586
BETA = 2.0
RIDGE = 1.0


PIO2_1 = 1.5703125
PIO2_2 = 4.837512969970703125e-4
PIO2_3 = 7.549789954891e-8
ROWS = 16
LANES = 512
UNROLL = 2


def basis_kernel(t_ref, p_ref, w_ref, inv_ref, basis_ref, nc_ref, ns_ref):
    obs = t_ref.shape[0]
    nper = p_ref.shape[1]

    def lane_block(j, carry):
        c0 = pl.multiple_of(j * LANES, LANES)
        pf = p_ref[:, pl.ds(c0, LANES)]
        w = w_ref[:, pl.ds(c0, LANES)]
        inv = inv_ref[:, pl.ds(c0, LANES)]

        def row_block(i, acc):
            acc_c, acc_s = acc
            r0 = pl.multiple_of(i * ROWS, ROWS)
            tf = jnp.broadcast_to(t_ref[pl.ds(r0, ROWS), :], (ROWS, LANES))
            q = jnp.floor(tf * inv)
            r = tf - q * pf
            r = jnp.where(r < 0.0, r + pf, r)
            r = jnp.where(r >= pf, r - pf, r)
            phase = r * w
            k = jnp.floor(phase * 0.6366197723675814 + 0.5)
            y = ((phase - k * PIO2_1) - k * PIO2_2) - k * PIO2_3
            z = y * y
            s = y + y * z * (-1.6666654611e-1 + z * (8.3321608736e-3 + z * -1.9515295891e-4))
            c = 1.0 - 0.5 * z + z * z * (4.166664568298827e-2 + z * (-1.388731625493765e-3 + z * 2.443315711809948e-5))
            odd = (k == 1.0) | (k == 3.0)
            cs = jnp.where(odd, s, c)
            sn = jnp.where(odd, c, s)
            cos_v = jnp.where((k == 1.0) | (k == 2.0), -cs, cs).astype(jnp.bfloat16)
            sin_v = jnp.where((k == 2.0) | (k == 3.0), -sn, sn).astype(jnp.bfloat16)
            basis_ref[pl.ds(r0, ROWS), pl.ds(c0, LANES)] = cos_v
            basis_ref[pl.ds(r0, ROWS), pl.ds(nper + c0, LANES)] = sin_v
            cf = cos_v.astype(jnp.float32)
            sf = sin_v.astype(jnp.float32)
            return acc_c + cf * cf, acc_s + sf * sf

        zero = jnp.zeros((ROWS, LANES), jnp.float32)
        acc_c, acc_s = lax.fori_loop(0, obs // ROWS, row_block, (zero, zero), unroll=UNROLL)
        nc_ref[:, pl.ds(c0, LANES)] = jnp.sum(acc_c, axis=0, keepdims=True) + RIDGE
        ns_ref[:, pl.ds(c0, LANES)] = jnp.sum(acc_s, axis=0, keepdims=True) + RIDGE
        return carry

    lax.fori_loop(0, nper // LANES, lane_block, 0)


def basis_and_norms(times, periods):
    plans, obs = times.shape
    nper = periods.shape[0]
    pf = periods.astype(jnp.float32)
    w = (TWO_PI / pf).reshape(1, nper)
    inv = (1.0 / pf).reshape(1, nper)
    pf = pf.reshape(1, nper)
    tf = times.astype(jnp.float32).reshape(plans, obs, 1)
    row = pl.BlockSpec((1, nper), lambda g: (0, 0))
    basis, nc, ns = pl.pallas_call(
        basis_kernel,
        grid=(plans,),
        in_specs=[pl.BlockSpec((None, obs, 1), lambda g: (g, 0, 0)), row, row, row],
        out_specs=[
            pl.BlockSpec((None, obs, 2 * nper), lambda g: (g, 0, 0)),
            pl.BlockSpec((None, 1, nper), lambda g: (g, 0, 0)),
            pl.BlockSpec((None, 1, nper), lambda g: (g, 0, 0)),
        ],
        out_shape=[
            jax.ShapeDtypeStruct((plans, obs, 2 * nper), jnp.bfloat16),
            jax.ShapeDtypeStruct((plans, 1, nper), jnp.float32),
            jax.ShapeDtypeStruct((plans, 1, nper), jnp.float32),
        ],
        cost_estimate=pl.CostEstimate(
            flops=60 * plans * obs * nper, transcendentals=0,
            bytes_accessed=plans * obs * 2 * nper * 2),
    )(tf, pf, w, inv)
    return basis, nc.reshape(plans, nper), ns.reshape(plans, nper)


def gather_kernel(idx_ref, src_ref, out_ref):
    def body(r, carry):
        out_ref[pl.ds(r, 1), :] = src_ref[pl.ds(idx_ref[r], 1), :]
        return carry

    lax.fori_loop(0, out_ref.shape[0], body, 0, unroll=16)


def row_gather(src, idx):
    rows, width = idx.shape[0], src.shape[1]
    return pl.pallas_call(
        gather_kernel,
        in_specs=[pl.BlockSpec(memory_space=pltpu.SMEM), pl.BlockSpec(memory_space=pltpu.VMEM)],
        out_specs=pl.BlockSpec(memory_space=pltpu.VMEM),
        out_shape=jax.ShapeDtypeStruct((rows, width), src.dtype),
        cost_estimate=pl.CostEstimate(
            flops=0, transcendentals=0, bytes_accessed=2 * rows * width * src.dtype.itemsize),
    )(idx, src)


def with_zero_rows(flat):
    return jnp.concatenate([flat, jnp.zeros((8, flat.shape[1]), flat.dtype)], axis=0)

def fit_groups(basis, observed, norm_cos, norm_sin, nper):
    corr = jnp.einsum("fio,fic->foc", basis, observed, preferred_element_type=jnp.float32)
    cosine = corr[:, :nper]
    sine = corr[:, nper:]
    amp_c = cosine / norm_cos[:, :, None]
    amp_s = sine / norm_sin[:, :, None]
    power = cosine * amp_c + sine * amp_s
    logits = BETA * power
    highest = jnp.max(logits, axis=1)
    expo = jnp.exp(logits - highest[:, None, :])
    total = jnp.sum(expo, axis=1)
    share = expo / total[:, None, :]
    coeff = jnp.concatenate([share * amp_c, share * amp_s], axis=1).astype(jnp.bfloat16)
    model = jnp.einsum("fio,foc->fic", basis, coeff, preferred_element_type=jnp.float32)
    return (model, highest + jnp.log(total))


def on_device(residuals, seg_counts, attitude, sched_seg, sched_slot, periods):
    tm_count = lax.axis_size("tm")
    sched_dev, obs = sched_seg.shape
    seg_dev, slots, width = residuals.shape
    nper = periods.shape[0]
    column_blocks = width // SRC_GROUP
    capacity = 2 * sched_dev * obs // tm_count
    requests = sched_dev * obs
    seg_flat = sched_seg.reshape(-1)
    slot_flat = sched_slot.reshape(-1)
    block_of = jnp.repeat(jnp.arange(sched_dev, dtype=jnp.int32) % column_blocks, obs)
    target = seg_flat // seg_dev
    local_row = (seg_flat % seg_dev * slots + slot_flat) * column_blocks + block_of
    onehot = (target[:, None] == jnp.arange(tm_count, dtype=jnp.int32)[None, :]).astype(jnp.int32)
    position = jnp.sum(jnp.cumsum(onehot, axis=0) * onehot, axis=1) - 1
    empty_row = seg_dev * slots * column_blocks
    slot_of = target * capacity + position
    pair = (
        jnp.broadcast_to(jnp.array([empty_row, requests], jnp.int32), (tm_count * capacity, 2))
        .at[slot_of]
        .set(jnp.stack([local_row, jnp.arange(requests, dtype=jnp.int32)], axis=1))
    )
    wanted = pair[:, 0].reshape(tm_count, capacity)
    inverse = pair[:, 1]
    asked = lax.all_to_all(wanted, "tm", split_axis=0, concat_axis=0, tiled=True).reshape(-1)
    basis, norm_cos, norm_sin = basis_and_norms(sched_seg * slots + sched_slot, periods)
    valid = jnp.arange(slots, dtype=jnp.int32)[None, :] < seg_counts[:, None]
    current = residuals.astype(jnp.float32)
    evidence = jnp.zeros((sched_dev, SRC_GROUP), jnp.float32)
    attitude_all = lax.all_gather(attitude, "sky", axis=1, tiled=True)
    for iteration in range(ITERS):
        masked = jnp.where(valid[:, :, None], current, 0.0).astype(jnp.bfloat16)
        white = jnp.einsum(
            "sij,sjc->sic", attitude_all, masked, preferred_element_type=jnp.float32
        )
        picked = row_gather(with_zero_rows(white.reshape(-1, SRC_GROUP)), asked)
        arrived = lax.all_to_all(
            picked.astype(jnp.bfloat16).reshape(tm_count, capacity, SRC_GROUP),
            "tm", split_axis=0, concat_axis=0, tiled=True)
        observed = row_gather(arrived.reshape(-1, SRC_GROUP).astype(jnp.float32), slot_of)
        observed = observed.astype(jnp.bfloat16).reshape(sched_dev, obs, SRC_GROUP)
        model, evidence = fit_groups(basis, observed, norm_cos, norm_sin, nper)
        outgoing = row_gather(with_zero_rows(model.reshape(requests, SRC_GROUP)), inverse)
        returned = lax.all_to_all(
            outgoing.astype(jnp.bfloat16).reshape(tm_count, capacity, SRC_GROUP),
            "tm", split_axis=0, concat_axis=0, tiled=True)
        placed = (
            jnp.zeros((empty_row, SRC_GROUP), jnp.float32)
            .at[asked]
            .add(returned.reshape(-1, SRC_GROUP).astype(jnp.float32), mode="drop")
        )
        current = current - placed.reshape(seg_dev, slots, width)
    return (current, evidence)


def solution(mesh):
    in_specs = (
        P("tm", None, "sky"),
        P("tm"),
        P("tm", "sky", None),
        P(("tm", "sky"), None),
        P(("tm", "sky"), None),
        P(),
    )
    out_specs = (P("tm", None, "sky"), P(("tm", "sky"), None))
    return jax.shard_map(
        on_device, mesh=mesh, in_specs=in_specs, out_specs=out_specs, check_vma=False
    )
```

```python
import jax
import jax.numpy as jnp
from jax import lax
from jax.experimental import pallas as pl
from jax.experimental.pallas import tpu as pltpu
from jax.sharding import PartitionSpec as P

SRC_GROUP = 128
ITERS = 2


TWO_PI = 6.283185307179586
BETA = 2.0
RIDGE = 1.0


PIO2_1 = 1.5703125
PIO2_2 = 4.837512969970703125e-4
PIO2_3 = 7.549789954891e-8
ROWS = 16
LANES = 512
UNROLL = 2


def basis_kernel(t_ref, p_ref, w_ref, inv_ref, basis_ref, nc_ref, ns_ref):
    obs = t_ref.shape[0]
    nper = p_ref.shape[1]

    def lane_block(j, carry):
        c0 = pl.multiple_of(j * LANES, LANES)
        pf = p_ref[:, pl.ds(c0, LANES)]
        w = w_ref[:, pl.ds(c0, LANES)]
        inv = inv_ref[:, pl.ds(c0, LANES)]

        def row_block(i, acc):
            acc_c, acc_s = acc
            r0 = pl.multiple_of(i * ROWS, ROWS)
            tf = jnp.broadcast_to(t_ref[pl.ds(r0, ROWS), :], (ROWS, LANES))
            q = jnp.floor(tf * inv)
            r = tf - q * pf
            r = jnp.where(r < 0.0, r + pf, r)
            r = jnp.where(r >= pf, r - pf, r)
            phase = r * w
            k = jnp.floor(phase * 0.6366197723675814 + 0.5)
            y = ((phase - k * PIO2_1) - k * PIO2_2) - k * PIO2_3
            z = y * y
            s = y + y * z * (-1.6666654611e-1 + z * (8.3321608736e-3 + z * -1.9515295891e-4))
            c = 1.0 - 0.5 * z + z * z * (4.166664568298827e-2 + z * (-1.388731625493765e-3 + z * 2.443315711809948e-5))
            odd = (k == 1.0) | (k == 3.0)
            cs = jnp.where(odd, s, c)
            sn = jnp.where(odd, c, s)
            cos_v = jnp.where((k == 1.0) | (k == 2.0), -cs, cs).astype(jnp.bfloat16)
            sin_v = jnp.where((k == 2.0) | (k == 3.0), -sn, sn).astype(jnp.bfloat16)
            basis_ref[pl.ds(r0, ROWS), pl.ds(c0, LANES)] = cos_v
            basis_ref[pl.ds(r0, ROWS), pl.ds(nper + c0, LANES)] = sin_v
            cf = cos_v.astype(jnp.float32)
            sf = sin_v.astype(jnp.float32)
            return acc_c + cf * cf, acc_s + sf * sf

        zero = jnp.zeros((ROWS, LANES), jnp.float32)
        acc_c, acc_s = lax.fori_loop(0, obs // ROWS, row_block, (zero, zero), unroll=UNROLL)
        nc_ref[:, pl.ds(c0, LANES)] = jnp.sum(acc_c, axis=0, keepdims=True) + RIDGE
        ns_ref[:, pl.ds(c0, LANES)] = jnp.sum(acc_s, axis=0, keepdims=True) + RIDGE
        return carry

    lax.fori_loop(0, nper // LANES, lane_block, 0)


def basis_and_norms(times, periods):
    plans, obs = times.shape
    nper = periods.shape[0]
    pf = periods.astype(jnp.float32)
    w = (TWO_PI / pf).reshape(1, nper)
    inv = (1.0 / pf).reshape(1, nper)
    pf = pf.reshape(1, nper)
    tf = times.astype(jnp.float32).reshape(plans, obs, 1)
    row = pl.BlockSpec((1, nper), lambda g: (0, 0))
    basis, nc, ns = pl.pallas_call(
        basis_kernel,
        grid=(plans,),
        in_specs=[pl.BlockSpec((None, obs, 1), lambda g: (g, 0, 0)), row, row, row],
        out_specs=[
            pl.BlockSpec((None, obs, 2 * nper), lambda g: (g, 0, 0)),
            pl.BlockSpec((None, 1, nper), lambda g: (g, 0, 0)),
            pl.BlockSpec((None, 1, nper), lambda g: (g, 0, 0)),
        ],
        out_shape=[
            jax.ShapeDtypeStruct((plans, obs, 2 * nper), jnp.bfloat16),
            jax.ShapeDtypeStruct((plans, 1, nper), jnp.float32),
            jax.ShapeDtypeStruct((plans, 1, nper), jnp.float32),
        ],
        cost_estimate=pl.CostEstimate(
            flops=60 * plans * obs * nper, transcendentals=0,
            bytes_accessed=plans * obs * 2 * nper * 2),
    )(tf, pf, w, inv)
    return basis, nc.reshape(plans, nper), ns.reshape(plans, nper)


def gather_kernel(idx_ref, src_ref, out_ref):
    def body(r, carry):
        out_ref[pl.ds(r, 1), :] = src_ref[pl.ds(idx_ref[r], 1), :]
        return carry

    lax.fori_loop(0, out_ref.shape[0], body, 0, unroll=16)


def row_gather(src, idx):
    rows, width = idx.shape[0], src.shape[1]
    return pl.pallas_call(
        gather_kernel,
        in_specs=[pl.BlockSpec(memory_space=pltpu.SMEM), pl.BlockSpec(memory_space=pltpu.VMEM)],
        out_specs=pl.BlockSpec(memory_space=pltpu.VMEM),
        out_shape=jax.ShapeDtypeStruct((rows, width), src.dtype),
        cost_estimate=pl.CostEstimate(
            flops=0, transcendentals=0, bytes_accessed=2 * rows * width * src.dtype.itemsize),
    )(idx, src)


def with_zero_rows(flat):
    return jnp.concatenate([flat, jnp.zeros((8, flat.shape[1]), flat.dtype)], axis=0)


def a2a_kernel(x_ref, out_ref, held, send_sem, recv_sem):
    n = x_ref.shape[0]
    me = lax.axis_index("tm")
    sky = lax.axis_index("sky")
    barrier = pltpu.get_barrier_semaphore()

    def greet(k, carry):
        peer = lax.rem(me + k, n)
        pl.semaphore_signal(barrier, inc=1, device_id=(peer, sky), device_id_type=pl.DeviceIdType.MESH)
        return carry

    lax.fori_loop(1, n, greet, 0)
    pl.semaphore_wait(barrier, n - 1)

    def copy(k):
        peer = lax.rem(me + k, n)
        return pltpu.make_async_remote_copy(
            src_ref=x_ref.at[peer],
            dst_ref=held.at[me],
            send_sem=send_sem.at[k],
            recv_sem=recv_sem.at[k],
            device_id=(peer, sky),
            device_id_type=pl.DeviceIdType.MESH,
        )

    def start(k, carry):
        copy(k).start()
        return carry

    lax.fori_loop(1, n, start, 0)
    held[pl.ds(me, 1)] = x_ref[pl.ds(me, 1)]

    def finish(k, carry):
        copy(k).wait()
        return carry

    lax.fori_loop(1, n, finish, 0)
    out_ref[...] = held[...].astype(out_ref.dtype)


def tm_all_to_all(x, out_dtype, collective_id):
    n, rows, width = x.shape
    return pl.pallas_call(
        a2a_kernel,
        in_specs=[pl.BlockSpec(memory_space=pltpu.VMEM)],
        out_specs=pl.BlockSpec(memory_space=pltpu.VMEM),
        out_shape=jax.ShapeDtypeStruct((n, rows, width), out_dtype),
        scratch_shapes=[
            pltpu.VMEM((n, rows, width), x.dtype),
            pltpu.SemaphoreType.DMA((n,)),
            pltpu.SemaphoreType.DMA((n,)),
        ],
        compiler_params=pltpu.CompilerParams(collective_id=collective_id, has_side_effects=True),
    )(x)

def fit_groups(basis, observed, norm_cos, norm_sin, nper):
    corr = jnp.einsum("fio,fic->foc", basis, observed, preferred_element_type=jnp.float32)
    cosine = corr[:, :nper]
    sine = corr[:, nper:]
    amp_c = cosine / norm_cos[:, :, None]
    amp_s = sine / norm_sin[:, :, None]
    power = cosine * amp_c + sine * amp_s
    logits = BETA * power
    highest = jnp.max(logits, axis=1)
    expo = jnp.exp(logits - highest[:, None, :])
    total = jnp.sum(expo, axis=1)
    share = expo / total[:, None, :]
    coeff = jnp.concatenate([share * amp_c, share * amp_s], axis=1).astype(jnp.bfloat16)
    model = jnp.einsum("fio,foc->fic", basis, coeff, preferred_element_type=jnp.float32)
    return (model, highest + jnp.log(total))


def on_device(residuals, seg_counts, attitude, sched_seg, sched_slot, periods):
    tm_count = lax.axis_size("tm")
    sched_dev, obs = sched_seg.shape
    seg_dev, slots, width = residuals.shape
    nper = periods.shape[0]
    column_blocks = width // SRC_GROUP
    capacity = 2 * sched_dev * obs // tm_count
    requests = sched_dev * obs
    seg_flat = sched_seg.reshape(-1)
    slot_flat = sched_slot.reshape(-1)
    block_of = jnp.repeat(jnp.arange(sched_dev, dtype=jnp.int32) % column_blocks, obs)
    target = seg_flat // seg_dev
    local_row = (seg_flat % seg_dev * slots + slot_flat) * column_blocks + block_of
    onehot = (target[:, None] == jnp.arange(tm_count, dtype=jnp.int32)[None, :]).astype(jnp.int32)
    position = jnp.sum(jnp.cumsum(onehot, axis=0) * onehot, axis=1) - 1
    empty_row = seg_dev * slots * column_blocks
    slot_of = target * capacity + position
    pair = (
        jnp.broadcast_to(jnp.array([empty_row, requests], jnp.int32), (tm_count * capacity, 2))
        .at[slot_of]
        .set(jnp.stack([local_row, jnp.arange(requests, dtype=jnp.int32)], axis=1))
    )
    wanted = pair[:, 0].reshape(tm_count, capacity)
    inverse = pair[:, 1]
    asked = lax.all_to_all(wanted, "tm", split_axis=0, concat_axis=0, tiled=True).reshape(-1)
    basis, norm_cos, norm_sin = basis_and_norms(sched_seg * slots + sched_slot, periods)
    valid = jnp.arange(slots, dtype=jnp.int32)[None, :] < seg_counts[:, None]
    current = residuals.astype(jnp.float32)
    evidence = jnp.zeros((sched_dev, SRC_GROUP), jnp.float32)
    attitude_all = lax.all_gather(attitude, "sky", axis=1, tiled=True)
    for iteration in range(ITERS):
        masked = jnp.where(valid[:, :, None], current, 0.0).astype(jnp.bfloat16)
        white = jnp.einsum(
            "sij,sjc->sic", attitude_all, masked, preferred_element_type=jnp.float32
        )
        picked = row_gather(with_zero_rows(white.reshape(-1, SRC_GROUP)), asked)
        arrived = tm_all_to_all(
            picked.astype(jnp.bfloat16).reshape(tm_count, capacity, SRC_GROUP),
            jnp.float32, 1 + 2 * iteration)
        observed = row_gather(arrived.reshape(-1, SRC_GROUP), slot_of)
        observed = observed.astype(jnp.bfloat16).reshape(sched_dev, obs, SRC_GROUP)
        model, evidence = fit_groups(basis, observed, norm_cos, norm_sin, nper)
        outgoing = row_gather(with_zero_rows(model.reshape(requests, SRC_GROUP)), inverse)
        returned = tm_all_to_all(
            outgoing.astype(jnp.bfloat16).reshape(tm_count, capacity, SRC_GROUP),
            jnp.float32, 2 + 2 * iteration)
        placed = (
            jnp.zeros((empty_row, SRC_GROUP), jnp.float32)
            .at[asked]
            .add(returned.reshape(-1, SRC_GROUP).astype(jnp.float32), mode="drop")
        )
        current = current - placed.reshape(seg_dev, slots, width)
    return (current, evidence)


def solution(mesh):
    in_specs = (
        P("tm", None, "sky"),
        P("tm"),
        P("tm", "sky", None),
        P(("tm", "sky"), None),
        P(("tm", "sky"), None),
        P(),
    )
    out_specs = (P("tm", None, "sky"), P(("tm", "sky"), None))
    return jax.shard_map(
        on_device, mesh=mesh, in_specs=in_specs, out_specs=out_specs, check_vma=False
    )
```

```python
import jax
import jax.numpy as jnp
from jax import lax
from jax.experimental import pallas as pl
from jax.experimental.pallas import tpu as pltpu
from jax.sharding import PartitionSpec as P

SRC_GROUP = 128
ITERS = 2


TWO_PI = 6.283185307179586
BETA = 2.0
RIDGE = 1.0


PIO2_1 = 1.5703125
PIO2_2 = 4.837512969970703125e-4
PIO2_3 = 7.549789954891e-8
ROWS = 16
LANES = 512
UNROLL = 2


def basis_kernel(t_ref, p_ref, w_ref, inv_ref, basis_ref, nc_ref, ns_ref):
    obs = t_ref.shape[0]
    nper = p_ref.shape[1]

    def lane_block(j, carry):
        c0 = pl.multiple_of(j * LANES, LANES)
        pf = p_ref[:, pl.ds(c0, LANES)]
        w = w_ref[:, pl.ds(c0, LANES)]
        inv = inv_ref[:, pl.ds(c0, LANES)]

        def row_block(i, acc):
            acc_c, acc_s = acc
            r0 = pl.multiple_of(i * ROWS, ROWS)
            tf = jnp.broadcast_to(t_ref[pl.ds(r0, ROWS), :], (ROWS, LANES))
            q = jnp.floor(tf * inv)
            r = tf - q * pf
            r = jnp.where(r < 0.0, r + pf, r)
            r = jnp.where(r >= pf, r - pf, r)
            phase = r * w
            k = jnp.floor(phase * 0.6366197723675814 + 0.5)
            y = ((phase - k * PIO2_1) - k * PIO2_2) - k * PIO2_3
            z = y * y
            s = y + y * z * (-1.6666654611e-1 + z * (8.3321608736e-3 + z * -1.9515295891e-4))
            c = 1.0 - 0.5 * z + z * z * (4.166664568298827e-2 + z * (-1.388731625493765e-3 + z * 2.443315711809948e-5))
            odd = (k == 1.0) | (k == 3.0)
            cs = jnp.where(odd, s, c)
            sn = jnp.where(odd, c, s)
            cos_v = jnp.where((k == 1.0) | (k == 2.0), -cs, cs).astype(jnp.bfloat16)
            sin_v = jnp.where((k == 2.0) | (k == 3.0), -sn, sn).astype(jnp.bfloat16)
            basis_ref[pl.ds(r0, ROWS), pl.ds(c0, LANES)] = cos_v
            basis_ref[pl.ds(r0, ROWS), pl.ds(nper + c0, LANES)] = sin_v
            cf = cos_v.astype(jnp.float32)
            sf = sin_v.astype(jnp.float32)
            return acc_c + cf * cf, acc_s + sf * sf

        zero = jnp.zeros((ROWS, LANES), jnp.float32)
        acc_c, acc_s = lax.fori_loop(0, obs // ROWS, row_block, (zero, zero), unroll=UNROLL)
        nc_ref[:, pl.ds(c0, LANES)] = jnp.sum(acc_c, axis=0, keepdims=True) + RIDGE
        ns_ref[:, pl.ds(c0, LANES)] = jnp.sum(acc_s, axis=0, keepdims=True) + RIDGE
        return carry

    lax.fori_loop(0, nper // LANES, lane_block, 0)


def basis_and_norms(times, periods):
    plans, obs = times.shape
    nper = periods.shape[0]
    pf = periods.astype(jnp.float32)
    w = (TWO_PI / pf).reshape(1, nper)
    inv = (1.0 / pf).reshape(1, nper)
    pf = pf.reshape(1, nper)
    tf = times.astype(jnp.float32).reshape(plans, obs, 1)
    row = pl.BlockSpec((1, nper), lambda g: (0, 0))
    basis, nc, ns = pl.pallas_call(
        basis_kernel,
        grid=(plans,),
        in_specs=[pl.BlockSpec((None, obs, 1), lambda g: (g, 0, 0)), row, row, row],
        out_specs=[
            pl.BlockSpec((None, obs, 2 * nper), lambda g: (g, 0, 0)),
            pl.BlockSpec((None, 1, nper), lambda g: (g, 0, 0)),
            pl.BlockSpec((None, 1, nper), lambda g: (g, 0, 0)),
        ],
        out_shape=[
            jax.ShapeDtypeStruct((plans, obs, 2 * nper), jnp.bfloat16),
            jax.ShapeDtypeStruct((plans, 1, nper), jnp.float32),
            jax.ShapeDtypeStruct((plans, 1, nper), jnp.float32),
        ],
        cost_estimate=pl.CostEstimate(
            flops=60 * plans * obs * nper, transcendentals=0,
            bytes_accessed=plans * obs * 2 * nper * 2),
    )(tf, pf, w, inv)
    return basis, nc.reshape(plans, nper), ns.reshape(plans, nper)


def gather_kernel(idx_ref, src_ref, out_ref):
    def body(r, carry):
        out_ref[pl.ds(r, 1), :] = src_ref[pl.ds(idx_ref[r], 1), :]
        return carry

    lax.fori_loop(0, out_ref.shape[0], body, 0, unroll=16)


def row_gather(src, idx):
    rows, width = idx.shape[0], src.shape[1]
    return pl.pallas_call(
        gather_kernel,
        in_specs=[pl.BlockSpec(memory_space=pltpu.SMEM), pl.BlockSpec(memory_space=pltpu.VMEM)],
        out_specs=pl.BlockSpec(memory_space=pltpu.VMEM),
        out_shape=jax.ShapeDtypeStruct((rows, width), src.dtype),
        cost_estimate=pl.CostEstimate(
            flops=0, transcendentals=0, bytes_accessed=2 * rows * width * src.dtype.itemsize),
    )(idx, src)


def with_zero_rows(flat):
    return jnp.concatenate([flat, jnp.zeros((8, flat.shape[1]), flat.dtype)], axis=0)


def a2a_kernel(x_ref, out_ref, held, send_sem, recv_sem):
    n = x_ref.shape[0]
    me = lax.axis_index("tm")
    sky = lax.axis_index("sky")
    barrier = pltpu.get_barrier_semaphore()

    def greet(k, carry):
        peer = lax.rem(me + k, n)
        pl.semaphore_signal(barrier, inc=1, device_id=(peer, sky), device_id_type=pl.DeviceIdType.MESH)
        return carry

    lax.fori_loop(1, n, greet, 0)
    pl.semaphore_wait(barrier, n - 1)

    def copy(k):
        peer = lax.rem(me + k, n)
        return pltpu.make_async_remote_copy(
            src_ref=x_ref.at[peer],
            dst_ref=held.at[me],
            send_sem=send_sem.at[k],
            recv_sem=recv_sem.at[k],
            device_id=(peer, sky),
            device_id_type=pl.DeviceIdType.MESH,
        )

    def start(k, carry):
        copy(k).start()
        return carry

    lax.fori_loop(1, n, start, 0)
    held[pl.ds(me, 1)] = x_ref[pl.ds(me, 1)]

    def finish(k, carry):
        copy(k).wait()
        return carry

    lax.fori_loop(1, n, finish, 0)
    out_ref[...] = held[...].astype(out_ref.dtype)


def tm_all_to_all(x, out_dtype, collective_id):
    n, rows, width = x.shape
    return pl.pallas_call(
        a2a_kernel,
        in_specs=[pl.BlockSpec(memory_space=pltpu.VMEM)],
        out_specs=pl.BlockSpec(memory_space=pltpu.VMEM),
        out_shape=jax.ShapeDtypeStruct((n, rows, width), out_dtype),
        scratch_shapes=[
            pltpu.VMEM((n, rows, width), x.dtype),
            pltpu.SemaphoreType.DMA((n,)),
            pltpu.SemaphoreType.DMA((n,)),
        ],
        compiler_params=pltpu.CompilerParams(collective_id=collective_id, has_side_effects=True),
    )(x)


STREAMS = 4
SUNROLL = 2

def scatter_add_kernel(idx_ref, src_ref, out_ref, acc_ref):
    rows = src_ref.shape[0]
    streams = acc_ref.shape[0]
    acc_ref[...] = jnp.zeros_like(acc_ref)

    def body(step, carry):
        base = step * streams
        for s in range(streams):
            r = base + s
            i = idx_ref[r]
            acc_ref[s, pl.ds(i, 1), :] = acc_ref[s, pl.ds(i, 1), :] + src_ref[pl.ds(r, 1), :]
        return carry

    lax.fori_loop(0, rows // streams, body, 0, unroll=SUNROLL)
    total = acc_ref[0]
    for s in range(1, streams):
        total = total + acc_ref[s]
    out_ref[...] = total[: out_ref.shape[0]]


def scatter_add(src, idx, out_rows):
    rows, width = src.shape
    pad = out_rows + 8
    return pl.pallas_call(
        scatter_add_kernel,
        in_specs=[pl.BlockSpec(memory_space=pltpu.SMEM), pl.BlockSpec(memory_space=pltpu.VMEM)],
        out_specs=pl.BlockSpec(memory_space=pltpu.VMEM),
        out_shape=jax.ShapeDtypeStruct((out_rows, width), jnp.float32),
        scratch_shapes=[pltpu.VMEM((STREAMS, pad, width), jnp.float32)],
        cost_estimate=pl.CostEstimate(flops=rows * width, transcendentals=0, bytes_accessed=(rows + out_rows) * width * 4),
    )(idx, src)

def fit_groups(basis, observed, norm_cos, norm_sin, nper):
    corr = jnp.einsum("fio,fic->foc", basis, observed, preferred_element_type=jnp.float32)
    cosine = corr[:, :nper]
    sine = corr[:, nper:]
    amp_c = cosine / norm_cos[:, :, None]
    amp_s = sine / norm_sin[:, :, None]
    power = cosine * amp_c + sine * amp_s
    logits = BETA * power
    highest = jnp.max(logits, axis=1)
    expo = jnp.exp(logits - highest[:, None, :])
    total = jnp.sum(expo, axis=1)
    share = expo / total[:, None, :]
    coeff = jnp.concatenate([share * amp_c, share * amp_s], axis=1).astype(jnp.bfloat16)
    model = jnp.einsum("fio,foc->fic", basis, coeff, preferred_element_type=jnp.float32)
    return (model, highest + jnp.log(total))


def on_device(residuals, seg_counts, attitude, sched_seg, sched_slot, periods):
    tm_count = lax.axis_size("tm")
    sched_dev, obs = sched_seg.shape
    seg_dev, slots, width = residuals.shape
    nper = periods.shape[0]
    column_blocks = width // SRC_GROUP
    capacity = 2 * sched_dev * obs // tm_count
    requests = sched_dev * obs
    seg_flat = sched_seg.reshape(-1)
    slot_flat = sched_slot.reshape(-1)
    block_of = jnp.repeat(jnp.arange(sched_dev, dtype=jnp.int32) % column_blocks, obs)
    target = seg_flat // seg_dev
    local_row = (seg_flat % seg_dev * slots + slot_flat) * column_blocks + block_of
    onehot = (target[:, None] == jnp.arange(tm_count, dtype=jnp.int32)[None, :]).astype(jnp.int32)
    position = jnp.sum(jnp.cumsum(onehot, axis=0) * onehot, axis=1) - 1
    empty_row = seg_dev * slots * column_blocks
    slot_of = target * capacity + position
    pair = (
        jnp.broadcast_to(jnp.array([empty_row, requests], jnp.int32), (tm_count * capacity, 2))
        .at[slot_of]
        .set(jnp.stack([local_row, jnp.arange(requests, dtype=jnp.int32)], axis=1))
    )
    wanted = pair[:, 0].reshape(tm_count, capacity)
    inverse = pair[:, 1]
    asked = lax.all_to_all(wanted, "tm", split_axis=0, concat_axis=0, tiled=True).reshape(-1)
    basis, norm_cos, norm_sin = basis_and_norms(sched_seg * slots + sched_slot, periods)
    valid = jnp.arange(slots, dtype=jnp.int32)[None, :] < seg_counts[:, None]
    current = residuals.astype(jnp.float32)
    evidence = jnp.zeros((sched_dev, SRC_GROUP), jnp.float32)
    attitude_all = lax.all_gather(attitude, "sky", axis=1, tiled=True)
    for iteration in range(ITERS):
        masked = jnp.where(valid[:, :, None], current, 0.0).astype(jnp.bfloat16)
        white = jnp.einsum(
            "sij,sjc->sic", attitude_all, masked, preferred_element_type=jnp.float32
        )
        picked = row_gather(with_zero_rows(white.reshape(-1, SRC_GROUP)), asked)
        outbound = picked.astype(jnp.bfloat16).reshape(tm_count, capacity, SRC_GROUP)
        if iteration == 0:
            arrived = lax.all_to_all(outbound, "tm", split_axis=0, concat_axis=0, tiled=True)
            arrived = arrived.astype(jnp.float32)
        else:
            arrived = tm_all_to_all(outbound, jnp.float32, 1 + 2 * iteration)
        observed = row_gather(arrived.reshape(-1, SRC_GROUP), slot_of)
        observed = observed.astype(jnp.bfloat16).reshape(sched_dev, obs, SRC_GROUP)
        model, evidence = fit_groups(basis, observed, norm_cos, norm_sin, nper)
        outgoing = row_gather(with_zero_rows(model.reshape(requests, SRC_GROUP)), inverse)
        returned = tm_all_to_all(
            outgoing.astype(jnp.bfloat16).reshape(tm_count, capacity, SRC_GROUP),
            jnp.float32, 2 + 2 * iteration)
        placed = scatter_add(returned.reshape(-1, SRC_GROUP), asked, empty_row)
        current = current - placed.reshape(seg_dev, slots, width)
    return (current, evidence)


def solution(mesh):
    in_specs = (
        P("tm", None, "sky"),
        P("tm"),
        P("tm", "sky", None),
        P(("tm", "sky"), None),
        P(("tm", "sky"), None),
        P(),
    )
    out_specs = (P("tm", None, "sky"), P(("tm", "sky"), None))
    return jax.shard_map(
        on_device, mesh=mesh, in_specs=in_specs, out_specs=out_specs, check_vma=False
    )
```

```python
import jax
import jax.numpy as jnp
from jax import lax
from jax.experimental import pallas as pl
from jax.experimental.pallas import tpu as pltpu
from jax.sharding import PartitionSpec as P

SRC_GROUP = 128
ITERS = 2


TWO_PI = 6.283185307179586
BETA = 2.0
RIDGE = 1.0


PIO2_1 = 1.5703125
PIO2_2 = 4.837512969970703125e-4
PIO2_3 = 7.549789954891e-8
ROWS = 16
LANES = 512
UNROLL = 2


def basis_kernel(t_ref, p_ref, w_ref, inv_ref, basis_ref, nc_ref, ns_ref):
    obs = t_ref.shape[0]
    nper = p_ref.shape[1]

    def lane_block(j, carry):
        c0 = pl.multiple_of(j * LANES, LANES)
        pf = p_ref[:, pl.ds(c0, LANES)]
        w = w_ref[:, pl.ds(c0, LANES)]
        inv = inv_ref[:, pl.ds(c0, LANES)]

        def row_block(i, acc):
            acc_c, acc_s = acc
            r0 = pl.multiple_of(i * ROWS, ROWS)
            tf = jnp.broadcast_to(t_ref[pl.ds(r0, ROWS), :], (ROWS, LANES))
            q = jnp.floor(tf * inv)
            r = tf - q * pf
            r = jnp.where(r < 0.0, r + pf, r)
            r = jnp.where(r >= pf, r - pf, r)
            phase = r * w
            k = jnp.floor(phase * 0.6366197723675814 + 0.5)
            y = ((phase - k * PIO2_1) - k * PIO2_2) - k * PIO2_3
            z = y * y
            s = y + y * z * (-1.6666654611e-1 + z * (8.3321608736e-3 + z * -1.9515295891e-4))
            c = 1.0 - 0.5 * z + z * z * (4.166664568298827e-2 + z * (-1.388731625493765e-3 + z * 2.443315711809948e-5))
            odd = (k == 1.0) | (k == 3.0)
            cs = jnp.where(odd, s, c)
            sn = jnp.where(odd, c, s)
            cos_v = jnp.where((k == 1.0) | (k == 2.0), -cs, cs).astype(jnp.bfloat16)
            sin_v = jnp.where((k == 2.0) | (k == 3.0), -sn, sn).astype(jnp.bfloat16)
            basis_ref[pl.ds(r0, ROWS), pl.ds(c0, LANES)] = cos_v
            basis_ref[pl.ds(r0, ROWS), pl.ds(nper + c0, LANES)] = sin_v
            cf = cos_v.astype(jnp.float32)
            sf = sin_v.astype(jnp.float32)
            return acc_c + cf * cf, acc_s + sf * sf

        zero = jnp.zeros((ROWS, LANES), jnp.float32)
        acc_c, acc_s = lax.fori_loop(0, obs // ROWS, row_block, (zero, zero), unroll=UNROLL)
        nc_ref[:, pl.ds(c0, LANES)] = jnp.sum(acc_c, axis=0, keepdims=True) + RIDGE
        ns_ref[:, pl.ds(c0, LANES)] = jnp.sum(acc_s, axis=0, keepdims=True) + RIDGE
        return carry

    lax.fori_loop(0, nper // LANES, lane_block, 0)


def basis_and_norms(times, periods):
    plans, obs = times.shape
    nper = periods.shape[0]
    pf = periods.astype(jnp.float32)
    w = (TWO_PI / pf).reshape(1, nper)
    inv = (1.0 / pf).reshape(1, nper)
    pf = pf.reshape(1, nper)
    tf = times.astype(jnp.float32).reshape(plans, obs, 1)
    row = pl.BlockSpec((1, nper), lambda g: (0, 0))
    basis, nc, ns = pl.pallas_call(
        basis_kernel,
        grid=(plans,),
        in_specs=[pl.BlockSpec((None, obs, 1), lambda g: (g, 0, 0)), row, row, row],
        out_specs=[
            pl.BlockSpec((None, obs, 2 * nper), lambda g: (g, 0, 0)),
            pl.BlockSpec((None, 1, nper), lambda g: (g, 0, 0)),
            pl.BlockSpec((None, 1, nper), lambda g: (g, 0, 0)),
        ],
        out_shape=[
            jax.ShapeDtypeStruct((plans, obs, 2 * nper), jnp.bfloat16),
            jax.ShapeDtypeStruct((plans, 1, nper), jnp.float32),
            jax.ShapeDtypeStruct((plans, 1, nper), jnp.float32),
        ],
        cost_estimate=pl.CostEstimate(
            flops=60 * plans * obs * nper, transcendentals=0,
            bytes_accessed=plans * obs * 2 * nper * 2),
    )(tf, pf, w, inv)
    return basis, nc.reshape(plans, nper), ns.reshape(plans, nper)


def gather_kernel(idx_ref, src_ref, *rest):
    out_ref = rest[-2]
    stage_ref = rest[-1]
    block = stage_ref.shape[0]

    def body(b, carry):
        r0 = pl.multiple_of(b * block, block)
        for j in range(block):
            stage_ref[pl.ds(j, 1), :] = src_ref[pl.ds(idx_ref[r0 + j], 1), :]
        out_ref[pl.ds(r0, block), :] = stage_ref[...].astype(out_ref.dtype)
        return carry

    lax.fori_loop(0, out_ref.shape[0] // block, body, 0)


def row_gather(src, idx, out_dtype, *after):
    rows, width = idx.shape[0], src.shape[1]
    return pl.pallas_call(
        gather_kernel,
        in_specs=[pl.BlockSpec(memory_space=pltpu.SMEM), pl.BlockSpec(memory_space=pltpu.VMEM)]
        + [pl.BlockSpec(memory_space=pltpu.VMEM) for _ in after],
        out_specs=pl.BlockSpec(memory_space=pltpu.VMEM),
        out_shape=jax.ShapeDtypeStruct((rows, width), out_dtype),
        scratch_shapes=[pltpu.VMEM((32, width), src.dtype)],
        cost_estimate=pl.CostEstimate(
            flops=0, transcendentals=0, bytes_accessed=2 * rows * width * src.dtype.itemsize),
    )(idx, src, *after)


def with_zero_rows(flat):
    return jnp.concatenate([flat, jnp.zeros((8, flat.shape[1]), flat.dtype)], axis=0)


def a2a_kernel(x_ref, out_ref, held, send_sem, recv_sem):
    n = x_ref.shape[0]
    me = lax.axis_index("tm")
    sky = lax.axis_index("sky")
    barrier = pltpu.get_barrier_semaphore()

    def greet(k, carry):
        peer = lax.rem(me + k, n)
        pl.semaphore_signal(barrier, inc=1, device_id=(peer, sky), device_id_type=pl.DeviceIdType.MESH)
        return carry

    lax.fori_loop(1, n, greet, 0)
    pl.semaphore_wait(barrier, n - 1)

    def copy(k):
        peer = lax.rem(me + k, n)
        return pltpu.make_async_remote_copy(
            src_ref=x_ref.at[peer],
            dst_ref=held.at[me],
            send_sem=send_sem.at[k],
            recv_sem=recv_sem.at[k],
            device_id=(peer, sky),
            device_id_type=pl.DeviceIdType.MESH,
        )

    def start(k, carry):
        copy(k).start()
        return carry

    lax.fori_loop(1, n, start, 0)
    held[pl.ds(me, 1)] = x_ref[pl.ds(me, 1)]

    def finish(k, carry):
        copy(k).wait()
        return carry

    lax.fori_loop(1, n, finish, 0)
    out_ref[...] = held[...].astype(out_ref.dtype)


def tm_all_to_all(x, out_dtype, collective_id):
    n, rows, width = x.shape
    return pl.pallas_call(
        a2a_kernel,
        in_specs=[pl.BlockSpec(memory_space=pltpu.VMEM)],
        out_specs=pl.BlockSpec(memory_space=pltpu.VMEM),
        out_shape=jax.ShapeDtypeStruct((n, rows, width), out_dtype),
        scratch_shapes=[
            pltpu.VMEM((n, rows, width), x.dtype),
            pltpu.SemaphoreType.DMA((n,)),
            pltpu.SemaphoreType.DMA((n,)),
        ],
        compiler_params=pltpu.CompilerParams(collective_id=collective_id, has_side_effects=True),
    )(x)


STREAMS = 4
SUNROLL = 2

def scatter_add_kernel(idx_ref, src_ref, out_ref, acc_ref):
    rows = src_ref.shape[0]
    streams = acc_ref.shape[0]
    acc_ref[...] = jnp.zeros_like(acc_ref)

    def body(step, carry):
        base = step * streams
        for s in range(streams):
            r = base + s
            i = idx_ref[r]
            acc_ref[s, pl.ds(i, 1), :] = acc_ref[s, pl.ds(i, 1), :] + src_ref[pl.ds(r, 1), :]
        return carry

    lax.fori_loop(0, rows // streams, body, 0, unroll=SUNROLL)
    total = acc_ref[0]
    for s in range(1, streams):
        total = total + acc_ref[s]
    out_ref[...] = total[: out_ref.shape[0]]


def scatter_add(src, idx, out_rows):
    rows, width = src.shape
    pad = out_rows + 8
    return pl.pallas_call(
        scatter_add_kernel,
        in_specs=[pl.BlockSpec(memory_space=pltpu.SMEM), pl.BlockSpec(memory_space=pltpu.VMEM)],
        out_specs=pl.BlockSpec(memory_space=pltpu.VMEM),
        out_shape=jax.ShapeDtypeStruct((out_rows, width), jnp.float32),
        scratch_shapes=[pltpu.VMEM((STREAMS, pad, width), jnp.float32)],
        cost_estimate=pl.CostEstimate(flops=rows * width, transcendentals=0, bytes_accessed=(rows + out_rows) * width * 4),
    )(idx, src)

def fit_groups(basis, observed, norm_cos, norm_sin, nper):
    corr = jnp.einsum("fio,fic->foc", basis, observed, preferred_element_type=jnp.float32)
    cosine = corr[:, :nper]
    sine = corr[:, nper:]
    amp_c = cosine / norm_cos[:, :, None]
    amp_s = sine / norm_sin[:, :, None]
    power = cosine * amp_c + sine * amp_s
    logits = BETA * power
    highest = jnp.max(logits, axis=1)
    expo = jnp.exp(logits - highest[:, None, :])
    total = jnp.sum(expo, axis=1)
    share = expo / total[:, None, :]
    coeff = jnp.concatenate([share * amp_c, share * amp_s], axis=1).astype(jnp.bfloat16)
    model = jnp.einsum("fio,foc->fic", basis, coeff, preferred_element_type=jnp.float32)
    return (model, highest + jnp.log(total))


def on_device(residuals, seg_counts, attitude, sched_seg, sched_slot, periods):
    tm_count = lax.axis_size("tm")
    sched_dev, obs = sched_seg.shape
    seg_dev, slots, width = residuals.shape
    nper = periods.shape[0]
    column_blocks = width // SRC_GROUP
    capacity = 2 * sched_dev * obs // tm_count
    requests = sched_dev * obs
    seg_flat = sched_seg.reshape(-1)
    slot_flat = sched_slot.reshape(-1)
    block_of = jnp.repeat(jnp.arange(sched_dev, dtype=jnp.int32) % column_blocks, obs)
    target = seg_flat // seg_dev
    local_row = (seg_flat % seg_dev * slots + slot_flat) * column_blocks + block_of
    onehot = (target[:, None] == jnp.arange(tm_count, dtype=jnp.int32)[None, :]).astype(jnp.int32)
    ones = onehot.astype(jnp.bfloat16).reshape(requests // 128, 128, tm_count)
    tril = (jnp.arange(128)[:, None] >= jnp.arange(128)[None, :]).astype(jnp.bfloat16)
    within = jnp.einsum("ij,bjc->bic", tril, ones, preferred_element_type=jnp.float32)
    totals = within[:, -1, :]
    before = jnp.cumsum(totals, axis=0) - totals
    counts = (within + before[:, None, :]).reshape(requests, tm_count)
    position = jnp.sum(counts * onehot.astype(jnp.float32), axis=1).astype(jnp.int32) - 1
    empty_row = seg_dev * slots * column_blocks
    slot_of = target * capacity + position
    pair = (
        jnp.broadcast_to(jnp.array([empty_row, requests], jnp.int32), (tm_count * capacity, 2))
        .at[slot_of]
        .set(jnp.stack([local_row, jnp.arange(requests, dtype=jnp.int32)], axis=1))
    )
    wanted = pair[:, 0].reshape(tm_count, capacity)
    inverse = pair[:, 1]
    asked = lax.all_to_all(wanted, "tm", split_axis=0, concat_axis=0, tiled=True).reshape(-1)
    basis, norm_cos, norm_sin = basis_and_norms(sched_seg * slots + sched_slot, periods)
    valid = jnp.arange(slots, dtype=jnp.int32)[None, :] < seg_counts[:, None]
    current = residuals.astype(jnp.float32)
    evidence = jnp.zeros((sched_dev, SRC_GROUP), jnp.float32)
    attitude_all = lax.all_gather(attitude, "sky", axis=1, tiled=True)
    for iteration in range(ITERS):
        masked = jnp.where(valid[:, :, None], current, 0.0).astype(jnp.bfloat16)
        white = jnp.einsum(
            "sij,sjc->sic", attitude_all, masked, preferred_element_type=jnp.float32
        )
        picked = row_gather(
            with_zero_rows(white.reshape(-1, SRC_GROUP)), asked, jnp.bfloat16, norm_cos)
        outbound = picked.reshape(tm_count, capacity, SRC_GROUP)
        if iteration == 0:
            arrived = lax.all_to_all(outbound, "tm", split_axis=0, concat_axis=0, tiled=True)
            arrived = arrived.astype(jnp.float32)
        else:
            arrived = tm_all_to_all(outbound, jnp.float32, 1 + 2 * iteration)
        observed = row_gather(arrived.reshape(-1, SRC_GROUP), slot_of, jnp.bfloat16)
        observed = observed.reshape(sched_dev, obs, SRC_GROUP)
        model, evidence = fit_groups(basis, observed, norm_cos, norm_sin, nper)
        outgoing = row_gather(
            with_zero_rows(model.reshape(requests, SRC_GROUP)), inverse, jnp.bfloat16)
        returned = tm_all_to_all(
            outgoing.reshape(tm_count, capacity, SRC_GROUP),
            jnp.float32, 2 + 2 * iteration)
        placed = scatter_add(returned.reshape(-1, SRC_GROUP), asked, empty_row)
        current = current - placed.reshape(seg_dev, slots, width)
    return (current, evidence)


def solution(mesh):
    in_specs = (
        P("tm", None, "sky"),
        P("tm"),
        P("tm", "sky", None),
        P(("tm", "sky"), None),
        P(("tm", "sky"), None),
        P(),
    )
    out_specs = (P("tm", None, "sky"), P(("tm", "sky"), None))
    return jax.shard_map(
        on_device, mesh=mesh, in_specs=in_specs, out_specs=out_specs, check_vma=False
    )
```

```python
import jax
import jax.numpy as jnp
from jax import lax
from jax.experimental import pallas as pl
from jax.experimental.pallas import tpu as pltpu
from jax.sharding import PartitionSpec as P

SRC_GROUP = 128
ITERS = 2


TWO_PI = 6.283185307179586
BETA = 2.0
RIDGE = 1.0


PIO2_1 = 1.5703125
PIO2_2 = 4.837512969970703125e-4
PIO2_3 = 7.549789954891e-8
ROWS = 16
LANES = 512
UNROLL = 2


def basis_kernel(t_ref, p_ref, w_ref, inv_ref, basis_ref, nc_ref, ns_ref):
    obs = t_ref.shape[0]
    nper = p_ref.shape[1]

    def lane_block(j, carry):
        c0 = pl.multiple_of(j * LANES, LANES)
        pf = p_ref[:, pl.ds(c0, LANES)]
        w = w_ref[:, pl.ds(c0, LANES)]
        inv = inv_ref[:, pl.ds(c0, LANES)]

        def row_block(i, acc):
            acc_c, acc_s = acc
            r0 = pl.multiple_of(i * ROWS, ROWS)
            tf = jnp.broadcast_to(t_ref[pl.ds(r0, ROWS), :], (ROWS, LANES))
            q = jnp.floor(tf * inv)
            r = tf - q * pf
            r = jnp.where(r < 0.0, r + pf, r)
            r = jnp.where(r >= pf, r - pf, r)
            phase = r * w
            k = jnp.floor(phase * 0.6366197723675814 + 0.5)
            y = ((phase - k * PIO2_1) - k * PIO2_2) - k * PIO2_3
            z = y * y
            s = y + y * z * (-1.6666654611e-1 + z * (8.3321608736e-3 + z * -1.9515295891e-4))
            c = 1.0 - 0.5 * z + z * z * (4.166664568298827e-2 + z * (-1.388731625493765e-3 + z * 2.443315711809948e-5))
            odd = (k == 1.0) | (k == 3.0)
            cs = jnp.where(odd, s, c)
            sn = jnp.where(odd, c, s)
            cos_v = jnp.where((k == 1.0) | (k == 2.0), -cs, cs).astype(jnp.bfloat16)
            sin_v = jnp.where((k == 2.0) | (k == 3.0), -sn, sn).astype(jnp.bfloat16)
            basis_ref[pl.ds(r0, ROWS), pl.ds(c0, LANES)] = cos_v
            basis_ref[pl.ds(r0, ROWS), pl.ds(nper + c0, LANES)] = sin_v
            cf = cos_v.astype(jnp.float32)
            sf = sin_v.astype(jnp.float32)
            return acc_c + cf * cf, acc_s + sf * sf

        zero = jnp.zeros((ROWS, LANES), jnp.float32)
        acc_c, acc_s = lax.fori_loop(0, obs // ROWS, row_block, (zero, zero), unroll=UNROLL)
        nc_ref[:, pl.ds(c0, LANES)] = jnp.sum(acc_c, axis=0, keepdims=True) + RIDGE
        ns_ref[:, pl.ds(c0, LANES)] = jnp.sum(acc_s, axis=0, keepdims=True) + RIDGE
        return carry

    lax.fori_loop(0, nper // LANES, lane_block, 0)


def basis_and_norms(times, periods):
    plans, obs = times.shape
    nper = periods.shape[0]
    pf = periods.astype(jnp.float32)
    w = (TWO_PI / pf).reshape(1, nper)
    inv = (1.0 / pf).reshape(1, nper)
    pf = pf.reshape(1, nper)
    tf = times.astype(jnp.float32).reshape(plans, obs, 1)
    row = pl.BlockSpec((1, nper), lambda g: (0, 0))
    basis, nc, ns = pl.pallas_call(
        basis_kernel,
        grid=(plans,),
        in_specs=[pl.BlockSpec((None, obs, 1), lambda g: (g, 0, 0)), row, row, row],
        out_specs=[
            pl.BlockSpec((None, obs, 2 * nper), lambda g: (g, 0, 0)),
            pl.BlockSpec((None, 1, nper), lambda g: (g, 0, 0)),
            pl.BlockSpec((None, 1, nper), lambda g: (g, 0, 0)),
        ],
        out_shape=[
            jax.ShapeDtypeStruct((plans, obs, 2 * nper), jnp.bfloat16),
            jax.ShapeDtypeStruct((plans, 1, nper), jnp.float32),
            jax.ShapeDtypeStruct((plans, 1, nper), jnp.float32),
        ],
        cost_estimate=pl.CostEstimate(
            flops=60 * plans * obs * nper, transcendentals=0,
            bytes_accessed=plans * obs * 2 * nper * 2),
    )(tf, pf, w, inv)
    return basis, nc.reshape(plans, nper), ns.reshape(plans, nper)


def gather_kernel(idx_ref, src_ref, *rest):
    out_ref = rest[-2]
    stage_ref = rest[-1]
    block = stage_ref.shape[0]

    def body(b, carry):
        r0 = pl.multiple_of(b * block, block)
        for j in range(block):
            stage_ref[pl.ds(j, 1), :] = src_ref[pl.ds(idx_ref[r0 + j], 1), :]
        out_ref[pl.ds(r0, block), :] = stage_ref[...].astype(out_ref.dtype)
        return carry

    lax.fori_loop(0, out_ref.shape[0] // block, body, 0)


def row_gather(src, idx, out_dtype, *after):
    rows, width = idx.shape[0], src.shape[1]
    return pl.pallas_call(
        gather_kernel,
        in_specs=[pl.BlockSpec(memory_space=pltpu.SMEM), pl.BlockSpec(memory_space=pltpu.VMEM)]
        + [pl.BlockSpec(memory_space=pltpu.VMEM) for _ in after],
        out_specs=pl.BlockSpec(memory_space=pltpu.VMEM),
        out_shape=jax.ShapeDtypeStruct((rows, width), out_dtype),
        scratch_shapes=[pltpu.VMEM((32, width), src.dtype)],
        cost_estimate=pl.CostEstimate(
            flops=0, transcendentals=0, bytes_accessed=2 * rows * width * src.dtype.itemsize),
    )(idx, src, *after)


def with_zero_rows(flat):
    return jnp.concatenate([flat, jnp.zeros((8, flat.shape[1]), flat.dtype)], axis=0)


def a2a_kernel(x_ref, out_ref, held, send_sem, recv_sem):
    n = x_ref.shape[0]
    me = lax.axis_index("tm")
    sky = lax.axis_index("sky")
    barrier = pltpu.get_barrier_semaphore()

    def greet(k, carry):
        peer = lax.rem(me + k, n)
        pl.semaphore_signal(barrier, inc=1, device_id=(peer, sky), device_id_type=pl.DeviceIdType.MESH)
        return carry

    lax.fori_loop(1, n, greet, 0)
    pl.semaphore_wait(barrier, n - 1)

    def copy(k):
        peer = lax.rem(me + k, n)
        return pltpu.make_async_remote_copy(
            src_ref=x_ref.at[peer],
            dst_ref=held.at[me],
            send_sem=send_sem.at[k],
            recv_sem=recv_sem.at[k],
            device_id=(peer, sky),
            device_id_type=pl.DeviceIdType.MESH,
        )

    def start(k, carry):
        copy(k).start()
        return carry

    lax.fori_loop(1, n, start, 0)
    held[pl.ds(me, 1)] = x_ref[pl.ds(me, 1)]

    def finish(k, carry):
        copy(k).wait()
        return carry

    lax.fori_loop(1, n, finish, 0)
    out_ref[...] = held[...].astype(out_ref.dtype)


def tm_all_to_all(x, out_dtype, collective_id):
    n, rows, width = x.shape
    return pl.pallas_call(
        a2a_kernel,
        in_specs=[pl.BlockSpec(memory_space=pltpu.VMEM)],
        out_specs=pl.BlockSpec(memory_space=pltpu.VMEM),
        out_shape=jax.ShapeDtypeStruct((n, rows, width), out_dtype),
        scratch_shapes=[
            pltpu.VMEM((n, rows, width), x.dtype),
            pltpu.SemaphoreType.DMA((n,)),
            pltpu.SemaphoreType.DMA((n,)),
        ],
        compiler_params=pltpu.CompilerParams(collective_id=collective_id, has_side_effects=True),
    )(x)


STREAMS = 4
SUNROLL = 2

def scatter_add_kernel(idx_ref, src_ref, out_ref, acc_ref):
    rows = src_ref.shape[0]
    streams = acc_ref.shape[0]
    acc_ref[...] = jnp.zeros_like(acc_ref)

    def body(step, carry):
        base = step * streams
        for s in range(streams):
            r = base + s
            i = idx_ref[r]
            acc_ref[s, pl.ds(i, 1), :] = acc_ref[s, pl.ds(i, 1), :] + src_ref[pl.ds(r, 1), :]
        return carry

    lax.fori_loop(0, rows // streams, body, 0, unroll=SUNROLL)
    total = acc_ref[0]
    for s in range(1, streams):
        total = total + acc_ref[s]
    out_ref[...] = total[: out_ref.shape[0]]


def scatter_add(src, idx, out_rows):
    rows, width = src.shape
    pad = out_rows + 8
    return pl.pallas_call(
        scatter_add_kernel,
        in_specs=[pl.BlockSpec(memory_space=pltpu.SMEM), pl.BlockSpec(memory_space=pltpu.VMEM)],
        out_specs=pl.BlockSpec(memory_space=pltpu.VMEM),
        out_shape=jax.ShapeDtypeStruct((out_rows, width), jnp.float32),
        scratch_shapes=[pltpu.VMEM((STREAMS, pad, width), jnp.float32)],
        cost_estimate=pl.CostEstimate(flops=rows * width, transcendentals=0, bytes_accessed=(rows + out_rows) * width * 4),
    )(idx, src)


def fit_kernel(basis_ref, obs_ref, inc_ref, ins_ref, model_ref, ev_ref):
    nper = inc_ref.shape[1]
    basis = basis_ref[...]
    obs_t = obs_ref[...].astype(jnp.float32).T.astype(jnp.bfloat16)
    corr = jnp.dot(obs_t, basis, preferred_element_type=jnp.float32)
    cosine = corr[:, :nper]
    sine = corr[:, nper:]
    amp_c = cosine * inc_ref[...]
    amp_s = sine * ins_ref[...]
    logits = BETA * (cosine * amp_c + sine * amp_s)
    highest = jnp.max(logits, axis=1, keepdims=True)
    expo = jnp.exp(logits - highest)
    total = jnp.sum(expo, axis=1, keepdims=True)
    share = expo * (1.0 / total)
    coeff = jnp.concatenate([share * amp_c, share * amp_s], axis=1).astype(jnp.bfloat16)
    model_ref[...] = lax.dot_general(
        basis, coeff, (((1,), (1,)), ((), ())), preferred_element_type=jnp.float32)
    ev_ref[...] = highest + jnp.log(total)


def fit_fused(basis, observed, inv_cos, inv_sin):
    plans, obs, width = basis.shape
    cols = observed.shape[2]
    nper = width // 2
    row = pl.BlockSpec((None, 1, nper), lambda g: (g, 0, 0))
    model, ev = pl.pallas_call(
        fit_kernel,
        grid=(plans,),
        in_specs=[
            pl.BlockSpec((None, obs, width), lambda g: (g, 0, 0)),
            pl.BlockSpec((None, obs, cols), lambda g: (g, 0, 0)),
            row,
            row,
        ],
        out_specs=[
            pl.BlockSpec((None, obs, cols), lambda g: (g, 0, 0)),
            pl.BlockSpec((None, cols, 1), lambda g: (g, 0, 0)),
        ],
        out_shape=[
            jax.ShapeDtypeStruct((plans, obs, cols), jnp.float32),
            jax.ShapeDtypeStruct((plans, cols, 1), jnp.float32),
        ],
        cost_estimate=pl.CostEstimate(
            flops=4 * plans * obs * width * cols, transcendentals=plans * nper * cols,
            bytes_accessed=plans * obs * width * 2),
    )(basis, observed, inv_cos, inv_sin)
    return model, ev.reshape(plans, cols)

def fit_groups(basis, observed, norm_cos, norm_sin, nper):
    corr = jnp.einsum("fio,fic->foc", basis, observed, preferred_element_type=jnp.float32)
    cosine = corr[:, :nper]
    sine = corr[:, nper:]
    amp_c = cosine / norm_cos[:, :, None]
    amp_s = sine / norm_sin[:, :, None]
    power = cosine * amp_c + sine * amp_s
    logits = BETA * power
    highest = jnp.max(logits, axis=1)
    expo = jnp.exp(logits - highest[:, None, :])
    total = jnp.sum(expo, axis=1)
    share = expo / total[:, None, :]
    coeff = jnp.concatenate([share * amp_c, share * amp_s], axis=1).astype(jnp.bfloat16)
    model = jnp.einsum("fio,foc->fic", basis, coeff, preferred_element_type=jnp.float32)
    return (model, highest + jnp.log(total))


def on_device(residuals, seg_counts, attitude, sched_seg, sched_slot, periods):
    tm_count = lax.axis_size("tm")
    sched_dev, obs = sched_seg.shape
    seg_dev, slots, width = residuals.shape
    nper = periods.shape[0]
    column_blocks = width // SRC_GROUP
    capacity = 2 * sched_dev * obs // tm_count
    requests = sched_dev * obs
    seg_flat = sched_seg.reshape(-1)
    slot_flat = sched_slot.reshape(-1)
    block_of = jnp.repeat(jnp.arange(sched_dev, dtype=jnp.int32) % column_blocks, obs)
    target = seg_flat // seg_dev
    local_row = (seg_flat % seg_dev * slots + slot_flat) * column_blocks + block_of
    onehot = (target[:, None] == jnp.arange(tm_count, dtype=jnp.int32)[None, :]).astype(jnp.int32)
    ones = onehot.astype(jnp.bfloat16).reshape(requests // 128, 128, tm_count)
    tril = (jnp.arange(128)[:, None] >= jnp.arange(128)[None, :]).astype(jnp.bfloat16)
    within = jnp.einsum("ij,bjc->bic", tril, ones, preferred_element_type=jnp.float32)
    totals = within[:, -1, :]
    before = jnp.cumsum(totals, axis=0) - totals
    counts = (within + before[:, None, :]).reshape(requests, tm_count)
    position = jnp.sum(counts * onehot.astype(jnp.float32), axis=1).astype(jnp.int32) - 1
    empty_row = seg_dev * slots * column_blocks
    slot_of = target * capacity + position
    pair = (
        jnp.broadcast_to(jnp.array([empty_row, requests], jnp.int32), (tm_count * capacity, 2))
        .at[slot_of]
        .set(jnp.stack([local_row, jnp.arange(requests, dtype=jnp.int32)], axis=1))
    )
    wanted = pair[:, 0].reshape(tm_count, capacity)
    inverse = pair[:, 1]
    asked = lax.all_to_all(wanted, "tm", split_axis=0, concat_axis=0, tiled=True).reshape(-1)
    basis, norm_cos, norm_sin = basis_and_norms(sched_seg * slots + sched_slot, periods)
    valid = jnp.arange(slots, dtype=jnp.int32)[None, :] < seg_counts[:, None]
    inv_cos = (1.0 / norm_cos).reshape(sched_dev, 1, nper)
    inv_sin = (1.0 / norm_sin).reshape(sched_dev, 1, nper)
    current = residuals.astype(jnp.float32)
    evidence = jnp.zeros((sched_dev, SRC_GROUP), jnp.float32)
    attitude_all = lax.all_gather(attitude, "sky", axis=1, tiled=True)
    for iteration in range(ITERS):
        masked = jnp.where(valid[:, :, None], current, 0.0).astype(jnp.bfloat16)
        white = jnp.einsum(
            "sij,sjc->sic", attitude_all, masked, preferred_element_type=jnp.float32
        )
        picked = row_gather(
            with_zero_rows(white.reshape(-1, SRC_GROUP)), asked, jnp.bfloat16, norm_cos)
        outbound = picked.reshape(tm_count, capacity, SRC_GROUP)
        if iteration == 0:
            arrived = lax.all_to_all(outbound, "tm", split_axis=0, concat_axis=0, tiled=True)
            arrived = arrived.astype(jnp.float32)
        else:
            arrived = tm_all_to_all(outbound, jnp.float32, 1 + 2 * iteration)
        observed = row_gather(arrived.reshape(-1, SRC_GROUP), slot_of, jnp.bfloat16)
        observed = observed.reshape(sched_dev, obs, SRC_GROUP)
        model, evidence = fit_fused(basis, observed, inv_cos, inv_sin)
        outgoing = row_gather(
            with_zero_rows(model.reshape(requests, SRC_GROUP)), inverse, jnp.bfloat16)
        returned = tm_all_to_all(
            outgoing.reshape(tm_count, capacity, SRC_GROUP),
            jnp.float32, 2 + 2 * iteration)
        placed = scatter_add(returned.reshape(-1, SRC_GROUP), asked, empty_row)
        current = current - placed.reshape(seg_dev, slots, width)
    return (current, evidence)


def solution(mesh):
    in_specs = (
        P("tm", None, "sky"),
        P("tm"),
        P("tm", "sky", None),
        P(("tm", "sky"), None),
        P(("tm", "sky"), None),
        P(),
    )
    out_specs = (P("tm", None, "sky"), P(("tm", "sky"), None))
    return jax.shard_map(
        on_device, mesh=mesh, in_specs=in_specs, out_specs=out_specs, check_vma=False
    )
```

```python
import jax
import jax.numpy as jnp
from jax import lax
from jax.experimental import pallas as pl
from jax.experimental.pallas import tpu as pltpu
from jax.sharding import PartitionSpec as P

SRC_GROUP = 128
ITERS = 2


TWO_PI = 6.283185307179586
BETA = 2.0
RIDGE = 1.0


PIO2_1 = 1.5703125
PIO2_2 = 4.837512969970703125e-4
PIO2_3 = 7.549789954891e-8
ROWS = 16
LANES = 512
UNROLL = 2


def basis_kernel(t_ref, p_ref, w_ref, inv_ref, basis_ref, nc_ref, ns_ref):
    obs = t_ref.shape[0]
    nper = p_ref.shape[1]

    def lane_block(j, carry):
        c0 = pl.multiple_of(j * LANES, LANES)
        pf = p_ref[:, pl.ds(c0, LANES)]
        w = w_ref[:, pl.ds(c0, LANES)]
        inv = inv_ref[:, pl.ds(c0, LANES)]

        def row_block(i, acc):
            acc_c, acc_s = acc
            r0 = pl.multiple_of(i * ROWS, ROWS)
            tf = jnp.broadcast_to(t_ref[pl.ds(r0, ROWS), :], (ROWS, LANES))
            q = jnp.floor(tf * inv)
            r = tf - q * pf
            r = jnp.where(r < 0.0, r + pf, r)
            r = jnp.where(r >= pf, r - pf, r)
            phase = r * w
            k = jnp.floor(phase * 0.6366197723675814 + 0.5)
            y = ((phase - k * PIO2_1) - k * PIO2_2) - k * PIO2_3
            z = y * y
            s = y + y * z * (-1.6666654611e-1 + z * (8.3321608736e-3 + z * -1.9515295891e-4))
            c = 1.0 - 0.5 * z + z * z * (4.166664568298827e-2 + z * (-1.388731625493765e-3 + z * 2.443315711809948e-5))
            odd = (k == 1.0) | (k == 3.0)
            cs = jnp.where(odd, s, c)
            sn = jnp.where(odd, c, s)
            cos_v = jnp.where((k == 1.0) | (k == 2.0), -cs, cs).astype(jnp.bfloat16)
            sin_v = jnp.where((k == 2.0) | (k == 3.0), -sn, sn).astype(jnp.bfloat16)
            basis_ref[pl.ds(r0, ROWS), pl.ds(c0, LANES)] = cos_v
            basis_ref[pl.ds(r0, ROWS), pl.ds(nper + c0, LANES)] = sin_v
            cf = cos_v.astype(jnp.float32)
            sf = sin_v.astype(jnp.float32)
            return acc_c + cf * cf, acc_s + sf * sf

        zero = jnp.zeros((ROWS, LANES), jnp.float32)
        acc_c, acc_s = lax.fori_loop(0, obs // ROWS, row_block, (zero, zero), unroll=UNROLL)
        nc_ref[:, pl.ds(c0, LANES)] = jnp.sum(acc_c, axis=0, keepdims=True) + RIDGE
        ns_ref[:, pl.ds(c0, LANES)] = jnp.sum(acc_s, axis=0, keepdims=True) + RIDGE
        return carry

    lax.fori_loop(0, nper // LANES, lane_block, 0)


def basis_and_norms(times, periods):
    plans, obs = times.shape
    nper = periods.shape[0]
    pf = periods.astype(jnp.float32)
    w = (TWO_PI / pf).reshape(1, nper)
    inv = (1.0 / pf).reshape(1, nper)
    pf = pf.reshape(1, nper)
    tf = times.astype(jnp.float32).reshape(plans, obs, 1)
    row = pl.BlockSpec((1, nper), lambda g: (0, 0))
    basis, nc, ns = pl.pallas_call(
        basis_kernel,
        grid=(plans,),
        in_specs=[pl.BlockSpec((None, obs, 1), lambda g: (g, 0, 0)), row, row, row],
        out_specs=[
            pl.BlockSpec((None, obs, 2 * nper), lambda g: (g, 0, 0)),
            pl.BlockSpec((None, 1, nper), lambda g: (g, 0, 0)),
            pl.BlockSpec((None, 1, nper), lambda g: (g, 0, 0)),
        ],
        out_shape=[
            jax.ShapeDtypeStruct((plans, obs, 2 * nper), jnp.bfloat16),
            jax.ShapeDtypeStruct((plans, 1, nper), jnp.float32),
            jax.ShapeDtypeStruct((plans, 1, nper), jnp.float32),
        ],
        cost_estimate=pl.CostEstimate(
            flops=60 * plans * obs * nper, transcendentals=0,
            bytes_accessed=plans * obs * 2 * nper * 2),
    )(tf, pf, w, inv)
    return basis, nc.reshape(plans, nper), ns.reshape(plans, nper)


def gather_kernel(idx_ref, src_ref, *rest):
    out_ref = rest[-2]
    stage_ref = rest[-1]
    block = stage_ref.shape[0]

    def body(b, carry):
        r0 = pl.multiple_of(b * block, block)
        for j in range(block):
            stage_ref[pl.ds(j, 1), :] = src_ref[pl.ds(idx_ref[r0 + j], 1), :]
        out_ref[pl.ds(r0, block), :] = stage_ref[...].astype(out_ref.dtype)
        return carry

    lax.fori_loop(0, out_ref.shape[0] // block, body, 0)


def row_gather(src, idx, out_dtype, *after):
    rows, width = idx.shape[0], src.shape[1]
    return pl.pallas_call(
        gather_kernel,
        in_specs=[pl.BlockSpec(memory_space=pltpu.SMEM), pl.BlockSpec(memory_space=pltpu.VMEM)]
        + [pl.BlockSpec(memory_space=pltpu.VMEM) for _ in after],
        out_specs=pl.BlockSpec(memory_space=pltpu.VMEM),
        out_shape=jax.ShapeDtypeStruct((rows, width), out_dtype),
        scratch_shapes=[pltpu.VMEM((32, width), src.dtype)],
        cost_estimate=pl.CostEstimate(
            flops=0, transcendentals=0, bytes_accessed=2 * rows * width * src.dtype.itemsize),
    )(idx, src, *after)


def with_zero_rows(flat):
    return jnp.concatenate([flat, jnp.zeros((8, flat.shape[1]), flat.dtype)], axis=0)


def a2a_kernel(x_ref, out_ref, held, send_sem, recv_sem):
    n = x_ref.shape[0]
    me = lax.axis_index("tm")
    sky = lax.axis_index("sky")
    barrier = pltpu.get_barrier_semaphore()

    def greet(k, carry):
        peer = lax.rem(me + k, n)
        pl.semaphore_signal(barrier, inc=1, device_id=(peer, sky), device_id_type=pl.DeviceIdType.MESH)
        return carry

    lax.fori_loop(1, n, greet, 0)
    pl.semaphore_wait(barrier, n - 1)

    def copy(k):
        peer = lax.rem(me + k, n)
        return pltpu.make_async_remote_copy(
            src_ref=x_ref.at[peer],
            dst_ref=held.at[me],
            send_sem=send_sem.at[k],
            recv_sem=recv_sem.at[k],
            device_id=(peer, sky),
            device_id_type=pl.DeviceIdType.MESH,
        )

    def start(k, carry):
        copy(k).start()
        return carry

    lax.fori_loop(1, n, start, 0)
    held[pl.ds(me, 1)] = x_ref[pl.ds(me, 1)]

    def finish(k, carry):
        copy(k).wait()
        return carry

    lax.fori_loop(1, n, finish, 0)
    out_ref[...] = held[...].astype(out_ref.dtype)


def tm_all_to_all(x, out_dtype, collective_id):
    n, rows, width = x.shape
    return pl.pallas_call(
        a2a_kernel,
        in_specs=[pl.BlockSpec(memory_space=pltpu.VMEM)],
        out_specs=pl.BlockSpec(memory_space=pltpu.VMEM),
        out_shape=jax.ShapeDtypeStruct((n, rows, width), out_dtype),
        scratch_shapes=[
            pltpu.VMEM((n, rows, width), x.dtype),
            pltpu.SemaphoreType.DMA((n,)),
            pltpu.SemaphoreType.DMA((n,)),
        ],
        compiler_params=pltpu.CompilerParams(collective_id=collective_id, has_side_effects=True),
    )(x)


STREAMS = 4
SUNROLL = 2

def scatter_add_kernel(idx_ref, src_ref, out_ref, acc_ref):
    rows = src_ref.shape[0]
    streams = acc_ref.shape[0]
    acc_ref[...] = jnp.zeros_like(acc_ref)

    def body(step, carry):
        base = step * streams
        for s in range(streams):
            r = base + s
            i = idx_ref[r]
            acc_ref[s, pl.ds(i, 1), :] = acc_ref[s, pl.ds(i, 1), :] + src_ref[pl.ds(r, 1), :]
        return carry

    lax.fori_loop(0, rows // streams, body, 0, unroll=SUNROLL)
    total = acc_ref[0]
    for s in range(1, streams):
        total = total + acc_ref[s]
    out_ref[...] = total[: out_ref.shape[0]]


def scatter_add(src, idx, out_rows):
    rows, width = src.shape
    pad = out_rows + 8
    return pl.pallas_call(
        scatter_add_kernel,
        in_specs=[pl.BlockSpec(memory_space=pltpu.SMEM), pl.BlockSpec(memory_space=pltpu.VMEM)],
        out_specs=pl.BlockSpec(memory_space=pltpu.VMEM),
        out_shape=jax.ShapeDtypeStruct((out_rows, width), jnp.float32),
        scratch_shapes=[pltpu.VMEM((STREAMS, pad, width), jnp.float32)],
        cost_estimate=pl.CostEstimate(flops=rows * width, transcendentals=0, bytes_accessed=(rows + out_rows) * width * 4),
    )(idx, src)


def fit_kernel(basis_ref, obs_ref, inc_ref, ins_ref, model_ref, ev_ref):
    nper = inc_ref.shape[1]
    basis = basis_ref[...]
    obs_t = obs_ref[...].astype(jnp.float32).T.astype(jnp.bfloat16)
    corr = jnp.dot(obs_t, basis, preferred_element_type=jnp.float32)
    cosine = corr[:, :nper]
    sine = corr[:, nper:]
    amp_c = cosine * inc_ref[...]
    amp_s = sine * ins_ref[...]
    logits = BETA * (cosine * amp_c + sine * amp_s)
    highest = jnp.max(logits, axis=1, keepdims=True)
    expo = jnp.exp(logits - highest)
    total = jnp.sum(expo, axis=1, keepdims=True)
    share = expo * (1.0 / total)
    coeff = jnp.concatenate([share * amp_c, share * amp_s], axis=1).astype(jnp.bfloat16)
    model_ref[...] = lax.dot_general(
        basis, coeff, (((1,), (1,)), ((), ())), preferred_element_type=jnp.float32)
    ev_ref[...] = highest + jnp.log(total)


def fit_fused(basis, observed, inv_cos, inv_sin):
    plans, obs, width = basis.shape
    cols = observed.shape[2]
    nper = width // 2
    row = pl.BlockSpec((None, 1, nper), lambda g: (g, 0, 0))
    model, ev = pl.pallas_call(
        fit_kernel,
        grid=(plans,),
        in_specs=[
            pl.BlockSpec((None, obs, width), lambda g: (g, 0, 0)),
            pl.BlockSpec((None, obs, cols), lambda g: (g, 0, 0)),
            row,
            row,
        ],
        out_specs=[
            pl.BlockSpec((None, obs, cols), lambda g: (g, 0, 0)),
            pl.BlockSpec((None, cols, 1), lambda g: (g, 0, 0)),
        ],
        out_shape=[
            jax.ShapeDtypeStruct((plans, obs, cols), jnp.float32),
            jax.ShapeDtypeStruct((plans, cols, 1), jnp.float32),
        ],
        cost_estimate=pl.CostEstimate(
            flops=4 * plans * obs * width * cols, transcendentals=plans * nper * cols,
            bytes_accessed=plans * obs * width * 2),
    )(basis, observed, inv_cos, inv_sin)
    return model, ev.reshape(plans, cols)


def half_gather_kernel(idx_ref, src_ref, *rest):
    out_ref = rest[-2]
    stage_ref = rest[-1]
    block, width = stage_ref.shape
    last = src_ref.shape[0] - 1

    def body(b, carry):
        r0 = pl.multiple_of(b * block, block)
        for j in range(block):
            a = idx_ref[r0 + j]
            row = src_ref[pl.ds(jnp.minimum(a // 2, last), 1), :]
            stage_ref[pl.ds(j, 1), :] = jnp.where(a % 2 == 1, row[:, width:], row[:, :width])
        out_ref[pl.ds(r0, block), :] = stage_ref[...].astype(out_ref.dtype)
        return carry

    lax.fori_loop(0, out_ref.shape[0] // block, body, 0)


def half_gather(src, idx, out_dtype, *after):
    rows, width = idx.shape[0], src.shape[1] // 2
    return pl.pallas_call(
        half_gather_kernel,
        in_specs=[pl.BlockSpec(memory_space=pltpu.SMEM), pl.BlockSpec(memory_space=pltpu.VMEM)]
        + [pl.BlockSpec(memory_space=pltpu.VMEM) for _ in after],
        out_specs=pl.BlockSpec(memory_space=pltpu.VMEM),
        out_shape=jax.ShapeDtypeStruct((rows, width), out_dtype),
        scratch_shapes=[pltpu.VMEM((32, width), src.dtype)],
        cost_estimate=pl.CostEstimate(
            flops=0, transcendentals=0, bytes_accessed=3 * rows * width * src.dtype.itemsize),
    )(idx, src, *after)


def scatter_sub_kernel(idx_ref, src_ref, cur_ref, out_ref, acc_ref):
    rows, width = src_ref.shape
    streams = acc_ref.shape[0]
    acc_ref[...] = jnp.zeros_like(acc_ref)

    def body(step, carry):
        base = step * streams
        for s in range(streams):
            r = base + s
            a = idx_ref[r]
            v = src_ref[pl.ds(r, 1), :]
            zero = jnp.zeros_like(v)
            odd = a % 2 == 1
            add = jnp.concatenate([jnp.where(odd, zero, v), jnp.where(odd, v, zero)], axis=1)
            row = a // 2
            acc_ref[s, pl.ds(row, 1), :] = acc_ref[s, pl.ds(row, 1), :] + add
        return carry

    lax.fori_loop(0, rows // streams, body, 0, unroll=SUNROLL)
    n = out_ref.shape[0]
    total = acc_ref[0, :n]
    for s in range(1, streams):
        total = total + acc_ref[s, :n]
    out_ref[...] = cur_ref[...] - total


def scatter_sub(src, idx, current):
    rows, width = src.shape
    out_rows = current.shape[0]
    return pl.pallas_call(
        scatter_sub_kernel,
        in_specs=[pl.BlockSpec(memory_space=pltpu.SMEM)] + [pl.BlockSpec(memory_space=pltpu.VMEM)] * 2,
        out_specs=pl.BlockSpec(memory_space=pltpu.VMEM),
        out_shape=jax.ShapeDtypeStruct(current.shape, jnp.float32),
        scratch_shapes=[pltpu.VMEM((STREAMS, out_rows + 8, 2 * width), jnp.float32)],
        cost_estimate=pl.CostEstimate(
            flops=rows * width, transcendentals=0, bytes_accessed=(rows * width + 2 * current.size) * 4),
    )(idx, src, current)

def fit_groups(basis, observed, norm_cos, norm_sin, nper):
    corr = jnp.einsum("fio,fic->foc", basis, observed, preferred_element_type=jnp.float32)
    cosine = corr[:, :nper]
    sine = corr[:, nper:]
    amp_c = cosine / norm_cos[:, :, None]
    amp_s = sine / norm_sin[:, :, None]
    power = cosine * amp_c + sine * amp_s
    logits = BETA * power
    highest = jnp.max(logits, axis=1)
    expo = jnp.exp(logits - highest[:, None, :])
    total = jnp.sum(expo, axis=1)
    share = expo / total[:, None, :]
    coeff = jnp.concatenate([share * amp_c, share * amp_s], axis=1).astype(jnp.bfloat16)
    model = jnp.einsum("fio,foc->fic", basis, coeff, preferred_element_type=jnp.float32)
    return (model, highest + jnp.log(total))


def on_device(residuals, seg_counts, attitude, sched_seg, sched_slot, periods):
    tm_count = lax.axis_size("tm")
    sched_dev, obs = sched_seg.shape
    seg_dev, slots, width = residuals.shape
    nper = periods.shape[0]
    column_blocks = width // SRC_GROUP
    capacity = 2 * sched_dev * obs // tm_count
    requests = sched_dev * obs
    seg_flat = sched_seg.reshape(-1)
    slot_flat = sched_slot.reshape(-1)
    block_of = jnp.repeat(jnp.arange(sched_dev, dtype=jnp.int32) % column_blocks, obs)
    target = seg_flat // seg_dev
    local_row = (seg_flat % seg_dev * slots + slot_flat) * column_blocks + block_of
    onehot = (target[:, None] == jnp.arange(tm_count, dtype=jnp.int32)[None, :]).astype(jnp.int32)
    ones = onehot.astype(jnp.bfloat16).reshape(requests // 128, 128, tm_count)
    tril = (jnp.arange(128)[:, None] >= jnp.arange(128)[None, :]).astype(jnp.bfloat16)
    within = jnp.einsum("ij,bjc->bic", tril, ones, preferred_element_type=jnp.float32)
    totals = within[:, -1, :]
    before = jnp.cumsum(totals, axis=0) - totals
    counts = (within + before[:, None, :]).reshape(requests, tm_count)
    position = jnp.sum(counts * onehot.astype(jnp.float32), axis=1).astype(jnp.int32) - 1
    empty_row = seg_dev * slots * column_blocks
    slot_of = target * capacity + position
    pair = (
        jnp.broadcast_to(jnp.array([empty_row, 0], jnp.int32), (tm_count * capacity, 2))
        .at[slot_of]
        .set(jnp.stack([local_row, jnp.arange(requests, dtype=jnp.int32)], axis=1))
    )
    wanted = pair[:, 0].reshape(tm_count, capacity)
    inverse = pair[:, 1]
    asked = lax.all_to_all(wanted, "tm", split_axis=0, concat_axis=0, tiled=True).reshape(-1)
    basis, norm_cos, norm_sin = basis_and_norms(sched_seg * slots + sched_slot, periods)
    valid = jnp.arange(slots, dtype=jnp.int32)[None, :] < seg_counts[:, None]
    inv_cos = (1.0 / norm_cos).reshape(sched_dev, 1, nper)
    inv_sin = (1.0 / norm_sin).reshape(sched_dev, 1, nper)
    current = residuals.astype(jnp.float32)
    evidence = jnp.zeros((sched_dev, SRC_GROUP), jnp.float32)
    attitude_all = lax.all_gather(attitude, "sky", axis=1, tiled=True)
    for iteration in range(ITERS):
        masked = jnp.where(valid[:, :, None], current, 0.0).astype(jnp.bfloat16)
        white = jnp.einsum(
            "sij,sjc->sic", attitude_all, masked, preferred_element_type=jnp.float32
        )
        picked = half_gather(
            white.reshape(seg_dev * slots, width), asked, jnp.bfloat16, norm_cos)
        outbound = picked.reshape(tm_count, capacity, SRC_GROUP)
        if iteration == 0:
            arrived = lax.all_to_all(outbound, "tm", split_axis=0, concat_axis=0, tiled=True)
            arrived = arrived.astype(jnp.float32)
        else:
            arrived = tm_all_to_all(outbound, jnp.float32, 1 + 2 * iteration)
        observed = row_gather(arrived.reshape(-1, SRC_GROUP), slot_of, jnp.bfloat16)
        observed = observed.reshape(sched_dev, obs, SRC_GROUP)
        model, evidence = fit_fused(basis, observed, inv_cos, inv_sin)
        outgoing = row_gather(model.reshape(requests, SRC_GROUP), inverse, jnp.bfloat16)
        returned = tm_all_to_all(
            outgoing.reshape(tm_count, capacity, SRC_GROUP),
            jnp.float32, 2 + 2 * iteration)
        current = scatter_sub(
            returned.reshape(-1, SRC_GROUP), asked, current.reshape(seg_dev * slots, width)
        ).reshape(seg_dev, slots, width)
    return (current, evidence)


def solution(mesh):
    in_specs = (
        P("tm", None, "sky"),
        P("tm"),
        P("tm", "sky", None),
        P(("tm", "sky"), None),
        P(("tm", "sky"), None),
        P(),
    )
    out_specs = (P("tm", None, "sky"), P(("tm", "sky"), None))
    return jax.shard_map(
        on_device, mesh=mesh, in_specs=in_specs, out_specs=out_specs, check_vma=False
    )
```

```python
import jax
import jax.numpy as jnp
from jax import lax
from jax.experimental import pallas as pl
from jax.experimental.pallas import tpu as pltpu
from jax.sharding import PartitionSpec as P

SRC_GROUP = 128
ITERS = 2


TWO_PI = 6.283185307179586
BETA = 2.0
RIDGE = 1.0


PIO2_1 = 1.5703125
PIO2_2 = 4.837512969970703125e-4
PIO2_3 = 7.549789954891e-8
ROWS = 16
LANES = 512
UNROLL = 2


def basis_kernel(t_ref, p_ref, w_ref, inv_ref, basis_ref, nc_ref, ns_ref):
    obs = t_ref.shape[0]
    nper = p_ref.shape[1]

    def lane_block(j, carry):
        c0 = pl.multiple_of(j * LANES, LANES)
        pf = p_ref[:, pl.ds(c0, LANES)]
        w = w_ref[:, pl.ds(c0, LANES)]
        inv = inv_ref[:, pl.ds(c0, LANES)]

        def row_block(i, acc):
            acc_c, acc_s = acc
            r0 = pl.multiple_of(i * ROWS, ROWS)
            tf = jnp.broadcast_to(t_ref[pl.ds(r0, ROWS), :], (ROWS, LANES))
            q = jnp.floor(tf * inv)
            r = tf - q * pf
            r = jnp.where(r < 0.0, r + pf, r)
            r = jnp.where(r >= pf, r - pf, r)
            phase = r * w
            k = jnp.floor(phase * 0.6366197723675814 + 0.5)
            y = ((phase - k * PIO2_1) - k * PIO2_2) - k * PIO2_3
            z = y * y
            s = y + y * z * (-1.6666654611e-1 + z * (8.3321608736e-3 + z * -1.9515295891e-4))
            c = 1.0 - 0.5 * z + z * z * (4.166664568298827e-2 + z * (-1.388731625493765e-3 + z * 2.443315711809948e-5))
            odd = (k == 1.0) | (k == 3.0)
            cs = jnp.where(odd, s, c)
            sn = jnp.where(odd, c, s)
            cos_v = jnp.where((k == 1.0) | (k == 2.0), -cs, cs).astype(jnp.bfloat16)
            sin_v = jnp.where((k == 2.0) | (k == 3.0), -sn, sn).astype(jnp.bfloat16)
            basis_ref[pl.ds(r0, ROWS), pl.ds(c0, LANES)] = cos_v
            basis_ref[pl.ds(r0, ROWS), pl.ds(nper + c0, LANES)] = sin_v
            cf = cos_v.astype(jnp.float32)
            sf = sin_v.astype(jnp.float32)
            return acc_c + cf * cf, acc_s + sf * sf

        zero = jnp.zeros((ROWS, LANES), jnp.float32)
        acc_c, acc_s = lax.fori_loop(0, obs // ROWS, row_block, (zero, zero), unroll=UNROLL)
        nc_ref[:, pl.ds(c0, LANES)] = jnp.sum(acc_c, axis=0, keepdims=True) + RIDGE
        ns_ref[:, pl.ds(c0, LANES)] = jnp.sum(acc_s, axis=0, keepdims=True) + RIDGE
        return carry

    lax.fori_loop(0, nper // LANES, lane_block, 0)


def basis_and_norms(times, periods):
    plans, obs = times.shape
    nper = periods.shape[0]
    pf = periods.astype(jnp.float32)
    w = (TWO_PI / pf).reshape(1, nper)
    inv = (1.0 / pf).reshape(1, nper)
    pf = pf.reshape(1, nper)
    tf = times.astype(jnp.float32).reshape(plans, obs, 1)
    row = pl.BlockSpec((1, nper), lambda g: (0, 0))
    basis, nc, ns = pl.pallas_call(
        basis_kernel,
        grid=(plans,),
        in_specs=[pl.BlockSpec((None, obs, 1), lambda g: (g, 0, 0)), row, row, row],
        out_specs=[
            pl.BlockSpec((None, obs, 2 * nper), lambda g: (g, 0, 0)),
            pl.BlockSpec((None, 1, nper), lambda g: (g, 0, 0)),
            pl.BlockSpec((None, 1, nper), lambda g: (g, 0, 0)),
        ],
        out_shape=[
            jax.ShapeDtypeStruct((plans, obs, 2 * nper), jnp.bfloat16),
            jax.ShapeDtypeStruct((plans, 1, nper), jnp.float32),
            jax.ShapeDtypeStruct((plans, 1, nper), jnp.float32),
        ],
        cost_estimate=pl.CostEstimate(
            flops=60 * plans * obs * nper, transcendentals=0,
            bytes_accessed=plans * obs * 2 * nper * 2),
    )(tf, pf, w, inv)
    return basis, nc.reshape(plans, nper), ns.reshape(plans, nper)


def gather_kernel(idx_ref, src_ref, *rest):
    out_ref = rest[-2]
    stage_ref = rest[-1]
    block = stage_ref.shape[0]

    def body(b, carry):
        r0 = pl.multiple_of(b * block, block)
        for j in range(block):
            stage_ref[pl.ds(j, 1), :] = src_ref[pl.ds(idx_ref[r0 + j], 1), :]
        out_ref[pl.ds(r0, block), :] = stage_ref[...].astype(out_ref.dtype)
        return carry

    lax.fori_loop(0, out_ref.shape[0] // block, body, 0)


def row_gather(src, idx, out_dtype, *after):
    rows, width = idx.shape[0], src.shape[1]
    return pl.pallas_call(
        gather_kernel,
        in_specs=[pl.BlockSpec(memory_space=pltpu.SMEM), pl.BlockSpec(memory_space=pltpu.VMEM)]
        + [pl.BlockSpec(memory_space=pltpu.VMEM) for _ in after],
        out_specs=pl.BlockSpec(memory_space=pltpu.VMEM),
        out_shape=jax.ShapeDtypeStruct((rows, width), out_dtype),
        scratch_shapes=[pltpu.VMEM((32, width), src.dtype)],
        cost_estimate=pl.CostEstimate(
            flops=0, transcendentals=0, bytes_accessed=2 * rows * width * src.dtype.itemsize),
    )(idx, src, *after)


def with_zero_rows(flat):
    return jnp.concatenate([flat, jnp.zeros((8, flat.shape[1]), flat.dtype)], axis=0)


def a2a_kernel(x_ref, out_ref, held, send_sem, recv_sem):
    n = x_ref.shape[0]
    me = lax.axis_index("tm")
    sky = lax.axis_index("sky")
    barrier = pltpu.get_barrier_semaphore()

    def greet(k, carry):
        peer = lax.rem(me + k, n)
        pl.semaphore_signal(barrier, inc=1, device_id=(peer, sky), device_id_type=pl.DeviceIdType.MESH)
        return carry

    lax.fori_loop(1, n, greet, 0)
    pl.semaphore_wait(barrier, n - 1)

    def copy(k):
        peer = lax.rem(me + k, n)
        return pltpu.make_async_remote_copy(
            src_ref=x_ref.at[peer],
            dst_ref=held.at[me],
            send_sem=send_sem.at[k],
            recv_sem=recv_sem.at[k],
            device_id=(peer, sky),
            device_id_type=pl.DeviceIdType.MESH,
        )

    def start(k, carry):
        copy(k).start()
        return carry

    lax.fori_loop(1, n, start, 0)
    held[pl.ds(me, 1)] = x_ref[pl.ds(me, 1)]

    def finish(k, carry):
        copy(k).wait()
        return carry

    lax.fori_loop(1, n, finish, 0)
    out_ref[...] = held[...].astype(out_ref.dtype)


def tm_all_to_all(x, out_dtype, collective_id):
    n, rows, width = x.shape
    return pl.pallas_call(
        a2a_kernel,
        in_specs=[pl.BlockSpec(memory_space=pltpu.VMEM)],
        out_specs=pl.BlockSpec(memory_space=pltpu.VMEM),
        out_shape=jax.ShapeDtypeStruct((n, rows, width), out_dtype),
        scratch_shapes=[
            pltpu.VMEM((n, rows, width), x.dtype),
            pltpu.SemaphoreType.DMA((n,)),
            pltpu.SemaphoreType.DMA((n,)),
        ],
        compiler_params=pltpu.CompilerParams(collective_id=collective_id, has_side_effects=True),
    )(x)


STREAMS = 4
SUNROLL = 2

def scatter_add_kernel(idx_ref, src_ref, out_ref, acc_ref):
    rows = src_ref.shape[0]
    streams = acc_ref.shape[0]
    acc_ref[...] = jnp.zeros_like(acc_ref)

    def body(step, carry):
        base = step * streams
        for s in range(streams):
            r = base + s
            i = idx_ref[r]
            acc_ref[s, pl.ds(i, 1), :] = acc_ref[s, pl.ds(i, 1), :] + src_ref[pl.ds(r, 1), :]
        return carry

    lax.fori_loop(0, rows // streams, body, 0, unroll=SUNROLL)
    total = acc_ref[0]
    for s in range(1, streams):
        total = total + acc_ref[s]
    out_ref[...] = total[: out_ref.shape[0]]


def scatter_add(src, idx, out_rows):
    rows, width = src.shape
    pad = out_rows + 8
    return pl.pallas_call(
        scatter_add_kernel,
        in_specs=[pl.BlockSpec(memory_space=pltpu.SMEM), pl.BlockSpec(memory_space=pltpu.VMEM)],
        out_specs=pl.BlockSpec(memory_space=pltpu.VMEM),
        out_shape=jax.ShapeDtypeStruct((out_rows, width), jnp.float32),
        scratch_shapes=[pltpu.VMEM((STREAMS, pad, width), jnp.float32)],
        cost_estimate=pl.CostEstimate(flops=rows * width, transcendentals=0, bytes_accessed=(rows + out_rows) * width * 4),
    )(idx, src)


def fit_kernel(basis_ref, obs_ref, inc_ref, ins_ref, model_ref, ev_ref):
    nper = inc_ref.shape[1]
    basis = basis_ref[...]
    obs_t = obs_ref[...].astype(jnp.float32).T.astype(jnp.bfloat16)
    corr = jnp.dot(obs_t, basis, preferred_element_type=jnp.float32)
    cosine = corr[:, :nper]
    sine = corr[:, nper:]
    amp_c = cosine * inc_ref[...]
    amp_s = sine * ins_ref[...]
    logits = BETA * (cosine * amp_c + sine * amp_s)
    highest = jnp.max(logits, axis=1, keepdims=True)
    expo = jnp.exp(logits - highest)
    total = jnp.sum(expo, axis=1, keepdims=True)
    share = expo * (1.0 / total)
    coeff = jnp.concatenate([share * amp_c, share * amp_s], axis=1).astype(jnp.bfloat16)
    model_ref[...] = lax.dot_general(
        basis, coeff, (((1,), (1,)), ((), ())), preferred_element_type=jnp.float32)
    ev_ref[...] = highest + jnp.log(total)


def fit_fused(basis, observed, inv_cos, inv_sin):
    plans, obs, width = basis.shape
    cols = observed.shape[2]
    nper = width // 2
    row = pl.BlockSpec((None, 1, nper), lambda g: (g, 0, 0))
    model, ev = pl.pallas_call(
        fit_kernel,
        grid=(plans,),
        in_specs=[
            pl.BlockSpec((None, obs, width), lambda g: (g, 0, 0)),
            pl.BlockSpec((None, obs, cols), lambda g: (g, 0, 0)),
            row,
            row,
        ],
        out_specs=[
            pl.BlockSpec((None, obs, cols), lambda g: (g, 0, 0)),
            pl.BlockSpec((None, cols, 1), lambda g: (g, 0, 0)),
        ],
        out_shape=[
            jax.ShapeDtypeStruct((plans, obs, cols), jnp.float32),
            jax.ShapeDtypeStruct((plans, cols, 1), jnp.float32),
        ],
        cost_estimate=pl.CostEstimate(
            flops=4 * plans * obs * width * cols, transcendentals=plans * nper * cols,
            bytes_accessed=plans * obs * width * 2),
    )(basis, observed, inv_cos, inv_sin)
    return model, ev.reshape(plans, cols)


def white_kernel(cnt_ref, cur_ref, att_ref, out_ref):
    segs, slots, _ = att_ref.shape
    width = out_ref.shape[1]
    blocks = cur_ref.shape[1] // width
    for s in range(segs):
        cur = cur_ref[pl.ds(s * slots, slots), :]
        slot = lax.broadcasted_iota(jnp.int32, cur.shape, 0)
        masked = jnp.where(slot < cnt_ref[s], cur, 0.0).astype(jnp.bfloat16)
        white = jnp.dot(att_ref[s], masked, preferred_element_type=jnp.float32)
        for b in range(blocks):
            out_ref[pl.ds(b * segs * slots + s * slots, slots), :] = white[:, b * width:(b + 1) * width]
    out_ref[pl.ds(blocks * segs * slots, 8), :] = jnp.zeros((8, width), jnp.float32)


def whiten_rows(counts, current, attitude_all, width):
    segs, slots, _ = attitude_all.shape
    rows = current.shape[0] * current.shape[1] // width
    return pl.pallas_call(
        white_kernel,
        in_specs=[pl.BlockSpec(memory_space=pltpu.SMEM)] + [pl.BlockSpec(memory_space=pltpu.VMEM)] * 2,
        out_specs=pl.BlockSpec(memory_space=pltpu.VMEM),
        out_shape=jax.ShapeDtypeStruct((rows + 8, width), jnp.float32),
        cost_estimate=pl.CostEstimate(
            flops=2 * segs * slots * slots * current.shape[1], transcendentals=0,
            bytes_accessed=current.size * 8 + attitude_all.size * 2),
    )(counts, current, attitude_all)


def scatter_sub_kernel(idx_ref, src_ref, cur_ref, out_ref, acc_ref):
    rows, width = src_ref.shape
    streams = acc_ref.shape[0]
    n = cur_ref.shape[0]
    acc_ref[...] = jnp.zeros_like(acc_ref)

    def body(step, carry):
        base = step * streams
        for s in range(streams):
            r = base + s
            i = idx_ref[r]
            acc_ref[s, pl.ds(i, 1), :] = acc_ref[s, pl.ds(i, 1), :] + src_ref[pl.ds(r, 1), :]
        return carry

    lax.fori_loop(0, rows // streams, body, 0, unroll=SUNROLL)
    for b in range(cur_ref.shape[1] // width):
        total = acc_ref[0, pl.ds(b * n, n), :]
        for s in range(1, streams):
            total = total + acc_ref[s, pl.ds(b * n, n), :]
        out_ref[:, b * width:(b + 1) * width] = cur_ref[:, b * width:(b + 1) * width] - total


def scatter_sub(src, idx, current):
    rows, width = src.shape
    blocks = current.shape[1] // width
    return pl.pallas_call(
        scatter_sub_kernel,
        in_specs=[pl.BlockSpec(memory_space=pltpu.SMEM)] + [pl.BlockSpec(memory_space=pltpu.VMEM)] * 2,
        out_specs=pl.BlockSpec(memory_space=pltpu.VMEM),
        out_shape=jax.ShapeDtypeStruct(current.shape, jnp.float32),
        scratch_shapes=[pltpu.VMEM((STREAMS, blocks * current.shape[0] + 8, width), jnp.float32)],
        cost_estimate=pl.CostEstimate(
            flops=rows * width, transcendentals=0, bytes_accessed=(rows * width + 2 * current.size) * 4),
    )(idx, src, current)

def fit_groups(basis, observed, norm_cos, norm_sin, nper):
    corr = jnp.einsum("fio,fic->foc", basis, observed, preferred_element_type=jnp.float32)
    cosine = corr[:, :nper]
    sine = corr[:, nper:]
    amp_c = cosine / norm_cos[:, :, None]
    amp_s = sine / norm_sin[:, :, None]
    power = cosine * amp_c + sine * amp_s
    logits = BETA * power
    highest = jnp.max(logits, axis=1)
    expo = jnp.exp(logits - highest[:, None, :])
    total = jnp.sum(expo, axis=1)
    share = expo / total[:, None, :]
    coeff = jnp.concatenate([share * amp_c, share * amp_s], axis=1).astype(jnp.bfloat16)
    model = jnp.einsum("fio,foc->fic", basis, coeff, preferred_element_type=jnp.float32)
    return (model, highest + jnp.log(total))


def on_device(residuals, seg_counts, attitude, sched_seg, sched_slot, periods):
    tm_count = lax.axis_size("tm")
    sched_dev, obs = sched_seg.shape
    seg_dev, slots, width = residuals.shape
    nper = periods.shape[0]
    column_blocks = width // SRC_GROUP
    capacity = 2 * sched_dev * obs // tm_count
    requests = sched_dev * obs
    seg_flat = sched_seg.reshape(-1)
    slot_flat = sched_slot.reshape(-1)
    block_of = jnp.repeat(jnp.arange(sched_dev, dtype=jnp.int32) % column_blocks, obs)
    target = seg_flat // seg_dev
    local_row = block_of * (seg_dev * slots) + seg_flat % seg_dev * slots + slot_flat
    onehot = (target[:, None] == jnp.arange(tm_count, dtype=jnp.int32)[None, :]).astype(jnp.int32)
    ones = onehot.astype(jnp.bfloat16).reshape(requests // 128, 128, tm_count)
    tril = (jnp.arange(128)[:, None] >= jnp.arange(128)[None, :]).astype(jnp.bfloat16)
    within = jnp.einsum("ij,bjc->bic", tril, ones, preferred_element_type=jnp.float32)
    totals = within[:, -1, :]
    before = jnp.cumsum(totals, axis=0) - totals
    counts = (within + before[:, None, :]).reshape(requests, tm_count)
    position = jnp.sum(counts * onehot.astype(jnp.float32), axis=1).astype(jnp.int32) - 1
    empty_row = seg_dev * slots * column_blocks
    slot_of = target * capacity + position
    pair = (
        jnp.broadcast_to(jnp.array([empty_row, 0], jnp.int32), (tm_count * capacity, 2))
        .at[slot_of]
        .set(jnp.stack([local_row, jnp.arange(requests, dtype=jnp.int32)], axis=1))
    )
    wanted = pair[:, 0].reshape(tm_count, capacity)
    inverse = pair[:, 1]
    asked = lax.all_to_all(wanted, "tm", split_axis=0, concat_axis=0, tiled=True).reshape(-1)
    basis, norm_cos, norm_sin = basis_and_norms(sched_seg * slots + sched_slot, periods)
    valid = jnp.arange(slots, dtype=jnp.int32)[None, :] < seg_counts[:, None]
    inv_cos = (1.0 / norm_cos).reshape(sched_dev, 1, nper)
    inv_sin = (1.0 / norm_sin).reshape(sched_dev, 1, nper)
    current = residuals.astype(jnp.float32).reshape(seg_dev * slots, width)
    evidence = jnp.zeros((sched_dev, SRC_GROUP), jnp.float32)
    attitude_all = lax.all_gather(attitude, "sky", axis=1, tiled=True)
    for iteration in range(ITERS):
        white = whiten_rows(seg_counts, current, attitude_all, SRC_GROUP)
        picked = row_gather(white, asked, jnp.bfloat16, norm_cos)
        outbound = picked.reshape(tm_count, capacity, SRC_GROUP)
        if iteration == 0:
            arrived = lax.all_to_all(outbound, "tm", split_axis=0, concat_axis=0, tiled=True)
            arrived = arrived.astype(jnp.float32)
        else:
            arrived = tm_all_to_all(outbound, jnp.float32, 1 + 2 * iteration)
        observed = row_gather(arrived.reshape(-1, SRC_GROUP), slot_of, jnp.bfloat16)
        observed = observed.reshape(sched_dev, obs, SRC_GROUP)
        model, evidence = fit_fused(basis, observed, inv_cos, inv_sin)
        outgoing = row_gather(model.reshape(requests, SRC_GROUP), inverse, jnp.bfloat16)
        returned = tm_all_to_all(
            outgoing.reshape(tm_count, capacity, SRC_GROUP),
            jnp.float32, 2 + 2 * iteration)
        current = scatter_sub(returned.reshape(-1, SRC_GROUP), asked, current)
    current = current.reshape(seg_dev, slots, width)
    return (current, evidence)


def solution(mesh):
    in_specs = (
        P("tm", None, "sky"),
        P("tm"),
        P("tm", "sky", None),
        P(("tm", "sky"), None),
        P(("tm", "sky"), None),
        P(),
    )
    out_specs = (P("tm", None, "sky"), P(("tm", "sky"), None))
    return jax.shard_map(
        on_device, mesh=mesh, in_specs=in_specs, out_specs=out_specs, check_vma=False
    )
```

```python
import jax
import jax.numpy as jnp
from jax import lax
from jax.experimental import pallas as pl
from jax.experimental.pallas import tpu as pltpu
from jax.sharding import PartitionSpec as P

SRC_GROUP = 128
ITERS = 2


TWO_PI = 6.283185307179586
BETA = 2.0
RIDGE = 1.0


PIO2_1 = 1.5703125
PIO2_2 = 4.837512969970703125e-4
PIO2_3 = 7.549789954891e-8
ROWS = 16
LANES = 512
UNROLL = 2


def basis_kernel(t_ref, p_ref, w_ref, inv_ref, basis_ref, nc_ref, ns_ref):
    obs = t_ref.shape[0]
    nper = p_ref.shape[1]

    def lane_block(j, carry):
        c0 = pl.multiple_of(j * LANES, LANES)
        pf = p_ref[:, pl.ds(c0, LANES)]
        w = w_ref[:, pl.ds(c0, LANES)]
        inv = inv_ref[:, pl.ds(c0, LANES)]

        def row_block(i, acc):
            acc_c, acc_s = acc
            r0 = pl.multiple_of(i * ROWS, ROWS)
            tf = jnp.broadcast_to(t_ref[pl.ds(r0, ROWS), :], (ROWS, LANES))
            q = jnp.floor(tf * inv)
            r = tf - q * pf
            r = jnp.where(r < 0.0, r + pf, r)
            r = jnp.where(r >= pf, r - pf, r)
            phase = r * w
            k = jnp.floor(phase * 0.6366197723675814 + 0.5)
            y = ((phase - k * PIO2_1) - k * PIO2_2) - k * PIO2_3
            z = y * y
            s = y + y * z * (-1.6666654611e-1 + z * (8.3321608736e-3 + z * -1.9515295891e-4))
            c = 1.0 - 0.5 * z + z * z * (4.166664568298827e-2 + z * (-1.388731625493765e-3 + z * 2.443315711809948e-5))
            odd = (k == 1.0) | (k == 3.0)
            cs = jnp.where(odd, s, c)
            sn = jnp.where(odd, c, s)
            cos_v = jnp.where((k == 1.0) | (k == 2.0), -cs, cs).astype(jnp.bfloat16)
            sin_v = jnp.where((k == 2.0) | (k == 3.0), -sn, sn).astype(jnp.bfloat16)
            basis_ref[pl.ds(r0, ROWS), pl.ds(c0, LANES)] = cos_v
            basis_ref[pl.ds(r0, ROWS), pl.ds(nper + c0, LANES)] = sin_v
            cf = cos_v.astype(jnp.float32)
            sf = sin_v.astype(jnp.float32)
            return acc_c + cf * cf, acc_s + sf * sf

        zero = jnp.zeros((ROWS, LANES), jnp.float32)
        acc_c, acc_s = lax.fori_loop(0, obs // ROWS, row_block, (zero, zero), unroll=UNROLL)
        nc_ref[:, pl.ds(c0, LANES)] = jnp.sum(acc_c, axis=0, keepdims=True) + RIDGE
        ns_ref[:, pl.ds(c0, LANES)] = jnp.sum(acc_s, axis=0, keepdims=True) + RIDGE
        return carry

    lax.fori_loop(0, nper // LANES, lane_block, 0)


def basis_and_norms(times, periods):
    plans, obs = times.shape
    nper = periods.shape[0]
    pf = periods.astype(jnp.float32)
    w = (TWO_PI / pf).reshape(1, nper)
    inv = (1.0 / pf).reshape(1, nper)
    pf = pf.reshape(1, nper)
    tf = times.astype(jnp.float32).reshape(plans, obs, 1)
    row = pl.BlockSpec((1, nper), lambda g: (0, 0))
    basis, nc, ns = pl.pallas_call(
        basis_kernel,
        grid=(plans,),
        in_specs=[pl.BlockSpec((None, obs, 1), lambda g: (g, 0, 0)), row, row, row],
        out_specs=[
            pl.BlockSpec((None, obs, 2 * nper), lambda g: (g, 0, 0)),
            pl.BlockSpec((None, 1, nper), lambda g: (g, 0, 0)),
            pl.BlockSpec((None, 1, nper), lambda g: (g, 0, 0)),
        ],
        out_shape=[
            jax.ShapeDtypeStruct((plans, obs, 2 * nper), jnp.bfloat16),
            jax.ShapeDtypeStruct((plans, 1, nper), jnp.float32),
            jax.ShapeDtypeStruct((plans, 1, nper), jnp.float32),
        ],
        cost_estimate=pl.CostEstimate(
            flops=60 * plans * obs * nper, transcendentals=0,
            bytes_accessed=plans * obs * 2 * nper * 2),
    )(tf, pf, w, inv)
    return basis, nc.reshape(plans, nper), ns.reshape(plans, nper)


def gather_kernel(idx_ref, src_ref, *rest):
    out_ref = rest[-2]
    stage_ref = rest[-1]
    block = stage_ref.shape[0]

    def body(b, carry):
        r0 = pl.multiple_of(b * block, block)
        for j in range(block):
            stage_ref[pl.ds(j, 1), :] = src_ref[pl.ds(idx_ref[r0 + j], 1), :]
        out_ref[pl.ds(r0, block), :] = stage_ref[...].astype(out_ref.dtype)
        return carry

    lax.fori_loop(0, out_ref.shape[0] // block, body, 0)


def row_gather(src, idx, out_dtype, *after):
    rows, width = idx.shape[0], src.shape[1]
    return pl.pallas_call(
        gather_kernel,
        in_specs=[pl.BlockSpec(memory_space=pltpu.SMEM), pl.BlockSpec(memory_space=pltpu.VMEM)]
        + [pl.BlockSpec(memory_space=pltpu.VMEM) for _ in after],
        out_specs=pl.BlockSpec(memory_space=pltpu.VMEM),
        out_shape=jax.ShapeDtypeStruct((rows, width), out_dtype),
        scratch_shapes=[pltpu.VMEM((32, width), src.dtype)],
        cost_estimate=pl.CostEstimate(
            flops=0, transcendentals=0, bytes_accessed=2 * rows * width * src.dtype.itemsize),
    )(idx, src, *after)


def with_zero_rows(flat):
    return jnp.concatenate([flat, jnp.zeros((8, flat.shape[1]), flat.dtype)], axis=0)


def a2a_kernel(x_ref, out_ref, held, send_sem, recv_sem):
    n = x_ref.shape[0]
    me = lax.axis_index("tm")
    sky = lax.axis_index("sky")
    barrier = pltpu.get_barrier_semaphore()

    def greet(k, carry):
        peer = lax.rem(me + k, n)
        pl.semaphore_signal(barrier, inc=1, device_id=(peer, sky), device_id_type=pl.DeviceIdType.MESH)
        return carry

    lax.fori_loop(1, n, greet, 0)
    pl.semaphore_wait(barrier, n - 1)

    def copy(k):
        peer = lax.rem(me + k, n)
        return pltpu.make_async_remote_copy(
            src_ref=x_ref.at[peer],
            dst_ref=held.at[me],
            send_sem=send_sem.at[k],
            recv_sem=recv_sem.at[k],
            device_id=(peer, sky),
            device_id_type=pl.DeviceIdType.MESH,
        )

    def start(k, carry):
        copy(k).start()
        return carry

    lax.fori_loop(1, n, start, 0)
    held[pl.ds(me, 1)] = x_ref[pl.ds(me, 1)]

    def finish(k, carry):
        copy(k).wait()
        return carry

    lax.fori_loop(1, n, finish, 0)
    out_ref[...] = held[...].astype(out_ref.dtype)


def tm_all_to_all(x, out_dtype, collective_id):
    n, rows, width = x.shape
    return pl.pallas_call(
        a2a_kernel,
        in_specs=[pl.BlockSpec(memory_space=pltpu.VMEM)],
        out_specs=pl.BlockSpec(memory_space=pltpu.VMEM),
        out_shape=jax.ShapeDtypeStruct((n, rows, width), out_dtype),
        scratch_shapes=[
            pltpu.VMEM((n, rows, width), x.dtype),
            pltpu.SemaphoreType.DMA((n,)),
            pltpu.SemaphoreType.DMA((n,)),
        ],
        compiler_params=pltpu.CompilerParams(collective_id=collective_id, has_side_effects=True),
    )(x)


STREAMS = 2
SUNROLL = 4

def scatter_add_kernel(idx_ref, src_ref, out_ref, acc_ref):
    rows = src_ref.shape[0]
    streams = acc_ref.shape[0]
    acc_ref[...] = jnp.zeros_like(acc_ref)

    def body(step, carry):
        base = step * streams
        for s in range(streams):
            r = base + s
            i = idx_ref[r]
            acc_ref[s, pl.ds(i, 1), :] = acc_ref[s, pl.ds(i, 1), :] + src_ref[pl.ds(r, 1), :]
        return carry

    lax.fori_loop(0, rows // streams, body, 0, unroll=SUNROLL)
    total = acc_ref[0]
    for s in range(1, streams):
        total = total + acc_ref[s]
    out_ref[...] = total[: out_ref.shape[0]]


def scatter_add(src, idx, out_rows):
    rows, width = src.shape
    pad = out_rows + 8
    return pl.pallas_call(
        scatter_add_kernel,
        in_specs=[pl.BlockSpec(memory_space=pltpu.SMEM), pl.BlockSpec(memory_space=pltpu.VMEM)],
        out_specs=pl.BlockSpec(memory_space=pltpu.VMEM),
        out_shape=jax.ShapeDtypeStruct((out_rows, width), jnp.float32),
        scratch_shapes=[pltpu.VMEM((STREAMS, pad, width), jnp.float32)],
        cost_estimate=pl.CostEstimate(flops=rows * width, transcendentals=0, bytes_accessed=(rows + out_rows) * width * 4),
    )(idx, src)


def fit_kernel(basis_ref, obs_ref, inc_ref, ins_ref, model_ref, ev_ref):
    nper = inc_ref.shape[1]
    basis = basis_ref[...]
    obs_t = obs_ref[...].astype(jnp.float32).T.astype(jnp.bfloat16)
    corr = jnp.dot(obs_t, basis, preferred_element_type=jnp.float32)
    cosine = corr[:, :nper]
    sine = corr[:, nper:]
    amp_c = cosine * inc_ref[...]
    amp_s = sine * ins_ref[...]
    logits = BETA * (cosine * amp_c + sine * amp_s)
    highest = jnp.max(logits, axis=1, keepdims=True)
    expo = jnp.exp(logits - highest)
    total = jnp.sum(expo, axis=1, keepdims=True)
    share = expo * (1.0 / total)
    coeff = jnp.concatenate([share * amp_c, share * amp_s], axis=1).astype(jnp.bfloat16)
    model_ref[...] = lax.dot_general(
        basis, coeff, (((1,), (1,)), ((), ())), preferred_element_type=jnp.float32)
    ev_ref[...] = highest + jnp.log(total)


def fit_fused(basis, observed, inv_cos, inv_sin):
    plans, obs, width = basis.shape
    cols = observed.shape[2]
    nper = width // 2
    row = pl.BlockSpec((None, 1, nper), lambda g: (g, 0, 0))
    model, ev = pl.pallas_call(
        fit_kernel,
        grid=(plans,),
        in_specs=[
            pl.BlockSpec((None, obs, width), lambda g: (g, 0, 0)),
            pl.BlockSpec((None, obs, cols), lambda g: (g, 0, 0)),
            row,
            row,
        ],
        out_specs=[
            pl.BlockSpec((None, obs, cols), lambda g: (g, 0, 0)),
            pl.BlockSpec((None, cols, 1), lambda g: (g, 0, 0)),
        ],
        out_shape=[
            jax.ShapeDtypeStruct((plans, obs, cols), jnp.float32),
            jax.ShapeDtypeStruct((plans, cols, 1), jnp.float32),
        ],
        cost_estimate=pl.CostEstimate(
            flops=4 * plans * obs * width * cols, transcendentals=plans * nper * cols,
            bytes_accessed=plans * obs * width * 2),
    )(basis, observed, inv_cos, inv_sin)
    return model, ev.reshape(plans, cols)


def white_kernel(cnt_ref, cur_ref, att_ref, out_ref):
    segs, slots, _ = att_ref.shape
    width = out_ref.shape[1]
    blocks = cur_ref.shape[1] // width
    for s in range(segs):
        cur = cur_ref[pl.ds(s * slots, slots), :]
        slot = lax.broadcasted_iota(jnp.int32, cur.shape, 0)
        masked = jnp.where(slot < cnt_ref[s], cur, 0.0).astype(jnp.bfloat16)
        white = jnp.dot(att_ref[s], masked, preferred_element_type=jnp.float32)
        for b in range(blocks):
            out_ref[pl.ds(b * segs * slots + s * slots, slots), :] = white[:, b * width:(b + 1) * width]
    out_ref[pl.ds(blocks * segs * slots, 8), :] = jnp.zeros((8, width), jnp.float32)


def whiten_rows(counts, current, attitude_all, width):
    segs, slots, _ = attitude_all.shape
    rows = current.shape[0] * current.shape[1] // width
    return pl.pallas_call(
        white_kernel,
        in_specs=[pl.BlockSpec(memory_space=pltpu.SMEM)] + [pl.BlockSpec(memory_space=pltpu.VMEM)] * 2,
        out_specs=pl.BlockSpec(memory_space=pltpu.VMEM),
        out_shape=jax.ShapeDtypeStruct((rows + 8, width), jnp.float32),
        cost_estimate=pl.CostEstimate(
            flops=2 * segs * slots * slots * current.shape[1], transcendentals=0,
            bytes_accessed=current.size * 8 + attitude_all.size * 2),
    )(counts, current, attitude_all)


def scatter_sub_kernel(idx_ref, src_ref, cur_ref, out_ref, acc_ref):
    rows, width = src_ref.shape
    streams = acc_ref.shape[0]
    n = cur_ref.shape[0]
    acc_ref[...] = jnp.zeros_like(acc_ref)

    def body(step, carry):
        base = step * streams
        for s in range(streams):
            r = base + s
            i = idx_ref[r]
            acc_ref[s, pl.ds(i, 1), :] = acc_ref[s, pl.ds(i, 1), :] + src_ref[pl.ds(r, 1), :]
        return carry

    lax.fori_loop(0, rows // streams, body, 0, unroll=SUNROLL)
    for b in range(cur_ref.shape[1] // width):
        total = acc_ref[0, pl.ds(b * n, n), :]
        for s in range(1, streams):
            total = total + acc_ref[s, pl.ds(b * n, n), :]
        out_ref[:, b * width:(b + 1) * width] = cur_ref[:, b * width:(b + 1) * width] - total


def scatter_sub(src, idx, current):
    rows, width = src.shape
    blocks = current.shape[1] // width
    return pl.pallas_call(
        scatter_sub_kernel,
        in_specs=[pl.BlockSpec(memory_space=pltpu.SMEM)] + [pl.BlockSpec(memory_space=pltpu.VMEM)] * 2,
        out_specs=pl.BlockSpec(memory_space=pltpu.VMEM),
        out_shape=jax.ShapeDtypeStruct(current.shape, jnp.float32),
        scratch_shapes=[pltpu.VMEM((STREAMS, blocks * current.shape[0] + 8, width), jnp.float32)],
        cost_estimate=pl.CostEstimate(
            flops=rows * width, transcendentals=0, bytes_accessed=(rows * width + 2 * current.size) * 4),
    )(idx, src, current)

def fit_groups(basis, observed, norm_cos, norm_sin, nper):
    corr = jnp.einsum("fio,fic->foc", basis, observed, preferred_element_type=jnp.float32)
    cosine = corr[:, :nper]
    sine = corr[:, nper:]
    amp_c = cosine / norm_cos[:, :, None]
    amp_s = sine / norm_sin[:, :, None]
    power = cosine * amp_c + sine * amp_s
    logits = BETA * power
    highest = jnp.max(logits, axis=1)
    expo = jnp.exp(logits - highest[:, None, :])
    total = jnp.sum(expo, axis=1)
    share = expo / total[:, None, :]
    coeff = jnp.concatenate([share * amp_c, share * amp_s], axis=1).astype(jnp.bfloat16)
    model = jnp.einsum("fio,foc->fic", basis, coeff, preferred_element_type=jnp.float32)
    return (model, highest + jnp.log(total))


def on_device(residuals, seg_counts, attitude, sched_seg, sched_slot, periods):
    tm_count = lax.axis_size("tm")
    sched_dev, obs = sched_seg.shape
    seg_dev, slots, width = residuals.shape
    nper = periods.shape[0]
    column_blocks = width // SRC_GROUP
    capacity = 2 * sched_dev * obs // tm_count
    requests = sched_dev * obs
    seg_flat = sched_seg.reshape(-1)
    slot_flat = sched_slot.reshape(-1)
    block_of = jnp.repeat(jnp.arange(sched_dev, dtype=jnp.int32) % column_blocks, obs)
    target = seg_flat // seg_dev
    local_row = block_of * (seg_dev * slots) + seg_flat % seg_dev * slots + slot_flat
    onehot = (target[:, None] == jnp.arange(tm_count, dtype=jnp.int32)[None, :]).astype(jnp.int32)
    ones = onehot.astype(jnp.bfloat16).reshape(requests // 128, 128, tm_count)
    tril = (jnp.arange(128)[:, None] >= jnp.arange(128)[None, :]).astype(jnp.bfloat16)
    within = jnp.einsum("ij,bjc->bic", tril, ones, preferred_element_type=jnp.float32)
    totals = within[:, -1, :]
    before = jnp.cumsum(totals, axis=0) - totals
    counts = (within + before[:, None, :]).reshape(requests, tm_count)
    position = jnp.sum(counts * onehot.astype(jnp.float32), axis=1).astype(jnp.int32) - 1
    empty_row = seg_dev * slots * column_blocks
    slot_of = target * capacity + position
    pair = (
        jnp.broadcast_to(jnp.array([empty_row, 0], jnp.int32), (tm_count * capacity, 2))
        .at[slot_of]
        .set(jnp.stack([local_row, jnp.arange(requests, dtype=jnp.int32)], axis=1))
    )
    wanted = pair[:, 0].reshape(tm_count, capacity)
    inverse = pair[:, 1]
    asked = lax.all_to_all(wanted, "tm", split_axis=0, concat_axis=0, tiled=True).reshape(-1)
    basis, norm_cos, norm_sin = basis_and_norms(sched_seg * slots + sched_slot, periods)
    valid = jnp.arange(slots, dtype=jnp.int32)[None, :] < seg_counts[:, None]
    inv_cos = (1.0 / norm_cos).reshape(sched_dev, 1, nper)
    inv_sin = (1.0 / norm_sin).reshape(sched_dev, 1, nper)
    current = residuals.astype(jnp.float32).reshape(seg_dev * slots, width)
    evidence = jnp.zeros((sched_dev, SRC_GROUP), jnp.float32)
    attitude_all = lax.all_gather(attitude, "sky", axis=1, tiled=True)
    for iteration in range(ITERS):
        white = whiten_rows(seg_counts, current, attitude_all, SRC_GROUP)
        picked = row_gather(white, asked, jnp.bfloat16, norm_cos)
        outbound = picked.reshape(tm_count, capacity, SRC_GROUP)
        arrived = lax.all_to_all(outbound, "tm", split_axis=0, concat_axis=0, tiled=True)
        arrived = arrived.astype(jnp.float32)
        observed = row_gather(arrived.reshape(-1, SRC_GROUP), slot_of, jnp.bfloat16)
        observed = observed.reshape(sched_dev, obs, SRC_GROUP)
        model, evidence = fit_fused(basis, observed, inv_cos, inv_sin)
        outgoing = row_gather(model.reshape(requests, SRC_GROUP), inverse, jnp.bfloat16)
        returned = tm_all_to_all(
            outgoing.reshape(tm_count, capacity, SRC_GROUP),
            jnp.float32, 2 + 2 * iteration)
        current = scatter_sub(returned.reshape(-1, SRC_GROUP), asked, current)
    current = current.reshape(seg_dev, slots, width)
    return (current, evidence)


def solution(mesh):
    in_specs = (
        P("tm", None, "sky"),
        P("tm"),
        P("tm", "sky", None),
        P(("tm", "sky"), None),
        P(("tm", "sky"), None),
        P(),
    )
    out_specs = (P("tm", None, "sky"), P(("tm", "sky"), None))
    return jax.shard_map(
        on_device, mesh=mesh, in_specs=in_specs, out_specs=out_specs, check_vma=False
    )
```

```python
import jax
import jax.numpy as jnp
from jax import lax
from jax.experimental import pallas as pl
from jax.experimental.pallas import tpu as pltpu
from jax.sharding import PartitionSpec as P

SRC_GROUP = 128
ITERS = 2


TWO_PI = 6.283185307179586
BETA = 2.0
RIDGE = 1.0


PIO2_1 = 1.5703125
PIO2_2 = 4.837512969970703125e-4
PIO2_3 = 7.549789954891e-8
ROWS = 16
LANES = 512
UNROLL = 2


def basis_kernel(t_ref, p_ref, w_ref, inv_ref, basis_ref, nc_ref, ns_ref):
    obs = t_ref.shape[0]
    nper = p_ref.shape[1]

    def lane_block(j, carry):
        c0 = pl.multiple_of(j * LANES, LANES)
        pf = p_ref[:, pl.ds(c0, LANES)]
        w = w_ref[:, pl.ds(c0, LANES)]
        inv = inv_ref[:, pl.ds(c0, LANES)]

        def row_block(i, acc):
            acc_c, acc_s = acc
            r0 = pl.multiple_of(i * ROWS, ROWS)
            tf = jnp.broadcast_to(t_ref[pl.ds(r0, ROWS), :], (ROWS, LANES))
            q = jnp.floor(tf * inv)
            r = tf - q * pf
            r = jnp.where(r < 0.0, r + pf, r)
            r = jnp.where(r >= pf, r - pf, r)
            phase = r * w
            k = jnp.floor(phase * 0.6366197723675814 + 0.5)
            y = ((phase - k * PIO2_1) - k * PIO2_2) - k * PIO2_3
            z = y * y
            s = y + y * z * (-1.6666654611e-1 + z * (8.3321608736e-3 + z * -1.9515295891e-4))
            c = 1.0 - 0.5 * z + z * z * (4.166664568298827e-2 + z * (-1.388731625493765e-3 + z * 2.443315711809948e-5))
            odd = (k == 1.0) | (k == 3.0)
            cs = jnp.where(odd, s, c)
            sn = jnp.where(odd, c, s)
            cos_v = jnp.where((k == 1.0) | (k == 2.0), -cs, cs).astype(jnp.bfloat16)
            sin_v = jnp.where((k == 2.0) | (k == 3.0), -sn, sn).astype(jnp.bfloat16)
            basis_ref[pl.ds(r0, ROWS), pl.ds(c0, LANES)] = cos_v
            basis_ref[pl.ds(r0, ROWS), pl.ds(nper + c0, LANES)] = sin_v
            cf = cos_v.astype(jnp.float32)
            sf = sin_v.astype(jnp.float32)
            return acc_c + cf * cf, acc_s + sf * sf

        zero = jnp.zeros((ROWS, LANES), jnp.float32)
        acc_c, acc_s = lax.fori_loop(0, obs // ROWS, row_block, (zero, zero), unroll=UNROLL)
        nc_ref[:, pl.ds(c0, LANES)] = jnp.sum(acc_c, axis=0, keepdims=True) + RIDGE
        ns_ref[:, pl.ds(c0, LANES)] = jnp.sum(acc_s, axis=0, keepdims=True) + RIDGE
        return carry

    lax.fori_loop(0, nper // LANES, lane_block, 0)


def basis_and_norms(times, periods):
    plans, obs = times.shape
    nper = periods.shape[0]
    pf = periods.astype(jnp.float32)
    w = (TWO_PI / pf).reshape(1, nper)
    inv = (1.0 / pf).reshape(1, nper)
    pf = pf.reshape(1, nper)
    tf = times.astype(jnp.float32).reshape(plans, obs, 1)
    row = pl.BlockSpec((1, nper), lambda g: (0, 0))
    basis, nc, ns = pl.pallas_call(
        basis_kernel,
        grid=(plans,),
        in_specs=[pl.BlockSpec((None, obs, 1), lambda g: (g, 0, 0)), row, row, row],
        out_specs=[
            pl.BlockSpec((None, obs, 2 * nper), lambda g: (g, 0, 0)),
            pl.BlockSpec((None, 1, nper), lambda g: (g, 0, 0)),
            pl.BlockSpec((None, 1, nper), lambda g: (g, 0, 0)),
        ],
        out_shape=[
            jax.ShapeDtypeStruct((plans, obs, 2 * nper), jnp.bfloat16),
            jax.ShapeDtypeStruct((plans, 1, nper), jnp.float32),
            jax.ShapeDtypeStruct((plans, 1, nper), jnp.float32),
        ],
        cost_estimate=pl.CostEstimate(
            flops=60 * plans * obs * nper, transcendentals=0,
            bytes_accessed=plans * obs * 2 * nper * 2),
    )(tf, pf, w, inv)
    return basis, nc.reshape(plans, nper), ns.reshape(plans, nper)


def gather_kernel(idx_ref, src_ref, *rest):
    out_ref = rest[-2]
    stage_ref = rest[-1]
    block = stage_ref.shape[0]

    def body(b, carry):
        r0 = pl.multiple_of(b * block, block)
        for j in range(block):
            stage_ref[pl.ds(j, 1), :] = src_ref[pl.ds(idx_ref[r0 + j], 1), :]
        out_ref[pl.ds(r0, block), :] = stage_ref[...].astype(out_ref.dtype)
        return carry

    lax.fori_loop(0, out_ref.shape[0] // block, body, 0)


def row_gather(src, idx, out_dtype, *after):
    rows, width = idx.shape[0], src.shape[1]
    return pl.pallas_call(
        gather_kernel,
        in_specs=[pl.BlockSpec(memory_space=pltpu.SMEM), pl.BlockSpec(memory_space=pltpu.VMEM)]
        + [pl.BlockSpec(memory_space=pltpu.VMEM) for _ in after],
        out_specs=pl.BlockSpec(memory_space=pltpu.VMEM),
        out_shape=jax.ShapeDtypeStruct((rows, width), out_dtype),
        scratch_shapes=[pltpu.VMEM((32, width), src.dtype)],
        cost_estimate=pl.CostEstimate(
            flops=0, transcendentals=0, bytes_accessed=2 * rows * width * src.dtype.itemsize),
    )(idx, src, *after)


def with_zero_rows(flat):
    return jnp.concatenate([flat, jnp.zeros((8, flat.shape[1]), flat.dtype)], axis=0)


def a2a_kernel(x_ref, out_ref, held, send_sem, recv_sem):
    n = x_ref.shape[0]
    me = lax.axis_index("tm")
    sky = lax.axis_index("sky")
    barrier = pltpu.get_barrier_semaphore()

    def greet(k, carry):
        peer = lax.rem(me + k, n)
        pl.semaphore_signal(barrier, inc=1, device_id=(peer, sky), device_id_type=pl.DeviceIdType.MESH)
        return carry

    lax.fori_loop(1, n, greet, 0)
    pl.semaphore_wait(barrier, n - 1)

    def copy(k):
        peer = lax.rem(me + k, n)
        return pltpu.make_async_remote_copy(
            src_ref=x_ref.at[peer],
            dst_ref=held.at[me],
            send_sem=send_sem.at[k],
            recv_sem=recv_sem.at[k],
            device_id=(peer, sky),
            device_id_type=pl.DeviceIdType.MESH,
        )

    def start(k, carry):
        copy(k).start()
        return carry

    lax.fori_loop(1, n, start, 0)
    held[pl.ds(me, 1)] = x_ref[pl.ds(me, 1)]

    def finish(k, carry):
        copy(k).wait()
        return carry

    lax.fori_loop(1, n, finish, 0)
    out_ref[...] = held[...].astype(out_ref.dtype)


def tm_all_to_all(x, out_dtype, collective_id):
    n, rows, width = x.shape
    return pl.pallas_call(
        a2a_kernel,
        in_specs=[pl.BlockSpec(memory_space=pltpu.VMEM)],
        out_specs=pl.BlockSpec(memory_space=pltpu.VMEM),
        out_shape=jax.ShapeDtypeStruct((n, rows, width), out_dtype),
        scratch_shapes=[
            pltpu.VMEM((n, rows, width), x.dtype),
            pltpu.SemaphoreType.DMA((n,)),
            pltpu.SemaphoreType.DMA((n,)),
        ],
        compiler_params=pltpu.CompilerParams(collective_id=collective_id, has_side_effects=True),
    )(x)


STREAMS = 4
SUNROLL = 2

def scatter_add_kernel(idx_ref, src_ref, out_ref, acc_ref):
    rows = src_ref.shape[0]
    streams = acc_ref.shape[0]
    acc_ref[...] = jnp.zeros_like(acc_ref)

    def body(step, carry):
        base = step * streams
        for s in range(streams):
            r = base + s
            i = idx_ref[r]
            acc_ref[s, pl.ds(i, 1), :] = acc_ref[s, pl.ds(i, 1), :] + src_ref[pl.ds(r, 1), :]
        return carry

    lax.fori_loop(0, rows // streams, body, 0, unroll=SUNROLL)
    total = acc_ref[0]
    for s in range(1, streams):
        total = total + acc_ref[s]
    out_ref[...] = total[: out_ref.shape[0]]


def scatter_add(src, idx, out_rows):
    rows, width = src.shape
    pad = out_rows + 8
    return pl.pallas_call(
        scatter_add_kernel,
        in_specs=[pl.BlockSpec(memory_space=pltpu.SMEM), pl.BlockSpec(memory_space=pltpu.VMEM)],
        out_specs=pl.BlockSpec(memory_space=pltpu.VMEM),
        out_shape=jax.ShapeDtypeStruct((out_rows, width), jnp.float32),
        scratch_shapes=[pltpu.VMEM((STREAMS, pad, width), jnp.float32)],
        cost_estimate=pl.CostEstimate(flops=rows * width, transcendentals=0, bytes_accessed=(rows + out_rows) * width * 4),
    )(idx, src)


def fit_kernel(slot_ref, basis_ref, arrived_ref, inc_ref, ins_ref, model_ref, ev_ref, stage_ref):
    nper = inc_ref.shape[1]
    obs = stage_ref.shape[0]
    base = pl.program_id(0) * obs

    def pick(b, carry):
        r0 = pl.multiple_of(b * 32, 32)
        for j in range(32):
            stage_ref[pl.ds(r0 + j, 1), :] = arrived_ref[pl.ds(slot_ref[base + r0 + j], 1), :]
        return carry

    lax.fori_loop(0, obs // 32, pick, 0)
    basis = basis_ref[...]
    obs_t = stage_ref[...].T.astype(jnp.bfloat16)
    corr = jnp.dot(obs_t, basis, preferred_element_type=jnp.float32)
    cosine = corr[:, :nper]
    sine = corr[:, nper:]
    amp_c = cosine * inc_ref[...]
    amp_s = sine * ins_ref[...]
    logits = BETA * (cosine * amp_c + sine * amp_s)
    highest = jnp.max(logits, axis=1, keepdims=True)
    expo = jnp.exp(logits - highest)
    total = jnp.sum(expo, axis=1, keepdims=True)
    share = expo * (1.0 / total)
    coeff = jnp.concatenate([share * amp_c, share * amp_s], axis=1).astype(jnp.bfloat16)
    model_ref[...] = lax.dot_general(
        basis, coeff, (((1,), (1,)), ((), ())), preferred_element_type=jnp.float32)
    ev_ref[...] = highest + jnp.log(total)


def fit_fused(basis, arrived, slot_of, inv_cos, inv_sin):
    plans, obs, width = basis.shape
    cols = arrived.shape[1]
    nper = width // 2
    row = pl.BlockSpec((None, 1, nper), lambda g, s: (g, 0, 0))
    model, ev = pl.pallas_call(
        fit_kernel,
        grid_spec=pltpu.PrefetchScalarGridSpec(
            num_scalar_prefetch=1,
            grid=(plans,),
            in_specs=[
                pl.BlockSpec((None, obs, width), lambda g, s: (g, 0, 0)),
                pl.BlockSpec(arrived.shape, lambda g, s: (0, 0)),
                row,
                row,
            ],
            out_specs=[
                pl.BlockSpec((None, obs, cols), lambda g, s: (g, 0, 0)),
                pl.BlockSpec((None, cols, 1), lambda g, s: (g, 0, 0)),
            ],
            scratch_shapes=[pltpu.VMEM((obs, cols), jnp.float32)],
        ),
        out_shape=[
            jax.ShapeDtypeStruct((plans, obs, cols), jnp.float32),
            jax.ShapeDtypeStruct((plans, cols, 1), jnp.float32),
        ],
        cost_estimate=pl.CostEstimate(
            flops=4 * plans * obs * width * cols, transcendentals=plans * nper * cols,
            bytes_accessed=plans * obs * width * 2),
    )(slot_of, basis, arrived, inv_cos, inv_sin)
    return model, ev.reshape(plans, cols)


def white_kernel(cnt_ref, cur_ref, att_ref, out_ref):
    segs, slots, _ = att_ref.shape
    width = out_ref.shape[1]
    blocks = cur_ref.shape[1] // width
    for s in range(segs):
        cur = cur_ref[pl.ds(s * slots, slots), :]
        slot = lax.broadcasted_iota(jnp.int32, cur.shape, 0)
        masked = jnp.where(slot < cnt_ref[s], cur, 0.0).astype(jnp.bfloat16)
        white = jnp.dot(att_ref[s], masked, preferred_element_type=jnp.float32)
        for b in range(blocks):
            out_ref[pl.ds(b * segs * slots + s * slots, slots), :] = white[:, b * width:(b + 1) * width]
    out_ref[pl.ds(blocks * segs * slots, 8), :] = jnp.zeros((8, width), jnp.float32)


def whiten_rows(counts, current, attitude_all, width):
    segs, slots, _ = attitude_all.shape
    rows = current.shape[0] * current.shape[1] // width
    return pl.pallas_call(
        white_kernel,
        in_specs=[pl.BlockSpec(memory_space=pltpu.SMEM)] + [pl.BlockSpec(memory_space=pltpu.VMEM)] * 2,
        out_specs=pl.BlockSpec(memory_space=pltpu.VMEM),
        out_shape=jax.ShapeDtypeStruct((rows + 8, width), jnp.float32),
        cost_estimate=pl.CostEstimate(
            flops=2 * segs * slots * slots * current.shape[1], transcendentals=0,
            bytes_accessed=current.size * 8 + attitude_all.size * 2),
    )(counts, current, attitude_all)


def scatter_sub_kernel(idx_ref, src_ref, cur_ref, out_ref, acc_ref):
    rows, width = src_ref.shape
    streams = acc_ref.shape[0]
    n = cur_ref.shape[0]
    acc_ref[...] = jnp.zeros_like(acc_ref)

    def body(step, carry):
        base = step * streams
        for s in range(streams):
            r = base + s
            i = idx_ref[r]
            acc_ref[s, pl.ds(i, 1), :] = acc_ref[s, pl.ds(i, 1), :] + src_ref[pl.ds(r, 1), :]
        return carry

    lax.fori_loop(0, rows // streams, body, 0, unroll=SUNROLL)
    for b in range(cur_ref.shape[1] // width):
        total = acc_ref[0, pl.ds(b * n, n), :]
        for s in range(1, streams):
            total = total + acc_ref[s, pl.ds(b * n, n), :]
        out_ref[:, b * width:(b + 1) * width] = cur_ref[:, b * width:(b + 1) * width] - total


def scatter_sub(src, idx, current):
    rows, width = src.shape
    blocks = current.shape[1] // width
    return pl.pallas_call(
        scatter_sub_kernel,
        in_specs=[pl.BlockSpec(memory_space=pltpu.SMEM)] + [pl.BlockSpec(memory_space=pltpu.VMEM)] * 2,
        out_specs=pl.BlockSpec(memory_space=pltpu.VMEM),
        out_shape=jax.ShapeDtypeStruct(current.shape, jnp.float32),
        scratch_shapes=[pltpu.VMEM((STREAMS, blocks * current.shape[0] + 8, width), jnp.float32)],
        cost_estimate=pl.CostEstimate(
            flops=rows * width, transcendentals=0, bytes_accessed=(rows * width + 2 * current.size) * 4),
    )(idx, src, current)

def fit_groups(basis, observed, norm_cos, norm_sin, nper):
    corr = jnp.einsum("fio,fic->foc", basis, observed, preferred_element_type=jnp.float32)
    cosine = corr[:, :nper]
    sine = corr[:, nper:]
    amp_c = cosine / norm_cos[:, :, None]
    amp_s = sine / norm_sin[:, :, None]
    power = cosine * amp_c + sine * amp_s
    logits = BETA * power
    highest = jnp.max(logits, axis=1)
    expo = jnp.exp(logits - highest[:, None, :])
    total = jnp.sum(expo, axis=1)
    share = expo / total[:, None, :]
    coeff = jnp.concatenate([share * amp_c, share * amp_s], axis=1).astype(jnp.bfloat16)
    model = jnp.einsum("fio,foc->fic", basis, coeff, preferred_element_type=jnp.float32)
    return (model, highest + jnp.log(total))


def on_device(residuals, seg_counts, attitude, sched_seg, sched_slot, periods):
    tm_count = lax.axis_size("tm")
    sched_dev, obs = sched_seg.shape
    seg_dev, slots, width = residuals.shape
    nper = periods.shape[0]
    column_blocks = width // SRC_GROUP
    capacity = 2 * sched_dev * obs // tm_count
    requests = sched_dev * obs
    seg_flat = sched_seg.reshape(-1)
    slot_flat = sched_slot.reshape(-1)
    block_of = jnp.repeat(jnp.arange(sched_dev, dtype=jnp.int32) % column_blocks, obs)
    target = seg_flat // seg_dev
    local_row = block_of * (seg_dev * slots) + seg_flat % seg_dev * slots + slot_flat
    onehot = (target[:, None] == jnp.arange(tm_count, dtype=jnp.int32)[None, :]).astype(jnp.int32)
    ones = onehot.astype(jnp.bfloat16).reshape(requests // 128, 128, tm_count)
    tril = (jnp.arange(128)[:, None] >= jnp.arange(128)[None, :]).astype(jnp.bfloat16)
    within = jnp.einsum("ij,bjc->bic", tril, ones, preferred_element_type=jnp.float32)
    totals = within[:, -1, :]
    before = jnp.cumsum(totals, axis=0) - totals
    counts = (within + before[:, None, :]).reshape(requests, tm_count)
    position = jnp.sum(counts * onehot.astype(jnp.float32), axis=1).astype(jnp.int32) - 1
    empty_row = seg_dev * slots * column_blocks
    slot_of = target * capacity + position
    pair = (
        jnp.broadcast_to(jnp.array([empty_row, 0], jnp.int32), (tm_count * capacity, 2))
        .at[slot_of]
        .set(jnp.stack([local_row, jnp.arange(requests, dtype=jnp.int32)], axis=1))
    )
    wanted = pair[:, 0].reshape(tm_count, capacity)
    inverse = pair[:, 1]
    asked = lax.all_to_all(wanted, "tm", split_axis=0, concat_axis=0, tiled=True).reshape(-1)
    basis, norm_cos, norm_sin = basis_and_norms(sched_seg * slots + sched_slot, periods)
    valid = jnp.arange(slots, dtype=jnp.int32)[None, :] < seg_counts[:, None]
    inv_cos = (1.0 / norm_cos).reshape(sched_dev, 1, nper)
    inv_sin = (1.0 / norm_sin).reshape(sched_dev, 1, nper)
    current = residuals.astype(jnp.float32).reshape(seg_dev * slots, width)
    evidence = jnp.zeros((sched_dev, SRC_GROUP), jnp.float32)
    attitude_all = lax.all_gather(attitude, "sky", axis=1, tiled=True)
    for iteration in range(ITERS):
        white = whiten_rows(seg_counts, current, attitude_all, SRC_GROUP)
        picked = row_gather(white, asked, jnp.bfloat16, norm_cos)
        outbound = picked.reshape(tm_count, capacity, SRC_GROUP)
        if iteration == 0:
            arrived = tm_all_to_all(outbound, jnp.float32, 1)
        else:
            arrived = lax.all_to_all(outbound, "tm", split_axis=0, concat_axis=0, tiled=True)
            arrived = arrived.astype(jnp.float32)
        model, evidence = fit_fused(
            basis, arrived.reshape(-1, SRC_GROUP), slot_of, inv_cos, inv_sin)
        outgoing = row_gather(model.reshape(requests, SRC_GROUP), inverse, jnp.bfloat16)
        returned = tm_all_to_all(
            outgoing.reshape(tm_count, capacity, SRC_GROUP),
            jnp.float32, 2 + 2 * iteration)
        current = scatter_sub(returned.reshape(-1, SRC_GROUP), asked, current)
    current = current.reshape(seg_dev, slots, width)
    return (current, evidence)


def solution(mesh):
    in_specs = (
        P("tm", None, "sky"),
        P("tm"),
        P("tm", "sky", None),
        P(("tm", "sky"), None),
        P(("tm", "sky"), None),
        P(),
    )
    out_specs = (P("tm", None, "sky"), P(("tm", "sky"), None))
    return jax.shard_map(
        on_device, mesh=mesh, in_specs=in_specs, out_specs=out_specs, check_vma=False
    )
```

```python
import jax
import jax.numpy as jnp
from jax import lax
from jax.experimental import pallas as pl
from jax.experimental.pallas import tpu as pltpu
from jax.sharding import PartitionSpec as P

SRC_GROUP = 128
ITERS = 2


TWO_PI = 6.283185307179586
BETA = 2.0
RIDGE = 1.0


PIO2_1 = 1.5703125
PIO2_2 = 4.837512969970703125e-4
PIO2_3 = 7.549789954891e-8
ROWS = 16
LANES = 512
UNROLL = 2


def basis_kernel(t_ref, p_ref, w_ref, inv_ref, basis_ref, nc_ref, ns_ref):
    obs = t_ref.shape[0]
    nper = p_ref.shape[1]

    def lane_block(j, carry):
        c0 = pl.multiple_of(j * LANES, LANES)
        pf = p_ref[:, pl.ds(c0, LANES)]
        w = w_ref[:, pl.ds(c0, LANES)]
        inv = inv_ref[:, pl.ds(c0, LANES)]

        def row_block(i, acc):
            acc_c, acc_s = acc
            r0 = pl.multiple_of(i * ROWS, ROWS)
            tf = jnp.broadcast_to(t_ref[pl.ds(r0, ROWS), :], (ROWS, LANES))
            q = jnp.floor(tf * inv)
            r = tf - q * pf
            r = jnp.where(r < 0.0, r + pf, r)
            r = jnp.where(r >= pf, r - pf, r)
            phase = r * w
            k = jnp.floor(phase * 0.6366197723675814 + 0.5)
            y = ((phase - k * PIO2_1) - k * PIO2_2) - k * PIO2_3
            z = y * y
            s = y + y * z * (-1.6666654611e-1 + z * (8.3321608736e-3 + z * -1.9515295891e-4))
            c = 1.0 - 0.5 * z + z * z * (4.166664568298827e-2 + z * (-1.388731625493765e-3 + z * 2.443315711809948e-5))
            odd = (k == 1.0) | (k == 3.0)
            cs = jnp.where(odd, s, c)
            sn = jnp.where(odd, c, s)
            cos_v = jnp.where((k == 1.0) | (k == 2.0), -cs, cs).astype(jnp.bfloat16)
            sin_v = jnp.where((k == 2.0) | (k == 3.0), -sn, sn).astype(jnp.bfloat16)
            basis_ref[pl.ds(r0, ROWS), pl.ds(c0, LANES)] = cos_v
            basis_ref[pl.ds(r0, ROWS), pl.ds(nper + c0, LANES)] = sin_v
            cf = cos_v.astype(jnp.float32)
            sf = sin_v.astype(jnp.float32)
            return acc_c + cf * cf, acc_s + sf * sf

        zero = jnp.zeros((ROWS, LANES), jnp.float32)
        acc_c, acc_s = lax.fori_loop(0, obs // ROWS, row_block, (zero, zero), unroll=UNROLL)
        nc_ref[:, pl.ds(c0, LANES)] = jnp.sum(acc_c, axis=0, keepdims=True) + RIDGE
        ns_ref[:, pl.ds(c0, LANES)] = jnp.sum(acc_s, axis=0, keepdims=True) + RIDGE
        return carry

    lax.fori_loop(0, nper // LANES, lane_block, 0)


def basis_and_norms(times, periods):
    plans, obs = times.shape
    nper = periods.shape[0]
    pf = periods.astype(jnp.float32)
    w = (TWO_PI / pf).reshape(1, nper)
    inv = (1.0 / pf).reshape(1, nper)
    pf = pf.reshape(1, nper)
    tf = times.astype(jnp.float32).reshape(plans, obs, 1)
    row = pl.BlockSpec((1, nper), lambda g: (0, 0))
    basis, nc, ns = pl.pallas_call(
        basis_kernel,
        grid=(plans,),
        in_specs=[pl.BlockSpec((None, obs, 1), lambda g: (g, 0, 0)), row, row, row],
        out_specs=[
            pl.BlockSpec((None, obs, 2 * nper), lambda g: (g, 0, 0)),
            pl.BlockSpec((None, 1, nper), lambda g: (g, 0, 0)),
            pl.BlockSpec((None, 1, nper), lambda g: (g, 0, 0)),
        ],
        out_shape=[
            jax.ShapeDtypeStruct((plans, obs, 2 * nper), jnp.bfloat16),
            jax.ShapeDtypeStruct((plans, 1, nper), jnp.float32),
            jax.ShapeDtypeStruct((plans, 1, nper), jnp.float32),
        ],
        cost_estimate=pl.CostEstimate(
            flops=60 * plans * obs * nper, transcendentals=0,
            bytes_accessed=plans * obs * 2 * nper * 2),
    )(tf, pf, w, inv)
    return basis, nc.reshape(plans, nper), ns.reshape(plans, nper)


def gather_kernel(idx_ref, src_ref, *rest):
    out_ref = rest[-2]
    stage_ref = rest[-1]
    block = stage_ref.shape[0]

    def body(b, carry):
        r0 = pl.multiple_of(b * block, block)
        for j in range(block):
            stage_ref[pl.ds(j, 1), :] = src_ref[pl.ds(idx_ref[r0 + j], 1), :]
        out_ref[pl.ds(r0, block), :] = stage_ref[...].astype(out_ref.dtype)
        return carry

    lax.fori_loop(0, out_ref.shape[0] // block, body, 0)


def row_gather(src, idx, out_dtype, *after):
    rows, width = idx.shape[0], src.shape[1]
    return pl.pallas_call(
        gather_kernel,
        in_specs=[pl.BlockSpec(memory_space=pltpu.SMEM), pl.BlockSpec(memory_space=pltpu.VMEM)]
        + [pl.BlockSpec(memory_space=pltpu.VMEM) for _ in after],
        out_specs=pl.BlockSpec(memory_space=pltpu.VMEM),
        out_shape=jax.ShapeDtypeStruct((rows, width), out_dtype),
        scratch_shapes=[pltpu.VMEM((32, width), src.dtype)],
        cost_estimate=pl.CostEstimate(
            flops=0, transcendentals=0, bytes_accessed=2 * rows * width * src.dtype.itemsize),
    )(idx, src, *after)


def with_zero_rows(flat):
    return jnp.concatenate([flat, jnp.zeros((8, flat.shape[1]), flat.dtype)], axis=0)


def a2a_kernel(x_ref, out_ref, held, send_sem, recv_sem):
    n = x_ref.shape[0]
    me = lax.axis_index("tm")
    sky = lax.axis_index("sky")
    barrier = pltpu.get_barrier_semaphore()

    def greet(k, carry):
        peer = lax.rem(me + k, n)
        pl.semaphore_signal(barrier, inc=1, device_id=(peer, sky), device_id_type=pl.DeviceIdType.MESH)
        return carry

    lax.fori_loop(1, n, greet, 0)
    pl.semaphore_wait(barrier, n - 1)

    def copy(k):
        peer = lax.rem(me + k, n)
        return pltpu.make_async_remote_copy(
            src_ref=x_ref.at[peer],
            dst_ref=held.at[me],
            send_sem=send_sem.at[k],
            recv_sem=recv_sem.at[k],
            device_id=(peer, sky),
            device_id_type=pl.DeviceIdType.MESH,
        )

    def start(j, carry):
        odd = j % 2
        copy((1 - odd) * (j // 2 + 1) + odd * (n - 1 - j // 2)).start()
        return carry

    lax.fori_loop(0, n - 1, start, 0)
    held[pl.ds(me, 1)] = x_ref[pl.ds(me, 1)]

    def finish(k, carry):
        copy(k).wait()
        return carry

    lax.fori_loop(1, n, finish, 0)
    out_ref[...] = held[...].astype(out_ref.dtype)


def tm_all_to_all(x, out_dtype, collective_id):
    n, rows, width = x.shape
    return pl.pallas_call(
        a2a_kernel,
        in_specs=[pl.BlockSpec(memory_space=pltpu.VMEM)],
        out_specs=pl.BlockSpec(memory_space=pltpu.VMEM),
        out_shape=jax.ShapeDtypeStruct((n, rows, width), out_dtype),
        scratch_shapes=[
            pltpu.VMEM((n, rows, width), x.dtype),
            pltpu.SemaphoreType.DMA((n,)),
            pltpu.SemaphoreType.DMA((n,)),
        ],
        compiler_params=pltpu.CompilerParams(collective_id=collective_id, has_side_effects=True),
    )(x)


STREAMS = 4
SUNROLL = 2

def scatter_add_kernel(idx_ref, src_ref, out_ref, acc_ref):
    rows = src_ref.shape[0]
    streams = acc_ref.shape[0]
    acc_ref[...] = jnp.zeros_like(acc_ref)

    def body(step, carry):
        base = step * streams
        for s in range(streams):
            r = base + s
            i = idx_ref[r]
            acc_ref[s, pl.ds(i, 1), :] = acc_ref[s, pl.ds(i, 1), :] + src_ref[pl.ds(r, 1), :]
        return carry

    lax.fori_loop(0, rows // streams, body, 0, unroll=SUNROLL)
    total = acc_ref[0]
    for s in range(1, streams):
        total = total + acc_ref[s]
    out_ref[...] = total[: out_ref.shape[0]]


def scatter_add(src, idx, out_rows):
    rows, width = src.shape
    pad = out_rows + 8
    return pl.pallas_call(
        scatter_add_kernel,
        in_specs=[pl.BlockSpec(memory_space=pltpu.SMEM), pl.BlockSpec(memory_space=pltpu.VMEM)],
        out_specs=pl.BlockSpec(memory_space=pltpu.VMEM),
        out_shape=jax.ShapeDtypeStruct((out_rows, width), jnp.float32),
        scratch_shapes=[pltpu.VMEM((STREAMS, pad, width), jnp.float32)],
        cost_estimate=pl.CostEstimate(flops=rows * width, transcendentals=0, bytes_accessed=(rows + out_rows) * width * 4),
    )(idx, src)


def fit_kernel(slot_ref, basis_ref, arrived_ref, inc_ref, ins_ref, model_ref, ev_ref, stage_ref):
    nper = inc_ref.shape[1]
    obs = stage_ref.shape[0]
    base = pl.program_id(0) * obs

    def pick(b, carry):
        r0 = pl.multiple_of(b * 32, 32)
        for j in range(32):
            stage_ref[pl.ds(r0 + j, 1), :] = arrived_ref[pl.ds(slot_ref[base + r0 + j], 1), :]
        return carry

    lax.fori_loop(0, obs // 32, pick, 0)
    basis = basis_ref[...]
    obs_t = stage_ref[...].T.astype(jnp.bfloat16)
    corr = jnp.dot(obs_t, basis, preferred_element_type=jnp.float32)
    cosine = corr[:, :nper]
    sine = corr[:, nper:]
    amp_c = cosine * inc_ref[...]
    amp_s = sine * ins_ref[...]
    logits = BETA * (cosine * amp_c + sine * amp_s)
    highest = jnp.max(logits, axis=1, keepdims=True)
    expo = jnp.exp(logits - highest)
    total = jnp.sum(expo, axis=1, keepdims=True)
    share = expo * (1.0 / total)
    coeff = jnp.concatenate([share * amp_c, share * amp_s], axis=1).astype(jnp.bfloat16)
    model_ref[...] = lax.dot_general(
        basis, coeff, (((1,), (1,)), ((), ())), preferred_element_type=jnp.float32)
    ev_ref[...] = highest + jnp.log(total)


def fit_fused(basis, arrived, slot_of, inv_cos, inv_sin):
    plans, obs, width = basis.shape
    cols = arrived.shape[1]
    nper = width // 2
    row = pl.BlockSpec((None, 1, nper), lambda g, s: (g, 0, 0))
    model, ev = pl.pallas_call(
        fit_kernel,
        grid_spec=pltpu.PrefetchScalarGridSpec(
            num_scalar_prefetch=1,
            grid=(plans,),
            in_specs=[
                pl.BlockSpec((None, obs, width), lambda g, s: (g, 0, 0)),
                pl.BlockSpec(arrived.shape, lambda g, s: (0, 0)),
                row,
                row,
            ],
            out_specs=[
                pl.BlockSpec((None, obs, cols), lambda g, s: (g, 0, 0)),
                pl.BlockSpec((None, cols, 1), lambda g, s: (g, 0, 0)),
            ],
            scratch_shapes=[pltpu.VMEM((obs, cols), jnp.float32)],
        ),
        out_shape=[
            jax.ShapeDtypeStruct((plans, obs, cols), jnp.float32),
            jax.ShapeDtypeStruct((plans, cols, 1), jnp.float32),
        ],
        cost_estimate=pl.CostEstimate(
            flops=4 * plans * obs * width * cols, transcendentals=plans * nper * cols,
            bytes_accessed=plans * obs * width * 2),
    )(slot_of, basis, arrived, inv_cos, inv_sin)
    return model, ev.reshape(plans, cols)


def white_kernel(cnt_ref, cur_ref, att_ref, out_ref):
    segs, slots, _ = att_ref.shape
    width = out_ref.shape[1]
    blocks = cur_ref.shape[1] // width
    for s in range(segs):
        cur = cur_ref[pl.ds(s * slots, slots), :]
        slot = lax.broadcasted_iota(jnp.int32, cur.shape, 0)
        masked = jnp.where(slot < cnt_ref[s], cur, 0.0).astype(jnp.bfloat16)
        white = jnp.dot(att_ref[s], masked, preferred_element_type=jnp.float32)
        for b in range(blocks):
            out_ref[pl.ds(b * segs * slots + s * slots, slots), :] = white[:, b * width:(b + 1) * width]
    out_ref[pl.ds(blocks * segs * slots, 8), :] = jnp.zeros((8, width), jnp.float32)


def whiten_rows(counts, current, attitude_all, width):
    segs, slots, _ = attitude_all.shape
    rows = current.shape[0] * current.shape[1] // width
    return pl.pallas_call(
        white_kernel,
        in_specs=[pl.BlockSpec(memory_space=pltpu.SMEM)] + [pl.BlockSpec(memory_space=pltpu.VMEM)] * 2,
        out_specs=pl.BlockSpec(memory_space=pltpu.VMEM),
        out_shape=jax.ShapeDtypeStruct((rows + 8, width), jnp.float32),
        cost_estimate=pl.CostEstimate(
            flops=2 * segs * slots * slots * current.shape[1], transcendentals=0,
            bytes_accessed=current.size * 8 + attitude_all.size * 2),
    )(counts, current, attitude_all)


def scatter_sub_kernel(idx_ref, src_ref, cur_ref, out_ref, acc_ref):
    rows, width = src_ref.shape
    streams = acc_ref.shape[0]
    n = cur_ref.shape[0]
    acc_ref[...] = jnp.zeros_like(acc_ref)

    def body(step, carry):
        base = step * streams
        for s in range(streams):
            r = base + s
            i = idx_ref[r]
            acc_ref[s, pl.ds(i, 1), :] = acc_ref[s, pl.ds(i, 1), :] + src_ref[pl.ds(r, 1), :]
        return carry

    lax.fori_loop(0, rows // streams, body, 0, unroll=SUNROLL)
    for b in range(cur_ref.shape[1] // width):
        total = acc_ref[0, pl.ds(b * n, n), :]
        for s in range(1, streams):
            total = total + acc_ref[s, pl.ds(b * n, n), :]
        out_ref[:, b * width:(b + 1) * width] = cur_ref[:, b * width:(b + 1) * width] - total


def scatter_sub(src, idx, current):
    rows, width = src.shape
    blocks = current.shape[1] // width
    return pl.pallas_call(
        scatter_sub_kernel,
        in_specs=[pl.BlockSpec(memory_space=pltpu.SMEM)] + [pl.BlockSpec(memory_space=pltpu.VMEM)] * 2,
        out_specs=pl.BlockSpec(memory_space=pltpu.VMEM),
        out_shape=jax.ShapeDtypeStruct(current.shape, jnp.float32),
        scratch_shapes=[pltpu.VMEM((STREAMS, blocks * current.shape[0] + 8, width), jnp.float32)],
        cost_estimate=pl.CostEstimate(
            flops=rows * width, transcendentals=0, bytes_accessed=(rows * width + 2 * current.size) * 4),
    )(idx, src, current)

def fit_groups(basis, observed, norm_cos, norm_sin, nper):
    corr = jnp.einsum("fio,fic->foc", basis, observed, preferred_element_type=jnp.float32)
    cosine = corr[:, :nper]
    sine = corr[:, nper:]
    amp_c = cosine / norm_cos[:, :, None]
    amp_s = sine / norm_sin[:, :, None]
    power = cosine * amp_c + sine * amp_s
    logits = BETA * power
    highest = jnp.max(logits, axis=1)
    expo = jnp.exp(logits - highest[:, None, :])
    total = jnp.sum(expo, axis=1)
    share = expo / total[:, None, :]
    coeff = jnp.concatenate([share * amp_c, share * amp_s], axis=1).astype(jnp.bfloat16)
    model = jnp.einsum("fio,foc->fic", basis, coeff, preferred_element_type=jnp.float32)
    return (model, highest + jnp.log(total))


def on_device(residuals, seg_counts, attitude, sched_seg, sched_slot, periods):
    tm_count = lax.axis_size("tm")
    sched_dev, obs = sched_seg.shape
    seg_dev, slots, width = residuals.shape
    nper = periods.shape[0]
    column_blocks = width // SRC_GROUP
    capacity = 2 * sched_dev * obs // tm_count
    requests = sched_dev * obs
    seg_flat = sched_seg.reshape(-1)
    slot_flat = sched_slot.reshape(-1)
    block_of = jnp.repeat(jnp.arange(sched_dev, dtype=jnp.int32) % column_blocks, obs)
    target = seg_flat // seg_dev
    local_row = block_of * (seg_dev * slots) + seg_flat % seg_dev * slots + slot_flat
    onehot = (target[:, None] == jnp.arange(tm_count, dtype=jnp.int32)[None, :]).astype(jnp.int32)
    ones = onehot.astype(jnp.bfloat16).reshape(requests // 128, 128, tm_count)
    tril = (jnp.arange(128)[:, None] >= jnp.arange(128)[None, :]).astype(jnp.bfloat16)
    within = jnp.einsum("ij,bjc->bic", tril, ones, preferred_element_type=jnp.float32)
    totals = within[:, -1, :]
    before = jnp.cumsum(totals, axis=0) - totals
    counts = (within + before[:, None, :]).reshape(requests, tm_count)
    position = jnp.sum(counts * onehot.astype(jnp.float32), axis=1).astype(jnp.int32) - 1
    empty_row = seg_dev * slots * column_blocks
    slot_of = target * capacity + position
    pair = (
        jnp.broadcast_to(jnp.array([empty_row, 0], jnp.int32), (tm_count * capacity, 2))
        .at[slot_of]
        .set(jnp.stack([local_row, jnp.arange(requests, dtype=jnp.int32)], axis=1))
    )
    wanted = pair[:, 0].reshape(tm_count, capacity)
    inverse = pair[:, 1]
    asked = lax.all_to_all(wanted, "tm", split_axis=0, concat_axis=0, tiled=True).reshape(-1)
    basis, norm_cos, norm_sin = basis_and_norms(sched_seg * slots + sched_slot, periods)
    valid = jnp.arange(slots, dtype=jnp.int32)[None, :] < seg_counts[:, None]
    inv_cos = (1.0 / norm_cos).reshape(sched_dev, 1, nper)
    inv_sin = (1.0 / norm_sin).reshape(sched_dev, 1, nper)
    current = residuals.astype(jnp.float32).reshape(seg_dev * slots, width)
    evidence = jnp.zeros((sched_dev, SRC_GROUP), jnp.float32)
    attitude_all = lax.all_gather(attitude, "sky", axis=1, tiled=True)
    for iteration in range(ITERS):
        white = whiten_rows(seg_counts, current, attitude_all, SRC_GROUP)
        picked = row_gather(white, asked, jnp.bfloat16, norm_cos)
        outbound = picked.reshape(tm_count, capacity, SRC_GROUP)
        if iteration == 0:
            arrived = tm_all_to_all(outbound, jnp.float32, 1)
        else:
            arrived = lax.all_to_all(outbound, "tm", split_axis=0, concat_axis=0, tiled=True)
            arrived = arrived.astype(jnp.float32)
        model, evidence = fit_fused(
            basis, arrived.reshape(-1, SRC_GROUP), slot_of, inv_cos, inv_sin)
        outgoing = row_gather(model.reshape(requests, SRC_GROUP), inverse, jnp.bfloat16)
        returned = tm_all_to_all(
            outgoing.reshape(tm_count, capacity, SRC_GROUP),
            jnp.float32, 2 + 2 * iteration)
        current = scatter_sub(returned.reshape(-1, SRC_GROUP), asked, current)
    current = current.reshape(seg_dev, slots, width)
    return (current, evidence)


def solution(mesh):
    in_specs = (
        P("tm", None, "sky"),
        P("tm"),
        P("tm", "sky", None),
        P(("tm", "sky"), None),
        P(("tm", "sky"), None),
        P(),
    )
    out_specs = (P("tm", None, "sky"), P(("tm", "sky"), None))
    return jax.shard_map(
        on_device, mesh=mesh, in_specs=in_specs, out_specs=out_specs, check_vma=False
    )
```

```python
import jax
import jax.numpy as jnp
from jax import lax
from jax.experimental import pallas as pl
from jax.experimental.pallas import tpu as pltpu
from jax.sharding import PartitionSpec as P

SRC_GROUP = 128
ITERS = 2


TWO_PI = 6.283185307179586
BETA = 2.0
RIDGE = 1.0


PIO2_1 = 1.5703125
PIO2_2 = 4.837512969970703125e-4
PIO2_3 = 7.549789954891e-8
ROWS = 16
LANES = 512
UNROLL = 2


def basis_kernel(t_ref, p_ref, w_ref, inv_ref, basis_ref, nc_ref, ns_ref):
    obs = t_ref.shape[0]
    nper = p_ref.shape[1]

    def lane_block(j, carry):
        c0 = pl.multiple_of(j * LANES, LANES)
        pf = p_ref[:, pl.ds(c0, LANES)]
        w = w_ref[:, pl.ds(c0, LANES)]
        inv = inv_ref[:, pl.ds(c0, LANES)]

        def row_block(i, acc):
            acc_c, acc_s = acc
            r0 = pl.multiple_of(i * ROWS, ROWS)
            tf = jnp.broadcast_to(t_ref[pl.ds(r0, ROWS), :], (ROWS, LANES))
            q = jnp.floor(tf * inv)
            r = tf - q * pf
            r = jnp.where(r < 0.0, r + pf, r)
            r = jnp.where(r >= pf, r - pf, r)
            phase = r * w
            k = jnp.floor(phase * 0.6366197723675814 + 0.5)
            y = ((phase - k * PIO2_1) - k * PIO2_2) - k * PIO2_3
            z = y * y
            s = y + y * z * (-1.6666654611e-1 + z * (8.3321608736e-3 + z * -1.9515295891e-4))
            c = 1.0 - 0.5 * z + z * z * (4.166664568298827e-2 + z * (-1.388731625493765e-3 + z * 2.443315711809948e-5))
            odd = (k == 1.0) | (k == 3.0)
            cs = jnp.where(odd, s, c)
            sn = jnp.where(odd, c, s)
            cos_v = jnp.where((k == 1.0) | (k == 2.0), -cs, cs).astype(jnp.bfloat16)
            sin_v = jnp.where((k == 2.0) | (k == 3.0), -sn, sn).astype(jnp.bfloat16)
            basis_ref[pl.ds(r0, ROWS), pl.ds(c0, LANES)] = cos_v
            basis_ref[pl.ds(r0, ROWS), pl.ds(nper + c0, LANES)] = sin_v
            cf = cos_v.astype(jnp.float32)
            sf = sin_v.astype(jnp.float32)
            return acc_c + cf * cf, acc_s + sf * sf

        zero = jnp.zeros((ROWS, LANES), jnp.float32)
        acc_c, acc_s = lax.fori_loop(0, obs // ROWS, row_block, (zero, zero), unroll=UNROLL)
        nc_ref[:, pl.ds(c0, LANES)] = jnp.sum(acc_c, axis=0, keepdims=True) + RIDGE
        ns_ref[:, pl.ds(c0, LANES)] = jnp.sum(acc_s, axis=0, keepdims=True) + RIDGE
        return carry

    lax.fori_loop(0, nper // LANES, lane_block, 0)


def basis_and_norms(times, periods):
    plans, obs = times.shape
    nper = periods.shape[0]
    pf = periods.astype(jnp.float32)
    w = (TWO_PI / pf).reshape(1, nper)
    inv = (1.0 / pf).reshape(1, nper)
    pf = pf.reshape(1, nper)
    tf = times.astype(jnp.float32).reshape(plans, obs, 1)
    row = pl.BlockSpec((1, nper), lambda g: (0, 0))
    basis, nc, ns = pl.pallas_call(
        basis_kernel,
        grid=(plans,),
        in_specs=[pl.BlockSpec((None, obs, 1), lambda g: (g, 0, 0)), row, row, row],
        out_specs=[
            pl.BlockSpec((None, obs, 2 * nper), lambda g: (g, 0, 0)),
            pl.BlockSpec((None, 1, nper), lambda g: (g, 0, 0)),
            pl.BlockSpec((None, 1, nper), lambda g: (g, 0, 0)),
        ],
        out_shape=[
            jax.ShapeDtypeStruct((plans, obs, 2 * nper), jnp.bfloat16),
            jax.ShapeDtypeStruct((plans, 1, nper), jnp.float32),
            jax.ShapeDtypeStruct((plans, 1, nper), jnp.float32),
        ],
        cost_estimate=pl.CostEstimate(
            flops=60 * plans * obs * nper, transcendentals=0,
            bytes_accessed=plans * obs * 2 * nper * 2),
    )(tf, pf, w, inv)
    return basis, nc.reshape(plans, nper), ns.reshape(plans, nper)


def gather_kernel(idx_ref, src_ref, *rest):
    out_ref = rest[-2]
    stage_ref = rest[-1]
    block = stage_ref.shape[0]

    def body(b, carry):
        r0 = pl.multiple_of(b * block, block)
        for j in range(block):
            stage_ref[pl.ds(j, 1), :] = src_ref[pl.ds(idx_ref[r0 + j], 1), :]
        out_ref[pl.ds(r0, block), :] = stage_ref[...].astype(out_ref.dtype)
        return carry

    lax.fori_loop(0, out_ref.shape[0] // block, body, 0)


def row_gather(src, idx, out_dtype, *after):
    rows, width = idx.shape[0], src.shape[1]
    return pl.pallas_call(
        gather_kernel,
        in_specs=[pl.BlockSpec(memory_space=pltpu.SMEM), pl.BlockSpec(memory_space=pltpu.VMEM)]
        + [pl.BlockSpec(memory_space=pltpu.VMEM) for _ in after],
        out_specs=pl.BlockSpec(memory_space=pltpu.VMEM),
        out_shape=jax.ShapeDtypeStruct((rows, width), out_dtype),
        scratch_shapes=[pltpu.VMEM((32, width), src.dtype)],
        cost_estimate=pl.CostEstimate(
            flops=0, transcendentals=0, bytes_accessed=2 * rows * width * src.dtype.itemsize),
    )(idx, src, *after)


def with_zero_rows(flat):
    return jnp.concatenate([flat, jnp.zeros((8, flat.shape[1]), flat.dtype)], axis=0)


def a2a_kernel(x_ref, out_ref, held, send_sem, recv_sem):
    n = x_ref.shape[0]
    me = lax.axis_index("tm")
    sky = lax.axis_index("sky")
    barrier = pltpu.get_barrier_semaphore()

    def greet(k, carry):
        peer = lax.rem(me + k, n)
        pl.semaphore_signal(barrier, inc=1, device_id=(peer, sky), device_id_type=pl.DeviceIdType.MESH)
        return carry

    lax.fori_loop(1, n, greet, 0)
    pl.semaphore_wait(barrier, n - 1)

    def copy(k):
        peer = lax.rem(me + k, n)
        return pltpu.make_async_remote_copy(
            src_ref=x_ref.at[peer],
            dst_ref=held.at[me],
            send_sem=send_sem.at[k],
            recv_sem=recv_sem.at[k],
            device_id=(peer, sky),
            device_id_type=pl.DeviceIdType.MESH,
        )

    def start(j, carry):
        odd = j % 2
        copy((1 - odd) * (j // 2 + 1) + odd * (n - 1 - j // 2)).start()
        return carry

    lax.fori_loop(0, n - 1, start, 0)
    held[pl.ds(me, 1)] = x_ref[pl.ds(me, 1)]

    def finish(k, carry):
        copy(k).wait()
        return carry

    lax.fori_loop(1, n, finish, 0)
    out_ref[...] = held[...].astype(out_ref.dtype)


def tm_all_to_all(x, out_dtype, collective_id):
    n, rows, width = x.shape
    return pl.pallas_call(
        a2a_kernel,
        in_specs=[pl.BlockSpec(memory_space=pltpu.VMEM)],
        out_specs=pl.BlockSpec(memory_space=pltpu.VMEM),
        out_shape=jax.ShapeDtypeStruct((n, rows, width), out_dtype),
        scratch_shapes=[
            pltpu.VMEM((n, rows, width), x.dtype),
            pltpu.SemaphoreType.DMA((n,)),
            pltpu.SemaphoreType.DMA((n,)),
        ],
        compiler_params=pltpu.CompilerParams(collective_id=collective_id, has_side_effects=True),
    )(x)


STREAMS = 4
SUNROLL = 2

def scatter_add_kernel(idx_ref, src_ref, out_ref, acc_ref):
    rows = src_ref.shape[0]
    streams = acc_ref.shape[0]
    acc_ref[...] = jnp.zeros_like(acc_ref)

    def body(step, carry):
        base = step * streams
        for s in range(streams):
            r = base + s
            i = idx_ref[r]
            acc_ref[s, pl.ds(i, 1), :] = acc_ref[s, pl.ds(i, 1), :] + src_ref[pl.ds(r, 1), :]
        return carry

    lax.fori_loop(0, rows // streams, body, 0, unroll=SUNROLL)
    total = acc_ref[0]
    for s in range(1, streams):
        total = total + acc_ref[s]
    out_ref[...] = total[: out_ref.shape[0]]


def scatter_add(src, idx, out_rows):
    rows, width = src.shape
    pad = out_rows + 8
    return pl.pallas_call(
        scatter_add_kernel,
        in_specs=[pl.BlockSpec(memory_space=pltpu.SMEM), pl.BlockSpec(memory_space=pltpu.VMEM)],
        out_specs=pl.BlockSpec(memory_space=pltpu.VMEM),
        out_shape=jax.ShapeDtypeStruct((out_rows, width), jnp.float32),
        scratch_shapes=[pltpu.VMEM((STREAMS, pad, width), jnp.float32)],
        cost_estimate=pl.CostEstimate(flops=rows * width, transcendentals=0, bytes_accessed=(rows + out_rows) * width * 4),
    )(idx, src)


def fit_kernel(slot_ref, basis_ref, arrived_ref, inc_ref, ins_ref, model_ref, ev_ref, stage_ref):
    nper = inc_ref.shape[1]
    obs = stage_ref.shape[0]
    base = pl.program_id(0) * obs

    def pick(b, carry):
        r0 = pl.multiple_of(b * 32, 32)
        for j in range(32):
            stage_ref[pl.ds(r0 + j, 1), :] = arrived_ref[pl.ds(slot_ref[base + r0 + j], 1), :]
        return carry

    lax.fori_loop(0, obs // 32, pick, 0)
    basis = basis_ref[...]
    obs_t = stage_ref[...].T.astype(jnp.bfloat16)
    corr = jnp.dot(obs_t, basis, preferred_element_type=jnp.float32)
    cosine = corr[:, :nper]
    sine = corr[:, nper:]
    amp_c = cosine * inc_ref[...]
    amp_s = sine * ins_ref[...]
    logits = BETA * (cosine * amp_c + sine * amp_s)
    highest = jnp.max(logits, axis=1, keepdims=True)
    expo = jnp.exp(logits - highest)
    total = jnp.sum(expo, axis=1, keepdims=True)
    share = expo * (1.0 / total)
    coeff = jnp.concatenate([share * amp_c, share * amp_s], axis=1).astype(jnp.bfloat16)
    model_ref[...] = lax.dot_general(
        basis, coeff, (((1,), (1,)), ((), ())), preferred_element_type=jnp.float32)
    ev_ref[...] = highest + jnp.log(total)


def fit_fused(basis, arrived, slot_of, inv_cos, inv_sin):
    plans, obs, width = basis.shape
    cols = arrived.shape[1]
    nper = width // 2
    row = pl.BlockSpec((None, 1, nper), lambda g, s: (g, 0, 0))
    model, ev = pl.pallas_call(
        fit_kernel,
        grid_spec=pltpu.PrefetchScalarGridSpec(
            num_scalar_prefetch=1,
            grid=(plans,),
            in_specs=[
                pl.BlockSpec((None, obs, width), lambda g, s: (g, 0, 0)),
                pl.BlockSpec(arrived.shape, lambda g, s: (0, 0)),
                row,
                row,
            ],
            out_specs=[
                pl.BlockSpec((None, obs, cols), lambda g, s: (g, 0, 0)),
                pl.BlockSpec((None, cols, 1), lambda g, s: (g, 0, 0)),
            ],
            scratch_shapes=[pltpu.VMEM((obs, cols), jnp.float32)],
        ),
        out_shape=[
            jax.ShapeDtypeStruct((plans, obs, cols), jnp.float32),
            jax.ShapeDtypeStruct((plans, cols, 1), jnp.float32),
        ],
        cost_estimate=pl.CostEstimate(
            flops=4 * plans * obs * width * cols, transcendentals=plans * nper * cols,
            bytes_accessed=plans * obs * width * 2),
    )(slot_of, basis, arrived, inv_cos, inv_sin)
    return model, ev.reshape(plans, cols)


def white_kernel(cnt_ref, cur_ref, att_ref, out_ref):
    segs, slots, _ = att_ref.shape
    width = out_ref.shape[1]
    blocks = cur_ref.shape[1] // width
    for s in range(segs):
        cur = cur_ref[pl.ds(s * slots, slots), :]
        slot = lax.broadcasted_iota(jnp.int32, cur.shape, 0)
        masked = jnp.where(slot < cnt_ref[s], cur, 0.0).astype(jnp.bfloat16)
        white = jnp.dot(att_ref[s], masked, preferred_element_type=jnp.float32)
        for b in range(blocks):
            out_ref[pl.ds(b * segs * slots + s * slots, slots), :] = white[:, b * width:(b + 1) * width]
    out_ref[pl.ds(blocks * segs * slots, 8), :] = jnp.zeros((8, width), jnp.float32)


def whiten_rows(counts, current, attitude_all, width):
    segs, slots, _ = attitude_all.shape
    rows = current.shape[0] * current.shape[1] // width
    return pl.pallas_call(
        white_kernel,
        in_specs=[pl.BlockSpec(memory_space=pltpu.SMEM)] + [pl.BlockSpec(memory_space=pltpu.VMEM)] * 2,
        out_specs=pl.BlockSpec(memory_space=pltpu.VMEM),
        out_shape=jax.ShapeDtypeStruct((rows + 8, width), jnp.float32),
        cost_estimate=pl.CostEstimate(
            flops=2 * segs * slots * slots * current.shape[1], transcendentals=0,
            bytes_accessed=current.size * 8 + attitude_all.size * 2),
    )(counts, current, attitude_all)


def scatter_sub_kernel(idx_ref, src_ref, cur_ref, out_ref, acc_ref):
    rows, width = src_ref.shape
    streams = acc_ref.shape[0]
    n = cur_ref.shape[0]
    acc_ref[...] = jnp.zeros_like(acc_ref)

    def body(step, carry):
        base = step * streams
        for s in range(streams):
            r = base + s
            i = idx_ref[r]
            acc_ref[s, pl.ds(i, 1), :] = acc_ref[s, pl.ds(i, 1), :] + src_ref[pl.ds(r, 1), :]
        return carry

    lax.fori_loop(0, rows // streams, body, 0, unroll=SUNROLL)
    for b in range(cur_ref.shape[1] // width):
        total = acc_ref[0, pl.ds(b * n, n), :]
        for s in range(1, streams):
            total = total + acc_ref[s, pl.ds(b * n, n), :]
        out_ref[:, b * width:(b + 1) * width] = cur_ref[:, b * width:(b + 1) * width] - total


def scatter_sub(src, idx, current):
    rows, width = src.shape
    blocks = current.shape[1] // width
    return pl.pallas_call(
        scatter_sub_kernel,
        in_specs=[pl.BlockSpec(memory_space=pltpu.SMEM)] + [pl.BlockSpec(memory_space=pltpu.VMEM)] * 2,
        out_specs=pl.BlockSpec(memory_space=pltpu.VMEM),
        out_shape=jax.ShapeDtypeStruct(current.shape, jnp.float32),
        scratch_shapes=[pltpu.VMEM((STREAMS, blocks * current.shape[0] + 8, width), jnp.float32)],
        cost_estimate=pl.CostEstimate(
            flops=rows * width, transcendentals=0, bytes_accessed=(rows * width + 2 * current.size) * 4),
    )(idx, src, current)

def fit_groups(basis, observed, norm_cos, norm_sin, nper):
    corr = jnp.einsum("fio,fic->foc", basis, observed, preferred_element_type=jnp.float32)
    cosine = corr[:, :nper]
    sine = corr[:, nper:]
    amp_c = cosine / norm_cos[:, :, None]
    amp_s = sine / norm_sin[:, :, None]
    power = cosine * amp_c + sine * amp_s
    logits = BETA * power
    highest = jnp.max(logits, axis=1)
    expo = jnp.exp(logits - highest[:, None, :])
    total = jnp.sum(expo, axis=1)
    share = expo / total[:, None, :]
    coeff = jnp.concatenate([share * amp_c, share * amp_s], axis=1).astype(jnp.bfloat16)
    model = jnp.einsum("fio,foc->fic", basis, coeff, preferred_element_type=jnp.float32)
    return (model, highest + jnp.log(total))


def on_device(residuals, seg_counts, attitude, sched_seg, sched_slot, periods):
    tm_count = lax.axis_size("tm")
    sched_dev, obs = sched_seg.shape
    seg_dev, slots, width = residuals.shape
    nper = periods.shape[0]
    column_blocks = width // SRC_GROUP
    capacity = 2 * sched_dev * obs // tm_count
    requests = sched_dev * obs
    seg_flat = sched_seg.reshape(-1)
    slot_flat = sched_slot.reshape(-1)
    block_of = jnp.repeat(jnp.arange(sched_dev, dtype=jnp.int32) % column_blocks, obs)
    target = seg_flat // seg_dev
    local_row = block_of * (seg_dev * slots) + seg_flat % seg_dev * slots + slot_flat
    onehot = (target[:, None] == jnp.arange(tm_count, dtype=jnp.int32)[None, :]).astype(jnp.int32)
    ones = onehot.astype(jnp.bfloat16).reshape(requests // 128, 128, tm_count)
    tril = (jnp.arange(128)[:, None] >= jnp.arange(128)[None, :]).astype(jnp.bfloat16)
    within = jnp.einsum("ij,bjc->bic", tril, ones, preferred_element_type=jnp.float32)
    totals = within[:, -1, :]
    before = jnp.cumsum(totals, axis=0) - totals
    counts = (within + before[:, None, :]).reshape(requests, tm_count)
    position = jnp.sum(counts * onehot.astype(jnp.float32), axis=1).astype(jnp.int32) - 1
    empty_row = seg_dev * slots * column_blocks
    slot_of = target * capacity + position
    pair = (
        jnp.broadcast_to(jnp.array([empty_row, 0], jnp.int32), (tm_count * capacity, 2))
        .at[slot_of]
        .set(jnp.stack([local_row, jnp.arange(requests, dtype=jnp.int32)], axis=1))
    )
    wanted = pair[:, 0].reshape(tm_count, capacity)
    inverse = pair[:, 1]
    asked = lax.all_to_all(wanted, "tm", split_axis=0, concat_axis=0, tiled=True).reshape(-1)
    basis, norm_cos, norm_sin = basis_and_norms(sched_seg * slots + sched_slot, periods)
    valid = jnp.arange(slots, dtype=jnp.int32)[None, :] < seg_counts[:, None]
    inv_cos = (1.0 / norm_cos).reshape(sched_dev, 1, nper)
    inv_sin = (1.0 / norm_sin).reshape(sched_dev, 1, nper)
    current = residuals.astype(jnp.float32).reshape(seg_dev * slots, width)
    evidence = jnp.zeros((sched_dev, SRC_GROUP), jnp.float32)
    attitude_all = lax.all_gather(attitude, "sky", axis=1, tiled=True)
    for iteration in range(ITERS):
        white = whiten_rows(seg_counts, current, attitude_all, SRC_GROUP)
        picked = row_gather(white, asked, jnp.bfloat16, norm_cos)
        outbound = picked.reshape(tm_count, capacity, SRC_GROUP)
        arrived = tm_all_to_all(outbound, jnp.float32, 1 + 2 * iteration)
        model, evidence = fit_fused(
            basis, arrived.reshape(-1, SRC_GROUP), slot_of, inv_cos, inv_sin)
        outgoing = row_gather(model.reshape(requests, SRC_GROUP), inverse, jnp.bfloat16)
        returned = tm_all_to_all(
            outgoing.reshape(tm_count, capacity, SRC_GROUP),
            jnp.float32, 2 + 2 * iteration)
        current = scatter_sub(returned.reshape(-1, SRC_GROUP), asked, current)
    current = current.reshape(seg_dev, slots, width)
    return (current, evidence)


def solution(mesh):
    in_specs = (
        P("tm", None, "sky"),
        P("tm"),
        P("tm", "sky", None),
        P(("tm", "sky"), None),
        P(("tm", "sky"), None),
        P(),
    )
    out_specs = (P("tm", None, "sky"), P(("tm", "sky"), None))
    return jax.shard_map(
        on_device, mesh=mesh, in_specs=in_specs, out_specs=out_specs, check_vma=False
    )
```

```python
import jax
import jax.numpy as jnp
from jax import lax
from jax.experimental import pallas as pl
from jax.experimental.pallas import tpu as pltpu
from jax.sharding import PartitionSpec as P

SRC_GROUP = 128
ITERS = 2


TWO_PI = 6.283185307179586
BETA = 2.0
RIDGE = 1.0


PIO2_1 = 1.5703125
PIO2_2 = 4.837512969970703125e-4
PIO2_3 = 7.549789954891e-8
ROWS = 16
LANES = 512
UNROLL = 2


def basis_kernel(t_ref, p_ref, w_ref, inv_ref, basis_ref, nc_ref, ns_ref):
    obs = t_ref.shape[0]
    nper = p_ref.shape[1]

    def lane_block(j, carry):
        c0 = pl.multiple_of(j * LANES, LANES)
        pf = p_ref[:, pl.ds(c0, LANES)]
        w = w_ref[:, pl.ds(c0, LANES)]
        inv = inv_ref[:, pl.ds(c0, LANES)]

        def row_block(i, acc):
            acc_c, acc_s = acc
            r0 = pl.multiple_of(i * ROWS, ROWS)
            tf = jnp.broadcast_to(t_ref[pl.ds(r0, ROWS), :], (ROWS, LANES))
            q = jnp.floor(tf * inv)
            r = tf - q * pf
            r = jnp.where(r < 0.0, r + pf, r)
            r = jnp.where(r >= pf, r - pf, r)
            phase = r * w
            k = jnp.floor(phase * 0.6366197723675814 + 0.5)
            y = ((phase - k * PIO2_1) - k * PIO2_2) - k * PIO2_3
            z = y * y
            s = y + y * z * (-1.6666654611e-1 + z * (8.3321608736e-3 + z * -1.9515295891e-4))
            c = 1.0 - 0.5 * z + z * z * (4.166664568298827e-2 + z * (-1.388731625493765e-3 + z * 2.443315711809948e-5))
            odd = (k == 1.0) | (k == 3.0)
            cs = jnp.where(odd, s, c)
            sn = jnp.where(odd, c, s)
            cos_v = jnp.where((k == 1.0) | (k == 2.0), -cs, cs).astype(jnp.bfloat16)
            sin_v = jnp.where((k == 2.0) | (k == 3.0), -sn, sn).astype(jnp.bfloat16)
            basis_ref[pl.ds(r0, ROWS), pl.ds(c0, LANES)] = cos_v
            basis_ref[pl.ds(r0, ROWS), pl.ds(nper + c0, LANES)] = sin_v
            cf = cos_v.astype(jnp.float32)
            sf = sin_v.astype(jnp.float32)
            return acc_c + cf * cf, acc_s + sf * sf

        zero = jnp.zeros((ROWS, LANES), jnp.float32)
        acc_c, acc_s = lax.fori_loop(0, obs // ROWS, row_block, (zero, zero), unroll=UNROLL)
        nc_ref[:, pl.ds(c0, LANES)] = jnp.sum(acc_c, axis=0, keepdims=True) + RIDGE
        ns_ref[:, pl.ds(c0, LANES)] = jnp.sum(acc_s, axis=0, keepdims=True) + RIDGE
        return carry

    lax.fori_loop(0, nper // LANES, lane_block, 0)


def basis_and_norms(times, periods):
    plans, obs = times.shape
    nper = periods.shape[0]
    pf = periods.astype(jnp.float32)
    w = (TWO_PI / pf).reshape(1, nper)
    inv = (1.0 / pf).reshape(1, nper)
    pf = pf.reshape(1, nper)
    tf = times.astype(jnp.float32).reshape(plans, obs, 1)
    row = pl.BlockSpec((1, nper), lambda g: (0, 0))
    basis, nc, ns = pl.pallas_call(
        basis_kernel,
        grid=(plans,),
        in_specs=[pl.BlockSpec((None, obs, 1), lambda g: (g, 0, 0)), row, row, row],
        out_specs=[
            pl.BlockSpec((None, obs, 2 * nper), lambda g: (g, 0, 0)),
            pl.BlockSpec((None, 1, nper), lambda g: (g, 0, 0)),
            pl.BlockSpec((None, 1, nper), lambda g: (g, 0, 0)),
        ],
        out_shape=[
            jax.ShapeDtypeStruct((plans, obs, 2 * nper), jnp.bfloat16),
            jax.ShapeDtypeStruct((plans, 1, nper), jnp.float32),
            jax.ShapeDtypeStruct((plans, 1, nper), jnp.float32),
        ],
        cost_estimate=pl.CostEstimate(
            flops=60 * plans * obs * nper, transcendentals=0,
            bytes_accessed=plans * obs * 2 * nper * 2),
    )(tf, pf, w, inv)
    return basis, nc.reshape(plans, nper), ns.reshape(plans, nper)


def gather_kernel(idx_ref, src_ref, *rest):
    out_ref = rest[-2]
    stage_ref = rest[-1]
    block = stage_ref.shape[0]

    def body(b, carry):
        r0 = pl.multiple_of(b * block, block)
        for j in range(block):
            stage_ref[pl.ds(j, 1), :] = src_ref[pl.ds(idx_ref[r0 + j], 1), :]
        out_ref[pl.ds(r0, block), :] = stage_ref[...].astype(out_ref.dtype)
        return carry

    lax.fori_loop(0, out_ref.shape[0] // block, body, 0)


def row_gather(src, idx, out_dtype, *after):
    rows, width = idx.shape[0], src.shape[1]
    return pl.pallas_call(
        gather_kernel,
        in_specs=[pl.BlockSpec(memory_space=pltpu.SMEM), pl.BlockSpec(memory_space=pltpu.VMEM)]
        + [pl.BlockSpec(memory_space=pltpu.VMEM) for _ in after],
        out_specs=pl.BlockSpec(memory_space=pltpu.VMEM),
        out_shape=jax.ShapeDtypeStruct((rows, width), out_dtype),
        scratch_shapes=[pltpu.VMEM((32, width), src.dtype)],
        cost_estimate=pl.CostEstimate(
            flops=0, transcendentals=0, bytes_accessed=2 * rows * width * src.dtype.itemsize),
    )(idx, src, *after)


def with_zero_rows(flat):
    return jnp.concatenate([flat, jnp.zeros((8, flat.shape[1]), flat.dtype)], axis=0)


def a2a_kernel(x_ref, out_ref, held, send_sem, recv_sem):
    n = x_ref.shape[0]
    me = lax.axis_index("tm")
    sky = lax.axis_index("sky")
    barrier = pltpu.get_barrier_semaphore()

    def greet(k, carry):
        peer = lax.rem(me + k, n)
        pl.semaphore_signal(barrier, inc=1, device_id=(peer, sky), device_id_type=pl.DeviceIdType.MESH)
        return carry

    lax.fori_loop(1, n, greet, 0)
    pl.semaphore_wait(barrier, n - 1)

    def copy(k):
        peer = lax.rem(me + k, n)
        return pltpu.make_async_remote_copy(
            src_ref=x_ref.at[peer],
            dst_ref=held.at[me],
            send_sem=send_sem.at[k],
            recv_sem=recv_sem.at[k],
            device_id=(peer, sky),
            device_id_type=pl.DeviceIdType.MESH,
        )

    def start(j, carry):
        half = (j + 1) // 2
        copy(n // 2 + half - 2 * (j % 2) * half).start()
        return carry

    lax.fori_loop(0, n - 1, start, 0)
    held[pl.ds(me, 1)] = x_ref[pl.ds(me, 1)]

    def finish(k, carry):
        copy(k).wait()
        return carry

    lax.fori_loop(1, n, finish, 0)
    out_ref[...] = held[...].astype(out_ref.dtype)


def tm_all_to_all(x, out_dtype, collective_id):
    n, rows, width = x.shape
    return pl.pallas_call(
        a2a_kernel,
        in_specs=[pl.BlockSpec(memory_space=pltpu.VMEM)],
        out_specs=pl.BlockSpec(memory_space=pltpu.VMEM),
        out_shape=jax.ShapeDtypeStruct((n, rows, width), out_dtype),
        scratch_shapes=[
            pltpu.VMEM((n, rows, width), x.dtype),
            pltpu.SemaphoreType.DMA((n,)),
            pltpu.SemaphoreType.DMA((n,)),
        ],
        compiler_params=pltpu.CompilerParams(collective_id=collective_id, has_side_effects=True),
    )(x)


STREAMS = 4
SUNROLL = 2

def scatter_add_kernel(idx_ref, src_ref, out_ref, acc_ref):
    rows = src_ref.shape[0]
    streams = acc_ref.shape[0]
    acc_ref[...] = jnp.zeros_like(acc_ref)

    def body(step, carry):
        base = step * streams
        for s in range(streams):
            r = base + s
            i = idx_ref[r]
            acc_ref[s, pl.ds(i, 1), :] = acc_ref[s, pl.ds(i, 1), :] + src_ref[pl.ds(r, 1), :]
        return carry

    lax.fori_loop(0, rows // streams, body, 0, unroll=SUNROLL)
    total = acc_ref[0]
    for s in range(1, streams):
        total = total + acc_ref[s]
    out_ref[...] = total[: out_ref.shape[0]]


def scatter_add(src, idx, out_rows):
    rows, width = src.shape
    pad = out_rows + 8
    return pl.pallas_call(
        scatter_add_kernel,
        in_specs=[pl.BlockSpec(memory_space=pltpu.SMEM), pl.BlockSpec(memory_space=pltpu.VMEM)],
        out_specs=pl.BlockSpec(memory_space=pltpu.VMEM),
        out_shape=jax.ShapeDtypeStruct((out_rows, width), jnp.float32),
        scratch_shapes=[pltpu.VMEM((STREAMS, pad, width), jnp.float32)],
        cost_estimate=pl.CostEstimate(flops=rows * width, transcendentals=0, bytes_accessed=(rows + out_rows) * width * 4),
    )(idx, src)


def fit_kernel(slot_ref, basis_ref, arrived_ref, inc_ref, ins_ref, model_ref, ev_ref, stage_ref):
    nper = inc_ref.shape[1]
    obs = stage_ref.shape[0]
    base = pl.program_id(0) * obs

    def pick(b, carry):
        r0 = pl.multiple_of(b * 32, 32)
        for j in range(32):
            stage_ref[pl.ds(r0 + j, 1), :] = arrived_ref[pl.ds(slot_ref[base + r0 + j], 1), :]
        return carry

    lax.fori_loop(0, obs // 32, pick, 0)
    basis = basis_ref[...]
    obs_t = stage_ref[...].T.astype(jnp.bfloat16)
    corr = jnp.dot(obs_t, basis, preferred_element_type=jnp.float32)
    cosine = corr[:, :nper]
    sine = corr[:, nper:]
    amp_c = cosine * inc_ref[...]
    amp_s = sine * ins_ref[...]
    logits = BETA * (cosine * amp_c + sine * amp_s)
    highest = jnp.max(logits, axis=1, keepdims=True)
    expo = jnp.exp(logits - highest)
    total = jnp.sum(expo, axis=1, keepdims=True)
    share = expo * (1.0 / total)
    coeff = jnp.concatenate([share * amp_c, share * amp_s], axis=1).astype(jnp.bfloat16)
    model_ref[...] = lax.dot_general(
        basis, coeff, (((1,), (1,)), ((), ())), preferred_element_type=jnp.float32)
    ev_ref[...] = highest + jnp.log(total)


def fit_fused(basis, arrived, slot_of, inv_cos, inv_sin):
    plans, obs, width = basis.shape
    cols = arrived.shape[1]
    nper = width // 2
    row = pl.BlockSpec((None, 1, nper), lambda g, s: (g, 0, 0))
    model, ev = pl.pallas_call(
        fit_kernel,
        grid_spec=pltpu.PrefetchScalarGridSpec(
            num_scalar_prefetch=1,
            grid=(plans,),
            in_specs=[
                pl.BlockSpec((None, obs, width), lambda g, s: (g, 0, 0)),
                pl.BlockSpec(arrived.shape, lambda g, s: (0, 0)),
                row,
                row,
            ],
            out_specs=[
                pl.BlockSpec((None, obs, cols), lambda g, s: (g, 0, 0)),
                pl.BlockSpec((None, cols, 1), lambda g, s: (g, 0, 0)),
            ],
            scratch_shapes=[pltpu.VMEM((obs, cols), jnp.float32)],
        ),
        out_shape=[
            jax.ShapeDtypeStruct((plans, obs, cols), jnp.float32),
            jax.ShapeDtypeStruct((plans, cols, 1), jnp.float32),
        ],
        cost_estimate=pl.CostEstimate(
            flops=4 * plans * obs * width * cols, transcendentals=plans * nper * cols,
            bytes_accessed=plans * obs * width * 2),
    )(slot_of, basis, arrived, inv_cos, inv_sin)
    return model, ev.reshape(plans, cols)


def white_kernel(cnt_ref, cur_ref, att_ref, out_ref):
    segs, slots, _ = att_ref.shape
    width = out_ref.shape[1]
    blocks = cur_ref.shape[1] // width
    for s in range(segs):
        cur = cur_ref[pl.ds(s * slots, slots), :]
        slot = lax.broadcasted_iota(jnp.int32, cur.shape, 0)
        masked = jnp.where(slot < cnt_ref[s], cur, 0.0).astype(jnp.bfloat16)
        white = jnp.dot(att_ref[s], masked, preferred_element_type=jnp.float32)
        for b in range(blocks):
            out_ref[pl.ds(b * segs * slots + s * slots, slots), :] = white[:, b * width:(b + 1) * width]
    out_ref[pl.ds(blocks * segs * slots, 8), :] = jnp.zeros((8, width), jnp.float32)


def whiten_rows(counts, current, attitude_all, width):
    segs, slots, _ = attitude_all.shape
    rows = current.shape[0] * current.shape[1] // width
    return pl.pallas_call(
        white_kernel,
        in_specs=[pl.BlockSpec(memory_space=pltpu.SMEM)] + [pl.BlockSpec(memory_space=pltpu.VMEM)] * 2,
        out_specs=pl.BlockSpec(memory_space=pltpu.VMEM),
        out_shape=jax.ShapeDtypeStruct((rows + 8, width), jnp.float32),
        cost_estimate=pl.CostEstimate(
            flops=2 * segs * slots * slots * current.shape[1], transcendentals=0,
            bytes_accessed=current.size * 8 + attitude_all.size * 2),
    )(counts, current, attitude_all)


def scatter_sub_kernel(idx_ref, src_ref, cur_ref, out_ref, acc_ref):
    rows, width = src_ref.shape
    streams = acc_ref.shape[0]
    n = cur_ref.shape[0]
    acc_ref[...] = jnp.zeros_like(acc_ref)

    def body(step, carry):
        base = step * streams
        for s in range(streams):
            r = base + s
            i = idx_ref[r]
            acc_ref[s, pl.ds(i, 1), :] = acc_ref[s, pl.ds(i, 1), :] + src_ref[pl.ds(r, 1), :]
        return carry

    lax.fori_loop(0, rows // streams, body, 0, unroll=SUNROLL)
    for b in range(cur_ref.shape[1] // width):
        total = acc_ref[0, pl.ds(b * n, n), :]
        for s in range(1, streams):
            total = total + acc_ref[s, pl.ds(b * n, n), :]
        out_ref[:, b * width:(b + 1) * width] = cur_ref[:, b * width:(b + 1) * width] - total


def scatter_sub(src, idx, current):
    rows, width = src.shape
    blocks = current.shape[1] // width
    return pl.pallas_call(
        scatter_sub_kernel,
        in_specs=[pl.BlockSpec(memory_space=pltpu.SMEM)] + [pl.BlockSpec(memory_space=pltpu.VMEM)] * 2,
        out_specs=pl.BlockSpec(memory_space=pltpu.VMEM),
        out_shape=jax.ShapeDtypeStruct(current.shape, jnp.float32),
        scratch_shapes=[pltpu.VMEM((STREAMS, blocks * current.shape[0] + 8, width), jnp.float32)],
        cost_estimate=pl.CostEstimate(
            flops=rows * width, transcendentals=0, bytes_accessed=(rows * width + 2 * current.size) * 4),
    )(idx, src, current)

def fit_groups(basis, observed, norm_cos, norm_sin, nper):
    corr = jnp.einsum("fio,fic->foc", basis, observed, preferred_element_type=jnp.float32)
    cosine = corr[:, :nper]
    sine = corr[:, nper:]
    amp_c = cosine / norm_cos[:, :, None]
    amp_s = sine / norm_sin[:, :, None]
    power = cosine * amp_c + sine * amp_s
    logits = BETA * power
    highest = jnp.max(logits, axis=1)
    expo = jnp.exp(logits - highest[:, None, :])
    total = jnp.sum(expo, axis=1)
    share = expo / total[:, None, :]
    coeff = jnp.concatenate([share * amp_c, share * amp_s], axis=1).astype(jnp.bfloat16)
    model = jnp.einsum("fio,foc->fic", basis, coeff, preferred_element_type=jnp.float32)
    return (model, highest + jnp.log(total))


def on_device(residuals, seg_counts, attitude, sched_seg, sched_slot, periods):
    tm_count = lax.axis_size("tm")
    sched_dev, obs = sched_seg.shape
    seg_dev, slots, width = residuals.shape
    nper = periods.shape[0]
    column_blocks = width // SRC_GROUP
    capacity = 2 * sched_dev * obs // tm_count
    requests = sched_dev * obs
    seg_flat = sched_seg.reshape(-1)
    slot_flat = sched_slot.reshape(-1)
    block_of = jnp.repeat(jnp.arange(sched_dev, dtype=jnp.int32) % column_blocks, obs)
    target = seg_flat // seg_dev
    local_row = block_of * (seg_dev * slots) + seg_flat % seg_dev * slots + slot_flat
    onehot = (target[:, None] == jnp.arange(tm_count, dtype=jnp.int32)[None, :]).astype(jnp.int32)
    ones = onehot.astype(jnp.bfloat16).reshape(requests // 128, 128, tm_count)
    tril = (jnp.arange(128)[:, None] >= jnp.arange(128)[None, :]).astype(jnp.bfloat16)
    within = jnp.einsum("ij,bjc->bic", tril, ones, preferred_element_type=jnp.float32)
    totals = within[:, -1, :]
    before = jnp.cumsum(totals, axis=0) - totals
    counts = (within + before[:, None, :]).reshape(requests, tm_count)
    position = jnp.sum(counts * onehot.astype(jnp.float32), axis=1).astype(jnp.int32) - 1
    empty_row = seg_dev * slots * column_blocks
    slot_of = target * capacity + position
    pair = (
        jnp.broadcast_to(jnp.array([empty_row, 0], jnp.int32), (tm_count * capacity, 2))
        .at[slot_of]
        .set(jnp.stack([local_row, jnp.arange(requests, dtype=jnp.int32)], axis=1))
    )
    wanted = pair[:, 0].reshape(tm_count, capacity)
    inverse = pair[:, 1]
    asked = lax.all_to_all(wanted, "tm", split_axis=0, concat_axis=0, tiled=True).reshape(-1)
    basis, norm_cos, norm_sin = basis_and_norms(sched_seg * slots + sched_slot, periods)
    valid = jnp.arange(slots, dtype=jnp.int32)[None, :] < seg_counts[:, None]
    inv_cos = (1.0 / norm_cos).reshape(sched_dev, 1, nper)
    inv_sin = (1.0 / norm_sin).reshape(sched_dev, 1, nper)
    current = residuals.astype(jnp.float32).reshape(seg_dev * slots, width)
    evidence = jnp.zeros((sched_dev, SRC_GROUP), jnp.float32)
    attitude_all = lax.all_gather(attitude, "sky", axis=1, tiled=True)
    for iteration in range(ITERS):
        white = whiten_rows(seg_counts, current, attitude_all, SRC_GROUP)
        picked = row_gather(white, asked, jnp.bfloat16, norm_cos)
        outbound = picked.reshape(tm_count, capacity, SRC_GROUP)
        arrived = tm_all_to_all(outbound, jnp.float32, 1 + 2 * iteration)
        model, evidence = fit_fused(
            basis, arrived.reshape(-1, SRC_GROUP), slot_of, inv_cos, inv_sin)
        outgoing = row_gather(model.reshape(requests, SRC_GROUP), inverse, jnp.bfloat16)
        returned = tm_all_to_all(
            outgoing.reshape(tm_count, capacity, SRC_GROUP),
            jnp.float32, 2 + 2 * iteration)
        current = scatter_sub(returned.reshape(-1, SRC_GROUP), asked, current)
    current = current.reshape(seg_dev, slots, width)
    return (current, evidence)


def solution(mesh):
    in_specs = (
        P("tm", None, "sky"),
        P("tm"),
        P("tm", "sky", None),
        P(("tm", "sky"), None),
        P(("tm", "sky"), None),
        P(),
    )
    out_specs = (P("tm", None, "sky"), P(("tm", "sky"), None))
    return jax.shard_map(
        on_device, mesh=mesh, in_specs=in_specs, out_specs=out_specs, check_vma=False
    )
```

```python
import jax
import jax.numpy as jnp
from jax import lax
from jax.experimental import pallas as pl
from jax.experimental.pallas import tpu as pltpu
from jax.sharding import PartitionSpec as P

SRC_GROUP = 128
ITERS = 2


TWO_PI = 6.283185307179586
BETA = 2.0
RIDGE = 1.0


PIO2_1 = 1.5703125
PIO2_2 = 4.837512969970703125e-4
PIO2_3 = 7.549789954891e-8
ROWS = 16
LANES = 512
UNROLL = 2


def basis_kernel(t_ref, p_ref, w_ref, inv_ref, basis_ref, nc_ref, ns_ref):
    obs = t_ref.shape[0]
    nper = p_ref.shape[1]

    def lane_block(j, carry):
        c0 = pl.multiple_of(j * LANES, LANES)
        pf = p_ref[:, pl.ds(c0, LANES)]
        w = w_ref[:, pl.ds(c0, LANES)]
        inv = inv_ref[:, pl.ds(c0, LANES)]

        def row_block(i, acc):
            acc_c, acc_s = acc
            r0 = pl.multiple_of(i * ROWS, ROWS)
            tf = jnp.broadcast_to(t_ref[pl.ds(r0, ROWS), :], (ROWS, LANES))
            q = jnp.floor(tf * inv)
            r = tf - q * pf
            r = jnp.where(r < 0.0, r + pf, r)
            r = jnp.where(r >= pf, r - pf, r)
            phase = r * w
            k = jnp.floor(phase * 0.6366197723675814 + 0.5)
            y = ((phase - k * PIO2_1) - k * PIO2_2) - k * PIO2_3
            z = y * y
            s = y + y * z * (-1.6666654611e-1 + z * (8.3321608736e-3 + z * -1.9515295891e-4))
            c = 1.0 - 0.5 * z + z * z * (4.166664568298827e-2 + z * (-1.388731625493765e-3 + z * 2.443315711809948e-5))
            odd = (k == 1.0) | (k == 3.0)
            cs = jnp.where(odd, s, c)
            sn = jnp.where(odd, c, s)
            cos_v = jnp.where((k == 1.0) | (k == 2.0), -cs, cs).astype(jnp.bfloat16)
            sin_v = jnp.where((k == 2.0) | (k == 3.0), -sn, sn).astype(jnp.bfloat16)
            basis_ref[pl.ds(r0, ROWS), pl.ds(c0, LANES)] = cos_v
            basis_ref[pl.ds(r0, ROWS), pl.ds(nper + c0, LANES)] = sin_v
            cf = cos_v.astype(jnp.float32)
            sf = sin_v.astype(jnp.float32)
            return acc_c + cf * cf, acc_s + sf * sf

        zero = jnp.zeros((ROWS, LANES), jnp.float32)
        acc_c, acc_s = lax.fori_loop(0, obs // ROWS, row_block, (zero, zero), unroll=UNROLL)
        nc_ref[:, pl.ds(c0, LANES)] = jnp.sum(acc_c, axis=0, keepdims=True) + RIDGE
        ns_ref[:, pl.ds(c0, LANES)] = jnp.sum(acc_s, axis=0, keepdims=True) + RIDGE
        return carry

    lax.fori_loop(0, nper // LANES, lane_block, 0)


def basis_and_norms(times, periods):
    plans, obs = times.shape
    nper = periods.shape[0]
    pf = periods.astype(jnp.float32)
    w = (TWO_PI / pf).reshape(1, nper)
    inv = (1.0 / pf).reshape(1, nper)
    pf = pf.reshape(1, nper)
    tf = times.astype(jnp.float32).reshape(plans, obs, 1)
    row = pl.BlockSpec((1, nper), lambda g: (0, 0))
    basis, nc, ns = pl.pallas_call(
        basis_kernel,
        grid=(plans,),
        in_specs=[pl.BlockSpec((None, obs, 1), lambda g: (g, 0, 0)), row, row, row],
        out_specs=[
            pl.BlockSpec((None, obs, 2 * nper), lambda g: (g, 0, 0)),
            pl.BlockSpec((None, 1, nper), lambda g: (g, 0, 0)),
            pl.BlockSpec((None, 1, nper), lambda g: (g, 0, 0)),
        ],
        out_shape=[
            jax.ShapeDtypeStruct((plans, obs, 2 * nper), jnp.bfloat16),
            jax.ShapeDtypeStruct((plans, 1, nper), jnp.float32),
            jax.ShapeDtypeStruct((plans, 1, nper), jnp.float32),
        ],
        cost_estimate=pl.CostEstimate(
            flops=60 * plans * obs * nper, transcendentals=0,
            bytes_accessed=plans * obs * 2 * nper * 2),
    )(tf, pf, w, inv)
    return basis, nc.reshape(plans, nper), ns.reshape(plans, nper)


def gather_kernel(idx_ref, src_ref, *rest):
    out_ref = rest[-2]
    stage_ref = rest[-1]
    block = stage_ref.shape[0]

    def body(b, carry):
        r0 = pl.multiple_of(b * block, block)
        for j in range(block):
            stage_ref[pl.ds(j, 1), :] = src_ref[pl.ds(idx_ref[r0 + j], 1), :]
        out_ref[pl.ds(r0, block), :] = stage_ref[...].astype(out_ref.dtype)
        return carry

    lax.fori_loop(0, out_ref.shape[0] // block, body, 0)


def row_gather(src, idx, out_dtype, *after):
    rows, width = idx.shape[0], src.shape[1]
    return pl.pallas_call(
        gather_kernel,
        in_specs=[pl.BlockSpec(memory_space=pltpu.SMEM), pl.BlockSpec(memory_space=pltpu.VMEM)]
        + [pl.BlockSpec(memory_space=pltpu.VMEM) for _ in after],
        out_specs=pl.BlockSpec(memory_space=pltpu.VMEM),
        out_shape=jax.ShapeDtypeStruct((rows, width), out_dtype),
        scratch_shapes=[pltpu.VMEM((32, width), src.dtype)],
        cost_estimate=pl.CostEstimate(
            flops=0, transcendentals=0, bytes_accessed=2 * rows * width * src.dtype.itemsize),
    )(idx, src, *after)


def with_zero_rows(flat):
    return jnp.concatenate([flat, jnp.zeros((8, flat.shape[1]), flat.dtype)], axis=0)


def a2a_kernel(x_ref, out_ref, held, send_sem, recv_sem, own_sem):
    n = x_ref.shape[0]
    me = lax.axis_index("tm")
    sky = lax.axis_index("sky")
    barrier = pltpu.get_barrier_semaphore()

    def greet(k, carry):
        peer = lax.rem(me + k, n)
        pl.semaphore_signal(barrier, inc=1, device_id=(peer, sky), device_id_type=pl.DeviceIdType.MESH)
        return carry

    lax.fori_loop(1, n, greet, 0)
    pl.semaphore_wait(barrier, n - 1)

    def copy(k):
        peer = lax.rem(me + k, n)
        return pltpu.make_async_remote_copy(
            src_ref=x_ref.at[peer],
            dst_ref=held.at[me],
            send_sem=send_sem.at[k],
            recv_sem=recv_sem.at[k],
            device_id=(peer, sky),
            device_id_type=pl.DeviceIdType.MESH,
        )

    def start(j, carry):
        odd = j % 2
        copy((1 - odd) * (j // 2 + 1) + odd * (n - 1 - j // 2)).start()
        return carry

    lax.fori_loop(0, n - 1, start, 0)
    own = pltpu.make_async_copy(x_ref.at[me], held.at[me], own_sem.at[0])
    own.start()

    def finish(k, carry):
        copy(k).wait()
        return carry

    lax.fori_loop(1, n, finish, 0)
    own.wait()
    out_ref[...] = held[...].astype(out_ref.dtype)


def tm_all_to_all(x, out_dtype, collective_id):
    n, rows, width = x.shape
    return pl.pallas_call(
        a2a_kernel,
        in_specs=[pl.BlockSpec(memory_space=pl.ANY)],
        out_specs=pl.BlockSpec(memory_space=pltpu.VMEM),
        out_shape=jax.ShapeDtypeStruct((n, rows, width), out_dtype),
        scratch_shapes=[
            pltpu.VMEM((n, rows, width), x.dtype),
            pltpu.SemaphoreType.DMA((n,)),
            pltpu.SemaphoreType.DMA((n,)),
            pltpu.SemaphoreType.DMA((1,)),
        ],
        compiler_params=pltpu.CompilerParams(collective_id=collective_id, has_side_effects=True),
    )(x)


STREAMS = 4
SUNROLL = 2

def scatter_add_kernel(idx_ref, src_ref, out_ref, acc_ref):
    rows = src_ref.shape[0]
    streams = acc_ref.shape[0]
    acc_ref[...] = jnp.zeros_like(acc_ref)

    def body(step, carry):
        base = step * streams
        for s in range(streams):
            r = base + s
            i = idx_ref[r]
            acc_ref[s, pl.ds(i, 1), :] = acc_ref[s, pl.ds(i, 1), :] + src_ref[pl.ds(r, 1), :]
        return carry

    lax.fori_loop(0, rows // streams, body, 0, unroll=SUNROLL)
    total = acc_ref[0]
    for s in range(1, streams):
        total = total + acc_ref[s]
    out_ref[...] = total[: out_ref.shape[0]]


def scatter_add(src, idx, out_rows):
    rows, width = src.shape
    pad = out_rows + 8
    return pl.pallas_call(
        scatter_add_kernel,
        in_specs=[pl.BlockSpec(memory_space=pltpu.SMEM), pl.BlockSpec(memory_space=pltpu.VMEM)],
        out_specs=pl.BlockSpec(memory_space=pltpu.VMEM),
        out_shape=jax.ShapeDtypeStruct((out_rows, width), jnp.float32),
        scratch_shapes=[pltpu.VMEM((STREAMS, pad, width), jnp.float32)],
        cost_estimate=pl.CostEstimate(flops=rows * width, transcendentals=0, bytes_accessed=(rows + out_rows) * width * 4),
    )(idx, src)


def fit_kernel(slot_ref, basis_ref, arrived_ref, inc_ref, ins_ref, model_ref, ev_ref, stage_ref):
    nper = inc_ref.shape[1]
    obs = stage_ref.shape[0]
    base = pl.program_id(0) * obs

    def pick(b, carry):
        r0 = pl.multiple_of(b * 32, 32)
        for j in range(32):
            stage_ref[pl.ds(r0 + j, 1), :] = arrived_ref[pl.ds(slot_ref[base + r0 + j], 1), :]
        return carry

    lax.fori_loop(0, obs // 32, pick, 0)
    basis = basis_ref[...]
    obs_t = stage_ref[...].T.astype(jnp.bfloat16)
    corr = jnp.dot(obs_t, basis, preferred_element_type=jnp.float32)
    cosine = corr[:, :nper]
    sine = corr[:, nper:]
    amp_c = cosine * inc_ref[...]
    amp_s = sine * ins_ref[...]
    logits = BETA * (cosine * amp_c + sine * amp_s)
    highest = jnp.max(logits, axis=1, keepdims=True)
    expo = jnp.exp(logits - highest)
    total = jnp.sum(expo, axis=1, keepdims=True)
    share = expo * (1.0 / total)
    coeff = jnp.concatenate([share * amp_c, share * amp_s], axis=1).astype(jnp.bfloat16)
    model_ref[...] = lax.dot_general(
        basis, coeff, (((1,), (1,)), ((), ())), preferred_element_type=jnp.float32)
    ev_ref[...] = highest + jnp.log(total)


def fit_fused(basis, arrived, slot_of, inv_cos, inv_sin):
    plans, obs, width = basis.shape
    cols = arrived.shape[1]
    nper = width // 2
    row = pl.BlockSpec((None, 1, nper), lambda g, s: (g, 0, 0))
    model, ev = pl.pallas_call(
        fit_kernel,
        grid_spec=pltpu.PrefetchScalarGridSpec(
            num_scalar_prefetch=1,
            grid=(plans,),
            in_specs=[
                pl.BlockSpec((None, obs, width), lambda g, s: (g, 0, 0)),
                pl.BlockSpec(arrived.shape, lambda g, s: (0, 0)),
                row,
                row,
            ],
            out_specs=[
                pl.BlockSpec((None, obs, cols), lambda g, s: (g, 0, 0)),
                pl.BlockSpec((None, cols, 1), lambda g, s: (g, 0, 0)),
            ],
            scratch_shapes=[pltpu.VMEM((obs, cols), jnp.float32)],
        ),
        out_shape=[
            jax.ShapeDtypeStruct((plans, obs, cols), jnp.float32),
            jax.ShapeDtypeStruct((plans, cols, 1), jnp.float32),
        ],
        cost_estimate=pl.CostEstimate(
            flops=4 * plans * obs * width * cols, transcendentals=plans * nper * cols,
            bytes_accessed=plans * obs * width * 2),
    )(slot_of, basis, arrived, inv_cos, inv_sin)
    return model, ev.reshape(plans, cols)


def white_kernel(cnt_ref, cur_ref, att_ref, out_ref):
    segs, slots, _ = att_ref.shape
    width = out_ref.shape[1]
    blocks = cur_ref.shape[1] // width
    for s in range(segs):
        cur = cur_ref[pl.ds(s * slots, slots), :]
        slot = lax.broadcasted_iota(jnp.int32, cur.shape, 0)
        masked = jnp.where(slot < cnt_ref[s], cur, 0.0).astype(jnp.bfloat16)
        white = jnp.dot(att_ref[s], masked, preferred_element_type=jnp.float32)
        for b in range(blocks):
            out_ref[pl.ds(b * segs * slots + s * slots, slots), :] = white[:, b * width:(b + 1) * width]
    out_ref[pl.ds(blocks * segs * slots, 8), :] = jnp.zeros((8, width), jnp.float32)


def whiten_rows(counts, current, attitude_all, width):
    segs, slots, _ = attitude_all.shape
    rows = current.shape[0] * current.shape[1] // width
    return pl.pallas_call(
        white_kernel,
        in_specs=[pl.BlockSpec(memory_space=pltpu.SMEM)] + [pl.BlockSpec(memory_space=pltpu.VMEM)] * 2,
        out_specs=pl.BlockSpec(memory_space=pltpu.VMEM),
        out_shape=jax.ShapeDtypeStruct((rows + 8, width), jnp.float32),
        cost_estimate=pl.CostEstimate(
            flops=2 * segs * slots * slots * current.shape[1], transcendentals=0,
            bytes_accessed=current.size * 8 + attitude_all.size * 2),
    )(counts, current, attitude_all)


def scatter_sub_kernel(idx_ref, src_ref, cur_ref, out_ref, acc_ref):
    rows, width = src_ref.shape
    streams = acc_ref.shape[0]
    n = cur_ref.shape[0]
    acc_ref[...] = jnp.zeros_like(acc_ref)

    def body(step, carry):
        base = step * streams
        for s in range(streams):
            r = base + s
            i = idx_ref[r]
            acc_ref[s, pl.ds(i, 1), :] = acc_ref[s, pl.ds(i, 1), :] + src_ref[pl.ds(r, 1), :]
        return carry

    lax.fori_loop(0, rows // streams, body, 0, unroll=SUNROLL)
    for b in range(cur_ref.shape[1] // width):
        total = acc_ref[0, pl.ds(b * n, n), :]
        for s in range(1, streams):
            total = total + acc_ref[s, pl.ds(b * n, n), :]
        out_ref[:, b * width:(b + 1) * width] = cur_ref[:, b * width:(b + 1) * width] - total


def scatter_sub(src, idx, current):
    rows, width = src.shape
    blocks = current.shape[1] // width
    return pl.pallas_call(
        scatter_sub_kernel,
        in_specs=[pl.BlockSpec(memory_space=pltpu.SMEM)] + [pl.BlockSpec(memory_space=pltpu.VMEM)] * 2,
        out_specs=pl.BlockSpec(memory_space=pltpu.VMEM),
        out_shape=jax.ShapeDtypeStruct(current.shape, jnp.float32),
        scratch_shapes=[pltpu.VMEM((STREAMS, blocks * current.shape[0] + 8, width), jnp.float32)],
        cost_estimate=pl.CostEstimate(
            flops=rows * width, transcendentals=0, bytes_accessed=(rows * width + 2 * current.size) * 4),
    )(idx, src, current)

def fit_groups(basis, observed, norm_cos, norm_sin, nper):
    corr = jnp.einsum("fio,fic->foc", basis, observed, preferred_element_type=jnp.float32)
    cosine = corr[:, :nper]
    sine = corr[:, nper:]
    amp_c = cosine / norm_cos[:, :, None]
    amp_s = sine / norm_sin[:, :, None]
    power = cosine * amp_c + sine * amp_s
    logits = BETA * power
    highest = jnp.max(logits, axis=1)
    expo = jnp.exp(logits - highest[:, None, :])
    total = jnp.sum(expo, axis=1)
    share = expo / total[:, None, :]
    coeff = jnp.concatenate([share * amp_c, share * amp_s], axis=1).astype(jnp.bfloat16)
    model = jnp.einsum("fio,foc->fic", basis, coeff, preferred_element_type=jnp.float32)
    return (model, highest + jnp.log(total))


def on_device(residuals, seg_counts, attitude, sched_seg, sched_slot, periods):
    tm_count = lax.axis_size("tm")
    sched_dev, obs = sched_seg.shape
    seg_dev, slots, width = residuals.shape
    nper = periods.shape[0]
    column_blocks = width // SRC_GROUP
    capacity = 2 * sched_dev * obs // tm_count
    requests = sched_dev * obs
    seg_flat = sched_seg.reshape(-1)
    slot_flat = sched_slot.reshape(-1)
    block_of = jnp.repeat(jnp.arange(sched_dev, dtype=jnp.int32) % column_blocks, obs)
    target = seg_flat // seg_dev
    local_row = block_of * (seg_dev * slots) + seg_flat % seg_dev * slots + slot_flat
    onehot = (target[:, None] == jnp.arange(tm_count, dtype=jnp.int32)[None, :]).astype(jnp.int32)
    ones = onehot.astype(jnp.bfloat16).reshape(requests // 128, 128, tm_count)
    tril = (jnp.arange(128)[:, None] >= jnp.arange(128)[None, :]).astype(jnp.bfloat16)
    within = jnp.einsum("ij,bjc->bic", tril, ones, preferred_element_type=jnp.float32)
    totals = within[:, -1, :]
    before = jnp.cumsum(totals, axis=0) - totals
    counts = (within + before[:, None, :]).reshape(requests, tm_count)
    position = jnp.sum(counts * onehot.astype(jnp.float32), axis=1).astype(jnp.int32) - 1
    empty_row = seg_dev * slots * column_blocks
    slot_of = target * capacity + position
    pair = (
        jnp.broadcast_to(jnp.array([empty_row, 0], jnp.int32), (tm_count * capacity, 2))
        .at[slot_of]
        .set(jnp.stack([local_row, jnp.arange(requests, dtype=jnp.int32)], axis=1))
    )
    wanted = pair[:, 0].reshape(tm_count, capacity)
    inverse = pair[:, 1]
    asked = lax.all_to_all(wanted, "tm", split_axis=0, concat_axis=0, tiled=True).reshape(-1)
    basis, norm_cos, norm_sin = basis_and_norms(sched_seg * slots + sched_slot, periods)
    valid = jnp.arange(slots, dtype=jnp.int32)[None, :] < seg_counts[:, None]
    inv_cos = (1.0 / norm_cos).reshape(sched_dev, 1, nper)
    inv_sin = (1.0 / norm_sin).reshape(sched_dev, 1, nper)
    current = residuals.astype(jnp.float32).reshape(seg_dev * slots, width)
    evidence = jnp.zeros((sched_dev, SRC_GROUP), jnp.float32)
    attitude_all = lax.all_gather(attitude, "sky", axis=1, tiled=True)
    for iteration in range(ITERS):
        white = whiten_rows(seg_counts, current, attitude_all, SRC_GROUP)
        picked = row_gather(white, asked, jnp.bfloat16, norm_cos)
        outbound = picked.reshape(tm_count, capacity, SRC_GROUP)
        arrived = tm_all_to_all(outbound, jnp.float32, 1 + 2 * iteration)
        model, evidence = fit_fused(
            basis, arrived.reshape(-1, SRC_GROUP), slot_of, inv_cos, inv_sin)
        outgoing = row_gather(model.reshape(requests, SRC_GROUP), inverse, jnp.bfloat16)
        returned = tm_all_to_all(
            outgoing.reshape(tm_count, capacity, SRC_GROUP),
            jnp.float32, 2 + 2 * iteration)
        current = scatter_sub(returned.reshape(-1, SRC_GROUP), asked, current)
    current = current.reshape(seg_dev, slots, width)
    return (current, evidence)


def solution(mesh):
    in_specs = (
        P("tm", None, "sky"),
        P("tm"),
        P("tm", "sky", None),
        P(("tm", "sky"), None),
        P(("tm", "sky"), None),
        P(),
    )
    out_specs = (P("tm", None, "sky"), P(("tm", "sky"), None))
    return jax.shard_map(
        on_device, mesh=mesh, in_specs=in_specs, out_specs=out_specs, check_vma=False
    )
```

```python
import jax
import jax.numpy as jnp
from jax import lax
from jax.experimental import pallas as pl
from jax.experimental.pallas import tpu as pltpu
from jax.sharding import PartitionSpec as P

SRC_GROUP = 128
ITERS = 2


TWO_PI = 6.283185307179586
BETA = 2.0
RIDGE = 1.0


PIO2_1 = 1.5703125
PIO2_2 = 4.837512969970703125e-4
PIO2_3 = 7.549789954891e-8
ROWS = 16
LANES = 512
UNROLL = 2


def basis_kernel(t_ref, p_ref, w_ref, inv_ref, basis_ref, nc_ref, ns_ref):
    obs = t_ref.shape[0]
    nper = p_ref.shape[1]

    def lane_block(j, carry):
        c0 = pl.multiple_of(j * LANES, LANES)
        pf = p_ref[:, pl.ds(c0, LANES)]
        w = w_ref[:, pl.ds(c0, LANES)]
        inv = inv_ref[:, pl.ds(c0, LANES)]

        def row_block(i, acc):
            acc_c, acc_s = acc
            r0 = pl.multiple_of(i * ROWS, ROWS)
            tf = jnp.broadcast_to(t_ref[pl.ds(r0, ROWS), :], (ROWS, LANES))
            q = jnp.floor(tf * inv)
            r = tf - q * pf
            r = jnp.where(r < 0.0, r + pf, r)
            r = jnp.where(r >= pf, r - pf, r)
            phase = r * w
            k = jnp.floor(phase * 0.6366197723675814 + 0.5)
            y = ((phase - k * PIO2_1) - k * PIO2_2) - k * PIO2_3
            z = y * y
            s = y + y * z * (-1.6666654611e-1 + z * (8.3321608736e-3 + z * -1.9515295891e-4))
            c = 1.0 - 0.5 * z + z * z * (4.166664568298827e-2 + z * (-1.388731625493765e-3 + z * 2.443315711809948e-5))
            odd = (k == 1.0) | (k == 3.0)
            cs = jnp.where(odd, s, c)
            sn = jnp.where(odd, c, s)
            cos_v = jnp.where((k == 1.0) | (k == 2.0), -cs, cs).astype(jnp.bfloat16)
            sin_v = jnp.where((k == 2.0) | (k == 3.0), -sn, sn).astype(jnp.bfloat16)
            basis_ref[pl.ds(r0, ROWS), pl.ds(c0, LANES)] = cos_v
            basis_ref[pl.ds(r0, ROWS), pl.ds(nper + c0, LANES)] = sin_v
            cf = cos_v.astype(jnp.float32)
            sf = sin_v.astype(jnp.float32)
            return acc_c + cf * cf, acc_s + sf * sf

        zero = jnp.zeros((ROWS, LANES), jnp.float32)
        acc_c, acc_s = lax.fori_loop(0, obs // ROWS, row_block, (zero, zero), unroll=UNROLL)
        nc_ref[:, pl.ds(c0, LANES)] = jnp.sum(acc_c, axis=0, keepdims=True) + RIDGE
        ns_ref[:, pl.ds(c0, LANES)] = jnp.sum(acc_s, axis=0, keepdims=True) + RIDGE
        return carry

    lax.fori_loop(0, nper // LANES, lane_block, 0)


def basis_and_norms(times, periods):
    plans, obs = times.shape
    nper = periods.shape[0]
    pf = periods.astype(jnp.float32)
    w = (TWO_PI / pf).reshape(1, nper)
    inv = (1.0 / pf).reshape(1, nper)
    pf = pf.reshape(1, nper)
    tf = times.astype(jnp.float32).reshape(plans, obs, 1)
    row = pl.BlockSpec((1, nper), lambda g: (0, 0))
    basis, nc, ns = pl.pallas_call(
        basis_kernel,
        grid=(plans,),
        in_specs=[pl.BlockSpec((None, obs, 1), lambda g: (g, 0, 0)), row, row, row],
        out_specs=[
            pl.BlockSpec((None, obs, 2 * nper), lambda g: (g, 0, 0)),
            pl.BlockSpec((None, 1, nper), lambda g: (g, 0, 0)),
            pl.BlockSpec((None, 1, nper), lambda g: (g, 0, 0)),
        ],
        out_shape=[
            jax.ShapeDtypeStruct((plans, obs, 2 * nper), jnp.bfloat16),
            jax.ShapeDtypeStruct((plans, 1, nper), jnp.float32),
            jax.ShapeDtypeStruct((plans, 1, nper), jnp.float32),
        ],
        cost_estimate=pl.CostEstimate(
            flops=60 * plans * obs * nper, transcendentals=0,
            bytes_accessed=plans * obs * 2 * nper * 2),
    )(tf, pf, w, inv)
    return basis, nc.reshape(plans, nper), ns.reshape(plans, nper)


def gather_kernel(idx_ref, src_ref, *rest):
    out_ref = rest[-2]
    stage_ref = rest[-1]
    block = stage_ref.shape[0]

    def body(b, carry):
        r0 = pl.multiple_of(b * block, block)
        for j in range(block):
            stage_ref[pl.ds(j, 1), :] = src_ref[pl.ds(idx_ref[r0 + j], 1), :]
        out_ref[pl.ds(r0, block), :] = stage_ref[...].astype(out_ref.dtype)
        return carry

    lax.fori_loop(0, out_ref.shape[0] // block, body, 0)


def row_gather(src, idx, out_dtype, *after):
    rows, width = idx.shape[0], src.shape[1]
    return pl.pallas_call(
        gather_kernel,
        in_specs=[pl.BlockSpec(memory_space=pltpu.SMEM), pl.BlockSpec(memory_space=pltpu.VMEM)]
        + [pl.BlockSpec(memory_space=pltpu.VMEM) for _ in after],
        out_specs=pl.BlockSpec(memory_space=pltpu.VMEM),
        out_shape=jax.ShapeDtypeStruct((rows, width), out_dtype),
        scratch_shapes=[pltpu.VMEM((32, width), src.dtype)],
        cost_estimate=pl.CostEstimate(
            flops=0, transcendentals=0, bytes_accessed=2 * rows * width * src.dtype.itemsize),
    )(idx, src, *after)


def with_zero_rows(flat):
    return jnp.concatenate([flat, jnp.zeros((8, flat.shape[1]), flat.dtype)], axis=0)


def a2a_kernel(x_ref, out_ref, held, send_sem, recv_sem, own_sem):
    n = x_ref.shape[0]
    me = lax.axis_index("tm")
    sky = lax.axis_index("sky")
    barrier = pltpu.get_barrier_semaphore()

    def greet(k, carry):
        peer = lax.rem(me + k, n)
        pl.semaphore_signal(barrier, inc=1, device_id=(peer, sky), device_id_type=pl.DeviceIdType.MESH)
        return carry

    lax.fori_loop(1, n, greet, 0)
    pl.semaphore_wait(barrier, n - 1)

    def copy(k):
        peer = lax.rem(me + k, n)
        return pltpu.make_async_remote_copy(
            src_ref=x_ref.at[peer],
            dst_ref=held.at[me],
            send_sem=send_sem.at[k],
            recv_sem=recv_sem.at[k],
            device_id=(peer, sky),
            device_id_type=pl.DeviceIdType.MESH,
        )

    def start(j, carry):
        odd = j % 2
        copy((1 - odd) * (j // 2 + 1) + odd * (n - 1 - j // 2)).start()
        return carry

    lax.fori_loop(0, n - 1, start, 0)
    own = pltpu.make_async_copy(x_ref.at[me], held.at[me], own_sem.at[0])
    own.start()

    def finish(k, carry):
        copy(k).wait()
        return carry

    lax.fori_loop(1, n, finish, 0)
    own.wait()
    out_ref[...] = held[...].astype(out_ref.dtype)


def tm_all_to_all(x, out_dtype, collective_id):
    n, rows, width = x.shape
    return pl.pallas_call(
        a2a_kernel,
        in_specs=[pl.BlockSpec(memory_space=pl.ANY)],
        out_specs=pl.BlockSpec(memory_space=pltpu.VMEM),
        out_shape=jax.ShapeDtypeStruct((n, rows, width), out_dtype),
        scratch_shapes=[
            pltpu.VMEM((n, rows, width), x.dtype),
            pltpu.SemaphoreType.DMA((n,)),
            pltpu.SemaphoreType.DMA((n,)),
            pltpu.SemaphoreType.DMA((1,)),
        ],
        compiler_params=pltpu.CompilerParams(collective_id=collective_id, has_side_effects=True),
    )(x)


STREAMS = 4
SUNROLL = 2

def scatter_add_kernel(idx_ref, src_ref, out_ref, acc_ref):
    rows = src_ref.shape[0]
    streams = acc_ref.shape[0]
    acc_ref[...] = jnp.zeros_like(acc_ref)

    def body(step, carry):
        base = step * streams
        for s in range(streams):
            r = base + s
            i = idx_ref[r]
            acc_ref[s, pl.ds(i, 1), :] = acc_ref[s, pl.ds(i, 1), :] + src_ref[pl.ds(r, 1), :]
        return carry

    lax.fori_loop(0, rows // streams, body, 0, unroll=SUNROLL)
    total = acc_ref[0]
    for s in range(1, streams):
        total = total + acc_ref[s]
    out_ref[...] = total[: out_ref.shape[0]]


def scatter_add(src, idx, out_rows):
    rows, width = src.shape
    pad = out_rows + 8
    return pl.pallas_call(
        scatter_add_kernel,
        in_specs=[pl.BlockSpec(memory_space=pltpu.SMEM), pl.BlockSpec(memory_space=pltpu.VMEM)],
        out_specs=pl.BlockSpec(memory_space=pltpu.VMEM),
        out_shape=jax.ShapeDtypeStruct((out_rows, width), jnp.float32),
        scratch_shapes=[pltpu.VMEM((STREAMS, pad, width), jnp.float32)],
        cost_estimate=pl.CostEstimate(flops=rows * width, transcendentals=0, bytes_accessed=(rows + out_rows) * width * 4),
    )(idx, src)


def fit_kernel(slot_ref, basis_ref, arrived_ref, inc_ref, ins_ref, model_ref, ev_ref, stage_ref):
    nper = inc_ref.shape[1]
    obs = stage_ref.shape[0]
    base = pl.program_id(0) * obs

    def pick(b, carry):
        r0 = pl.multiple_of(b * 32, 32)
        for j in range(32):
            stage_ref[pl.ds(r0 + j, 1), :] = arrived_ref[pl.ds(slot_ref[base + r0 + j], 1), :]
        return carry

    lax.fori_loop(0, obs // 32, pick, 0)
    basis = basis_ref[...]
    obs_t = stage_ref[...].T.astype(jnp.bfloat16)
    corr = jnp.dot(obs_t, basis, preferred_element_type=jnp.float32)
    cosine = corr[:, :nper]
    sine = corr[:, nper:]
    amp_c = cosine * inc_ref[...]
    amp_s = sine * ins_ref[...]
    logits = BETA * (cosine * amp_c + sine * amp_s)
    highest = jnp.max(logits, axis=1, keepdims=True)
    expo = jnp.exp(logits - highest)
    total = jnp.sum(expo, axis=1, keepdims=True)
    share = expo * (1.0 / total)
    coeff = jnp.concatenate([share * amp_c, share * amp_s], axis=1).astype(jnp.bfloat16)
    model_ref[...] = lax.dot_general(
        basis, coeff, (((1,), (1,)), ((), ())), preferred_element_type=jnp.float32)
    ev_ref[...] = highest + jnp.log(total)


def fit_fused(basis, arrived, slot_of, inv_cos, inv_sin):
    plans, obs, width = basis.shape
    cols = arrived.shape[1]
    nper = width // 2
    row = pl.BlockSpec((None, 1, nper), lambda g, s: (g, 0, 0))
    model, ev = pl.pallas_call(
        fit_kernel,
        grid_spec=pltpu.PrefetchScalarGridSpec(
            num_scalar_prefetch=1,
            grid=(plans,),
            in_specs=[
                pl.BlockSpec((None, obs, width), lambda g, s: (g, 0, 0)),
                pl.BlockSpec(arrived.shape, lambda g, s: (0, 0)),
                row,
                row,
            ],
            out_specs=[
                pl.BlockSpec((None, obs, cols), lambda g, s: (g, 0, 0)),
                pl.BlockSpec((None, cols, 1), lambda g, s: (g, 0, 0)),
            ],
            scratch_shapes=[pltpu.VMEM((obs, cols), jnp.float32)],
        ),
        out_shape=[
            jax.ShapeDtypeStruct((plans, obs, cols), jnp.float32),
            jax.ShapeDtypeStruct((plans, cols, 1), jnp.float32),
        ],
        cost_estimate=pl.CostEstimate(
            flops=4 * plans * obs * width * cols, transcendentals=plans * nper * cols,
            bytes_accessed=plans * obs * width * 2),
    )(slot_of, basis, arrived, inv_cos, inv_sin)
    return model, ev.reshape(plans, cols)


def white_kernel(cnt_ref, cur_ref, att_ref, out_ref):
    segs, slots, _ = att_ref.shape
    width = out_ref.shape[1]
    blocks = cur_ref.shape[1] // width
    for s in range(segs):
        cur = cur_ref[pl.ds(s * slots, slots), :]
        slot = lax.broadcasted_iota(jnp.int32, cur.shape, 0)
        masked = jnp.where(slot < cnt_ref[s], cur, 0.0).astype(jnp.bfloat16)
        white = jnp.dot(att_ref[s], masked, preferred_element_type=jnp.float32)
        for b in range(blocks):
            out_ref[pl.ds(b * segs * slots + s * slots, slots), :] = white[:, b * width:(b + 1) * width]
    out_ref[pl.ds(blocks * segs * slots, 8), :] = jnp.zeros((8, width), jnp.float32)


def whiten_rows(counts, current, attitude_all, width):
    segs, slots, _ = attitude_all.shape
    rows = current.shape[0] * current.shape[1] // width
    return pl.pallas_call(
        white_kernel,
        in_specs=[pl.BlockSpec(memory_space=pltpu.SMEM)] + [pl.BlockSpec(memory_space=pltpu.VMEM)] * 2,
        out_specs=pl.BlockSpec(memory_space=pltpu.VMEM),
        out_shape=jax.ShapeDtypeStruct((rows + 8, width), jnp.float32),
        cost_estimate=pl.CostEstimate(
            flops=2 * segs * slots * slots * current.shape[1], transcendentals=0,
            bytes_accessed=current.size * 8 + attitude_all.size * 2),
    )(counts, current, attitude_all)


def scatter_sub_kernel(idx_ref, src_hbm, cur_hbm, out_ref, acc_ref, src_ref, cur_ref, sems):
    rows, width = src_ref.shape
    streams = acc_ref.shape[0]
    n = cur_ref.shape[0]
    src_copy = pltpu.make_async_copy(src_hbm, src_ref, sems.at[0])
    cur_copy = pltpu.make_async_copy(cur_hbm, cur_ref, sems.at[1])
    src_copy.start()
    cur_copy.start()
    acc_ref[...] = jnp.zeros_like(acc_ref)
    src_copy.wait()

    def body(step, carry):
        base = step * streams
        for s in range(streams):
            r = base + s
            i = idx_ref[r]
            acc_ref[s, pl.ds(i, 1), :] = acc_ref[s, pl.ds(i, 1), :] + src_ref[pl.ds(r, 1), :]
        return carry

    lax.fori_loop(0, rows // streams, body, 0, unroll=SUNROLL)
    cur_copy.wait()
    for b in range(cur_ref.shape[1] // width):
        total = acc_ref[0, pl.ds(b * n, n), :]
        for s in range(1, streams):
            total = total + acc_ref[s, pl.ds(b * n, n), :]
        out_ref[:, b * width:(b + 1) * width] = cur_ref[:, b * width:(b + 1) * width] - total


def scatter_sub(src, idx, current):
    rows, width = src.shape
    blocks = current.shape[1] // width
    return pl.pallas_call(
        scatter_sub_kernel,
        in_specs=[pl.BlockSpec(memory_space=pltpu.SMEM)] + [pl.BlockSpec(memory_space=pl.ANY)] * 2,
        out_specs=pl.BlockSpec(memory_space=pltpu.VMEM),
        out_shape=jax.ShapeDtypeStruct(current.shape, jnp.float32),
        scratch_shapes=[
            pltpu.VMEM((STREAMS, blocks * current.shape[0] + 8, width), jnp.float32),
            pltpu.VMEM(src.shape, src.dtype),
            pltpu.VMEM(current.shape, current.dtype),
            pltpu.SemaphoreType.DMA((2,)),
        ],
        cost_estimate=pl.CostEstimate(
            flops=rows * width, transcendentals=0, bytes_accessed=(rows * width + 2 * current.size) * 4),
    )(idx, src, current)

def fit_groups(basis, observed, norm_cos, norm_sin, nper):
    corr = jnp.einsum("fio,fic->foc", basis, observed, preferred_element_type=jnp.float32)
    cosine = corr[:, :nper]
    sine = corr[:, nper:]
    amp_c = cosine / norm_cos[:, :, None]
    amp_s = sine / norm_sin[:, :, None]
    power = cosine * amp_c + sine * amp_s
    logits = BETA * power
    highest = jnp.max(logits, axis=1)
    expo = jnp.exp(logits - highest[:, None, :])
    total = jnp.sum(expo, axis=1)
    share = expo / total[:, None, :]
    coeff = jnp.concatenate([share * amp_c, share * amp_s], axis=1).astype(jnp.bfloat16)
    model = jnp.einsum("fio,foc->fic", basis, coeff, preferred_element_type=jnp.float32)
    return (model, highest + jnp.log(total))


def on_device(residuals, seg_counts, attitude, sched_seg, sched_slot, periods):
    tm_count = lax.axis_size("tm")
    sched_dev, obs = sched_seg.shape
    seg_dev, slots, width = residuals.shape
    nper = periods.shape[0]
    column_blocks = width // SRC_GROUP
    capacity = 2 * sched_dev * obs // tm_count
    requests = sched_dev * obs
    seg_flat = sched_seg.reshape(-1)
    slot_flat = sched_slot.reshape(-1)
    block_of = jnp.repeat(jnp.arange(sched_dev, dtype=jnp.int32) % column_blocks, obs)
    target = seg_flat // seg_dev
    local_row = block_of * (seg_dev * slots) + seg_flat % seg_dev * slots + slot_flat
    onehot = (target[:, None] == jnp.arange(tm_count, dtype=jnp.int32)[None, :]).astype(jnp.int32)
    ones = onehot.astype(jnp.bfloat16).reshape(requests // 128, 128, tm_count)
    tril = (jnp.arange(128)[:, None] >= jnp.arange(128)[None, :]).astype(jnp.bfloat16)
    within = jnp.einsum("ij,bjc->bic", tril, ones, preferred_element_type=jnp.float32)
    totals = within[:, -1, :]
    before = jnp.cumsum(totals, axis=0) - totals
    counts = (within + before[:, None, :]).reshape(requests, tm_count)
    position = jnp.sum(counts * onehot.astype(jnp.float32), axis=1).astype(jnp.int32) - 1
    empty_row = seg_dev * slots * column_blocks
    slot_of = target * capacity + position
    pair = (
        jnp.broadcast_to(jnp.array([empty_row, 0], jnp.int32), (tm_count * capacity, 2))
        .at[slot_of]
        .set(jnp.stack([local_row, jnp.arange(requests, dtype=jnp.int32)], axis=1))
    )
    wanted = pair[:, 0].reshape(tm_count, capacity)
    inverse = pair[:, 1]
    asked = lax.all_to_all(wanted, "tm", split_axis=0, concat_axis=0, tiled=True).reshape(-1)
    basis, norm_cos, norm_sin = basis_and_norms(sched_seg * slots + sched_slot, periods)
    valid = jnp.arange(slots, dtype=jnp.int32)[None, :] < seg_counts[:, None]
    inv_cos = (1.0 / norm_cos).reshape(sched_dev, 1, nper)
    inv_sin = (1.0 / norm_sin).reshape(sched_dev, 1, nper)
    current = residuals.astype(jnp.float32).reshape(seg_dev * slots, width)
    evidence = jnp.zeros((sched_dev, SRC_GROUP), jnp.float32)
    attitude_all = lax.all_gather(attitude, "sky", axis=1, tiled=True)
    for iteration in range(ITERS):
        white = whiten_rows(seg_counts, current, attitude_all, SRC_GROUP)
        picked = row_gather(white, asked, jnp.bfloat16, norm_cos)
        outbound = picked.reshape(tm_count, capacity, SRC_GROUP)
        arrived = tm_all_to_all(outbound, jnp.float32, 1 + 2 * iteration)
        model, evidence = fit_fused(
            basis, arrived.reshape(-1, SRC_GROUP), slot_of, inv_cos, inv_sin)
        outgoing = row_gather(model.reshape(requests, SRC_GROUP), inverse, jnp.bfloat16)
        returned = tm_all_to_all(
            outgoing.reshape(tm_count, capacity, SRC_GROUP),
            jnp.float32, 2 + 2 * iteration)
        current = scatter_sub(returned.reshape(-1, SRC_GROUP), asked, current)
    current = current.reshape(seg_dev, slots, width)
    return (current, evidence)


def solution(mesh):
    in_specs = (
        P("tm", None, "sky"),
        P("tm"),
        P("tm", "sky", None),
        P(("tm", "sky"), None),
        P(("tm", "sky"), None),
        P(),
    )
    out_specs = (P("tm", None, "sky"), P(("tm", "sky"), None))
    return jax.shard_map(
        on_device, mesh=mesh, in_specs=in_specs, out_specs=out_specs, check_vma=False
    )
```

```python
import jax
import jax.numpy as jnp
from jax import lax
from jax.experimental import pallas as pl
from jax.experimental.pallas import tpu as pltpu
from jax.sharding import PartitionSpec as P

SRC_GROUP = 128
ITERS = 2


TWO_PI = 6.283185307179586
BETA = 2.0
RIDGE = 1.0


PIO2_1 = 1.5703125
PIO2_2 = 4.837512969970703125e-4
PIO2_3 = 7.549789954891e-8
ROWS = 16
LANES = 512
UNROLL = 2


def basis_kernel(t_ref, p_ref, w_ref, inv_ref, basis_ref, nc_ref, ns_ref):
    obs = t_ref.shape[0]
    nper = p_ref.shape[1]

    def lane_block(j, carry):
        c0 = pl.multiple_of(j * LANES, LANES)
        pf = p_ref[:, pl.ds(c0, LANES)]
        w = w_ref[:, pl.ds(c0, LANES)]
        inv = inv_ref[:, pl.ds(c0, LANES)]

        def row_block(i, acc):
            acc_c, acc_s = acc
            r0 = pl.multiple_of(i * ROWS, ROWS)
            tf = jnp.broadcast_to(t_ref[pl.ds(r0, ROWS), :], (ROWS, LANES))
            q = jnp.floor(tf * inv)
            r = tf - q * pf
            r = jnp.where(r < 0.0, r + pf, r)
            r = jnp.where(r >= pf, r - pf, r)
            phase = r * w
            k = jnp.floor(phase * 0.6366197723675814 + 0.5)
            y = ((phase - k * PIO2_1) - k * PIO2_2) - k * PIO2_3
            z = y * y
            s = y + y * z * (-1.6666654611e-1 + z * (8.3321608736e-3 + z * -1.9515295891e-4))
            c = 1.0 - 0.5 * z + z * z * (4.166664568298827e-2 + z * (-1.388731625493765e-3 + z * 2.443315711809948e-5))
            odd = (k == 1.0) | (k == 3.0)
            cs = jnp.where(odd, s, c)
            sn = jnp.where(odd, c, s)
            cos_v = jnp.where((k == 1.0) | (k == 2.0), -cs, cs).astype(jnp.bfloat16)
            sin_v = jnp.where((k == 2.0) | (k == 3.0), -sn, sn).astype(jnp.bfloat16)
            basis_ref[pl.ds(r0, ROWS), pl.ds(c0, LANES)] = cos_v
            basis_ref[pl.ds(r0, ROWS), pl.ds(nper + c0, LANES)] = sin_v
            cf = cos_v.astype(jnp.float32)
            sf = sin_v.astype(jnp.float32)
            return acc_c + cf * cf, acc_s + sf * sf

        zero = jnp.zeros((ROWS, LANES), jnp.float32)
        acc_c, acc_s = lax.fori_loop(0, obs // ROWS, row_block, (zero, zero), unroll=UNROLL)
        nc_ref[:, pl.ds(c0, LANES)] = jnp.sum(acc_c, axis=0, keepdims=True) + RIDGE
        ns_ref[:, pl.ds(c0, LANES)] = jnp.sum(acc_s, axis=0, keepdims=True) + RIDGE
        return carry

    lax.fori_loop(0, nper // LANES, lane_block, 0)


def basis_and_norms(times, periods):
    plans, obs = times.shape
    nper = periods.shape[0]
    pf = periods.astype(jnp.float32)
    w = (TWO_PI / pf).reshape(1, nper)
    inv = (1.0 / pf).reshape(1, nper)
    pf = pf.reshape(1, nper)
    tf = times.astype(jnp.float32).reshape(plans, obs, 1)
    row = pl.BlockSpec((1, nper), lambda g: (0, 0))
    basis, nc, ns = pl.pallas_call(
        basis_kernel,
        grid=(plans,),
        in_specs=[pl.BlockSpec((None, obs, 1), lambda g: (g, 0, 0)), row, row, row],
        out_specs=[
            pl.BlockSpec((None, obs, 2 * nper), lambda g: (g, 0, 0)),
            pl.BlockSpec((None, 1, nper), lambda g: (g, 0, 0)),
            pl.BlockSpec((None, 1, nper), lambda g: (g, 0, 0)),
        ],
        out_shape=[
            jax.ShapeDtypeStruct((plans, obs, 2 * nper), jnp.bfloat16),
            jax.ShapeDtypeStruct((plans, 1, nper), jnp.float32),
            jax.ShapeDtypeStruct((plans, 1, nper), jnp.float32),
        ],
        cost_estimate=pl.CostEstimate(
            flops=60 * plans * obs * nper, transcendentals=0,
            bytes_accessed=plans * obs * 2 * nper * 2),
    )(tf, pf, w, inv)
    return basis, nc.reshape(plans, nper), ns.reshape(plans, nper)


def gather_kernel(idx_ref, src_ref, *rest):
    out_ref = rest[-2]
    stage_ref = rest[-1]
    block = stage_ref.shape[0]

    def body(b, carry):
        r0 = pl.multiple_of(b * block, block)
        for j in range(block):
            stage_ref[pl.ds(j, 1), :] = src_ref[pl.ds(idx_ref[r0 + j], 1), :]
        out_ref[pl.ds(r0, block), :] = stage_ref[...].astype(out_ref.dtype)
        return carry

    lax.fori_loop(0, out_ref.shape[0] // block, body, 0)


def row_gather(src, idx, out_dtype, *after):
    rows, width = idx.shape[0], src.shape[1]
    return pl.pallas_call(
        gather_kernel,
        in_specs=[pl.BlockSpec(memory_space=pltpu.SMEM), pl.BlockSpec(memory_space=pltpu.VMEM)]
        + [pl.BlockSpec(memory_space=pltpu.VMEM) for _ in after],
        out_specs=pl.BlockSpec(memory_space=pltpu.VMEM),
        out_shape=jax.ShapeDtypeStruct((rows, width), out_dtype),
        scratch_shapes=[pltpu.VMEM((32, width), src.dtype)],
        cost_estimate=pl.CostEstimate(
            flops=0, transcendentals=0, bytes_accessed=2 * rows * width * src.dtype.itemsize),
    )(idx, src, *after)


def with_zero_rows(flat):
    return jnp.concatenate([flat, jnp.zeros((8, flat.shape[1]), flat.dtype)], axis=0)


def a2a_kernel(x_ref, out_ref, held, send_sem, recv_sem, own_sem):
    n = x_ref.shape[0]
    me = lax.axis_index("tm")
    sky = lax.axis_index("sky")
    barrier = pltpu.get_barrier_semaphore()

    def greet(k, carry):
        peer = lax.rem(me + k, n)
        pl.semaphore_signal(barrier, inc=1, device_id=(peer, sky), device_id_type=pl.DeviceIdType.MESH)
        return carry

    lax.fori_loop(1, n, greet, 0)
    pl.semaphore_wait(barrier, n - 1)

    def copy(k):
        peer = lax.rem(me + k, n)
        return pltpu.make_async_remote_copy(
            src_ref=x_ref.at[peer],
            dst_ref=held.at[me],
            send_sem=send_sem.at[k],
            recv_sem=recv_sem.at[k],
            device_id=(peer, sky),
            device_id_type=pl.DeviceIdType.MESH,
        )

    def start(j, carry):
        odd = j % 2
        copy((1 - odd) * (j // 2 + 1) + odd * (n - 1 - j // 2)).start()
        return carry

    lax.fori_loop(0, n - 1, start, 0)
    own = pltpu.make_async_copy(x_ref.at[me], held.at[me], own_sem.at[0])
    own.start()

    def finish(k, carry):
        copy(k).wait()
        return carry

    lax.fori_loop(1, n, finish, 0)
    own.wait()
    out_ref[...] = held[...].astype(out_ref.dtype)


def tm_all_to_all(x, out_dtype, collective_id):
    n, rows, width = x.shape
    return pl.pallas_call(
        a2a_kernel,
        in_specs=[pl.BlockSpec(memory_space=pl.ANY)],
        out_specs=pl.BlockSpec(memory_space=pltpu.VMEM),
        out_shape=jax.ShapeDtypeStruct((n, rows, width), out_dtype),
        scratch_shapes=[
            pltpu.VMEM((n, rows, width), x.dtype),
            pltpu.SemaphoreType.DMA((n,)),
            pltpu.SemaphoreType.DMA((n,)),
            pltpu.SemaphoreType.DMA((1,)),
        ],
        compiler_params=pltpu.CompilerParams(collective_id=collective_id, has_side_effects=True),
    )(x)


STREAMS = 4
SUNROLL = 2

def scatter_add_kernel(idx_ref, src_ref, out_ref, acc_ref):
    rows = src_ref.shape[0]
    streams = acc_ref.shape[0]
    acc_ref[...] = jnp.zeros_like(acc_ref)

    def body(step, carry):
        base = step * streams
        for s in range(streams):
            r = base + s
            i = idx_ref[r]
            acc_ref[s, pl.ds(i, 1), :] = acc_ref[s, pl.ds(i, 1), :] + src_ref[pl.ds(r, 1), :]
        return carry

    lax.fori_loop(0, rows // streams, body, 0, unroll=SUNROLL)
    total = acc_ref[0]
    for s in range(1, streams):
        total = total + acc_ref[s]
    out_ref[...] = total[: out_ref.shape[0]]


def scatter_add(src, idx, out_rows):
    rows, width = src.shape
    pad = out_rows + 8
    return pl.pallas_call(
        scatter_add_kernel,
        in_specs=[pl.BlockSpec(memory_space=pltpu.SMEM), pl.BlockSpec(memory_space=pltpu.VMEM)],
        out_specs=pl.BlockSpec(memory_space=pltpu.VMEM),
        out_shape=jax.ShapeDtypeStruct((out_rows, width), jnp.float32),
        scratch_shapes=[pltpu.VMEM((STREAMS, pad, width), jnp.float32)],
        cost_estimate=pl.CostEstimate(flops=rows * width, transcendentals=0, bytes_accessed=(rows + out_rows) * width * 4),
    )(idx, src)


def fit_kernel(slot_ref, basis_ref, arrived_in, inc_ref, ins_ref, model_ref, ev_ref, stage_ref, arrived_ref):
    nper = inc_ref.shape[1]
    obs = stage_ref.shape[0]
    base = pl.program_id(0) * obs

    @pl.when(pl.program_id(0) == 0)
    def _():
        arrived_ref[...] = arrived_in[...].astype(jnp.float32)

    def pick(b, carry):
        r0 = pl.multiple_of(b * 32, 32)
        for j in range(32):
            stage_ref[pl.ds(r0 + j, 1), :] = arrived_ref[pl.ds(slot_ref[base + r0 + j], 1), :]
        return carry

    lax.fori_loop(0, obs // 32, pick, 0)
    basis = basis_ref[...]
    obs_t = stage_ref[...].T.astype(jnp.bfloat16)
    corr = jnp.dot(obs_t, basis, preferred_element_type=jnp.float32)
    cosine = corr[:, :nper]
    sine = corr[:, nper:]
    amp_c = cosine * inc_ref[...]
    amp_s = sine * ins_ref[...]
    logits = BETA * (cosine * amp_c + sine * amp_s)
    highest = jnp.max(logits, axis=1, keepdims=True)
    expo = jnp.exp(logits - highest)
    total = jnp.sum(expo, axis=1, keepdims=True)
    share = expo * (1.0 / total)
    coeff = jnp.concatenate([share * amp_c, share * amp_s], axis=1).astype(jnp.bfloat16)
    model_ref[...] = lax.dot_general(
        basis, coeff, (((1,), (1,)), ((), ())), preferred_element_type=jnp.float32)
    ev_ref[...] = highest + jnp.log(total)


def fit_fused(basis, arrived, slot_of, inv_cos, inv_sin):
    plans, obs, width = basis.shape
    cols = arrived.shape[1]
    nper = width // 2
    row = pl.BlockSpec((None, 1, nper), lambda g, s: (g, 0, 0))
    model, ev = pl.pallas_call(
        fit_kernel,
        grid_spec=pltpu.PrefetchScalarGridSpec(
            num_scalar_prefetch=1,
            grid=(plans,),
            in_specs=[
                pl.BlockSpec((None, obs, width), lambda g, s: (g, 0, 0)),
                pl.BlockSpec(arrived.shape, lambda g, s: (0, 0)),
                row,
                row,
            ],
            out_specs=[
                pl.BlockSpec((None, obs, cols), lambda g, s: (g, 0, 0)),
                pl.BlockSpec((None, cols, 1), lambda g, s: (g, 0, 0)),
            ],
            scratch_shapes=[pltpu.VMEM((obs, cols), jnp.float32), pltpu.VMEM(arrived.shape, jnp.float32)],
        ),
        out_shape=[
            jax.ShapeDtypeStruct((plans, obs, cols), jnp.float32),
            jax.ShapeDtypeStruct((plans, cols, 1), jnp.float32),
        ],
        cost_estimate=pl.CostEstimate(
            flops=4 * plans * obs * width * cols, transcendentals=plans * nper * cols,
            bytes_accessed=plans * obs * width * 2),
    )(slot_of, basis, arrived, inv_cos, inv_sin)
    return model, ev.reshape(plans, cols)


def white_kernel(cnt_ref, cur_ref, att_ref, out_ref):
    segs, slots, _ = att_ref.shape
    width = out_ref.shape[1]
    blocks = cur_ref.shape[1] // width
    for s in range(segs):
        cur = cur_ref[pl.ds(s * slots, slots), :]
        slot = lax.broadcasted_iota(jnp.int32, cur.shape, 0)
        masked = jnp.where(slot < cnt_ref[s], cur, 0.0).astype(jnp.bfloat16)
        white = jnp.dot(att_ref[s], masked, preferred_element_type=jnp.float32)
        for b in range(blocks):
            out_ref[pl.ds(b * segs * slots + s * slots, slots), :] = white[:, b * width:(b + 1) * width]
    out_ref[pl.ds(blocks * segs * slots, 8), :] = jnp.zeros((8, width), jnp.float32)


def whiten_rows(counts, current, attitude_all, width):
    segs, slots, _ = attitude_all.shape
    rows = current.shape[0] * current.shape[1] // width
    return pl.pallas_call(
        white_kernel,
        in_specs=[pl.BlockSpec(memory_space=pltpu.SMEM)] + [pl.BlockSpec(memory_space=pltpu.VMEM)] * 2,
        out_specs=pl.BlockSpec(memory_space=pltpu.VMEM),
        out_shape=jax.ShapeDtypeStruct((rows + 8, width), jnp.float32),
        cost_estimate=pl.CostEstimate(
            flops=2 * segs * slots * slots * current.shape[1], transcendentals=0,
            bytes_accessed=current.size * 8 + attitude_all.size * 2),
    )(counts, current, attitude_all)


def scatter_sub_kernel(idx_ref, src_in, cur_ref, out_ref, acc_ref, src_ref):
    rows, width = src_ref.shape
    streams = acc_ref.shape[0]
    n = cur_ref.shape[0]
    src_ref[...] = src_in[...].astype(jnp.float32)
    acc_ref[...] = jnp.zeros_like(acc_ref)

    def body(step, carry):
        base = step * streams
        for s in range(streams):
            r = base + s
            i = idx_ref[r]
            acc_ref[s, pl.ds(i, 1), :] = acc_ref[s, pl.ds(i, 1), :] + src_ref[pl.ds(r, 1), :]
        return carry

    lax.fori_loop(0, rows // streams, body, 0, unroll=SUNROLL)
    for b in range(cur_ref.shape[1] // width):
        total = acc_ref[0, pl.ds(b * n, n), :]
        for s in range(1, streams):
            total = total + acc_ref[s, pl.ds(b * n, n), :]
        out_ref[:, b * width:(b + 1) * width] = cur_ref[:, b * width:(b + 1) * width] - total


def scatter_sub(src, idx, current):
    rows, width = src.shape
    blocks = current.shape[1] // width
    return pl.pallas_call(
        scatter_sub_kernel,
        in_specs=[pl.BlockSpec(memory_space=pltpu.SMEM)] + [pl.BlockSpec(memory_space=pltpu.VMEM)] * 2,
        out_specs=pl.BlockSpec(memory_space=pltpu.VMEM),
        out_shape=jax.ShapeDtypeStruct(current.shape, jnp.float32),
        scratch_shapes=[pltpu.VMEM((STREAMS, blocks * current.shape[0] + 8, width), jnp.float32),
                        pltpu.VMEM(src.shape, jnp.float32)],
        cost_estimate=pl.CostEstimate(
            flops=rows * width, transcendentals=0, bytes_accessed=(rows * width + 2 * current.size) * 4),
    )(idx, src, current)

def fit_groups(basis, observed, norm_cos, norm_sin, nper):
    corr = jnp.einsum("fio,fic->foc", basis, observed, preferred_element_type=jnp.float32)
    cosine = corr[:, :nper]
    sine = corr[:, nper:]
    amp_c = cosine / norm_cos[:, :, None]
    amp_s = sine / norm_sin[:, :, None]
    power = cosine * amp_c + sine * amp_s
    logits = BETA * power
    highest = jnp.max(logits, axis=1)
    expo = jnp.exp(logits - highest[:, None, :])
    total = jnp.sum(expo, axis=1)
    share = expo / total[:, None, :]
    coeff = jnp.concatenate([share * amp_c, share * amp_s], axis=1).astype(jnp.bfloat16)
    model = jnp.einsum("fio,foc->fic", basis, coeff, preferred_element_type=jnp.float32)
    return (model, highest + jnp.log(total))


def on_device(residuals, seg_counts, attitude, sched_seg, sched_slot, periods):
    tm_count = lax.axis_size("tm")
    sched_dev, obs = sched_seg.shape
    seg_dev, slots, width = residuals.shape
    nper = periods.shape[0]
    column_blocks = width // SRC_GROUP
    capacity = 2 * sched_dev * obs // tm_count
    requests = sched_dev * obs
    seg_flat = sched_seg.reshape(-1)
    slot_flat = sched_slot.reshape(-1)
    block_of = jnp.repeat(jnp.arange(sched_dev, dtype=jnp.int32) % column_blocks, obs)
    target = seg_flat // seg_dev
    local_row = block_of * (seg_dev * slots) + seg_flat % seg_dev * slots + slot_flat
    onehot = (target[:, None] == jnp.arange(tm_count, dtype=jnp.int32)[None, :]).astype(jnp.int32)
    ones = onehot.astype(jnp.bfloat16).reshape(requests // 128, 128, tm_count)
    tril = (jnp.arange(128)[:, None] >= jnp.arange(128)[None, :]).astype(jnp.bfloat16)
    within = jnp.einsum("ij,bjc->bic", tril, ones, preferred_element_type=jnp.float32)
    totals = within[:, -1, :]
    before = jnp.cumsum(totals, axis=0) - totals
    counts = (within + before[:, None, :]).reshape(requests, tm_count)
    position = jnp.sum(counts * onehot.astype(jnp.float32), axis=1).astype(jnp.int32) - 1
    empty_row = seg_dev * slots * column_blocks
    slot_of = target * capacity + position
    pair = (
        jnp.broadcast_to(jnp.array([empty_row, 0], jnp.int32), (tm_count * capacity, 2))
        .at[slot_of]
        .set(jnp.stack([local_row, jnp.arange(requests, dtype=jnp.int32)], axis=1))
    )
    wanted = pair[:, 0].reshape(tm_count, capacity)
    inverse = pair[:, 1]
    asked = lax.all_to_all(wanted, "tm", split_axis=0, concat_axis=0, tiled=True).reshape(-1)
    basis, norm_cos, norm_sin = basis_and_norms(sched_seg * slots + sched_slot, periods)
    valid = jnp.arange(slots, dtype=jnp.int32)[None, :] < seg_counts[:, None]
    inv_cos = (1.0 / norm_cos).reshape(sched_dev, 1, nper)
    inv_sin = (1.0 / norm_sin).reshape(sched_dev, 1, nper)
    current = residuals.astype(jnp.float32).reshape(seg_dev * slots, width)
    evidence = jnp.zeros((sched_dev, SRC_GROUP), jnp.float32)
    attitude_all = lax.all_gather(attitude, "sky", axis=1, tiled=True)
    for iteration in range(ITERS):
        white = whiten_rows(seg_counts, current, attitude_all, SRC_GROUP)
        picked = row_gather(white, asked, jnp.bfloat16, norm_cos)
        outbound = picked.reshape(tm_count, capacity, SRC_GROUP)
        arrived = tm_all_to_all(outbound, jnp.bfloat16, 1 + 2 * iteration)
        model, evidence = fit_fused(
            basis, arrived.reshape(-1, SRC_GROUP), slot_of, inv_cos, inv_sin)
        outgoing = row_gather(model.reshape(requests, SRC_GROUP), inverse, jnp.bfloat16)
        returned = tm_all_to_all(
            outgoing.reshape(tm_count, capacity, SRC_GROUP),
            jnp.bfloat16, 2 + 2 * iteration)
        current = scatter_sub(returned.reshape(-1, SRC_GROUP), asked, current)
    current = current.reshape(seg_dev, slots, width)
    return (current, evidence)


def solution(mesh):
    in_specs = (
        P("tm", None, "sky"),
        P("tm"),
        P("tm", "sky", None),
        P(("tm", "sky"), None),
        P(("tm", "sky"), None),
        P(),
    )
    out_specs = (P("tm", None, "sky"), P(("tm", "sky"), None))
    return jax.shard_map(
        on_device, mesh=mesh, in_specs=in_specs, out_specs=out_specs, check_vma=False
    )
```

```python
import jax
import jax.numpy as jnp
from jax import lax
from jax.experimental import pallas as pl
from jax.experimental.pallas import tpu as pltpu
from jax.sharding import PartitionSpec as P

SRC_GROUP = 128
ITERS = 2


TWO_PI = 6.283185307179586
BETA = 2.0
RIDGE = 1.0


PIO2_1 = 1.5703125
PIO2_2 = 4.837512969970703125e-4
PIO2_3 = 7.549789954891e-8
ROWS = 16
LANES = 512
UNROLL = 2


def basis_kernel(t_ref, p_ref, w_ref, inv_ref, basis_ref, nc_ref, ns_ref):
    obs = t_ref.shape[0]
    nper = p_ref.shape[1]

    def lane_block(j, carry):
        c0 = pl.multiple_of(j * LANES, LANES)
        pf = p_ref[:, pl.ds(c0, LANES)]
        w = w_ref[:, pl.ds(c0, LANES)]
        inv = inv_ref[:, pl.ds(c0, LANES)]

        def row_block(i, acc):
            acc_c, acc_s = acc
            r0 = pl.multiple_of(i * ROWS, ROWS)
            tf = jnp.broadcast_to(t_ref[pl.ds(r0, ROWS), :], (ROWS, LANES))
            q = jnp.floor(tf * inv)
            r = tf - q * pf
            r = jnp.where(r < 0.0, r + pf, r)
            r = jnp.where(r >= pf, r - pf, r)
            phase = r * w
            k = jnp.floor(phase * 0.6366197723675814 + 0.5)
            y = ((phase - k * PIO2_1) - k * PIO2_2) - k * PIO2_3
            z = y * y
            s = y + y * z * (-1.6666654611e-1 + z * (8.3321608736e-3 + z * -1.9515295891e-4))
            c = 1.0 - 0.5 * z + z * z * (4.166664568298827e-2 + z * (-1.388731625493765e-3 + z * 2.443315711809948e-5))
            odd = (k == 1.0) | (k == 3.0)
            cs = jnp.where(odd, s, c)
            sn = jnp.where(odd, c, s)
            cos_v = jnp.where((k == 1.0) | (k == 2.0), -cs, cs).astype(jnp.bfloat16)
            sin_v = jnp.where((k == 2.0) | (k == 3.0), -sn, sn).astype(jnp.bfloat16)
            basis_ref[pl.ds(r0, ROWS), pl.ds(c0, LANES)] = cos_v
            basis_ref[pl.ds(r0, ROWS), pl.ds(nper + c0, LANES)] = sin_v
            cf = cos_v.astype(jnp.float32)
            sf = sin_v.astype(jnp.float32)
            return acc_c + cf * cf, acc_s + sf * sf

        zero = jnp.zeros((ROWS, LANES), jnp.float32)
        acc_c, acc_s = lax.fori_loop(0, obs // ROWS, row_block, (zero, zero), unroll=UNROLL)
        nc_ref[:, pl.ds(c0, LANES)] = jnp.sum(acc_c, axis=0, keepdims=True) + RIDGE
        ns_ref[:, pl.ds(c0, LANES)] = jnp.sum(acc_s, axis=0, keepdims=True) + RIDGE
        return carry

    lax.fori_loop(0, nper // LANES, lane_block, 0)


def basis_and_norms(times, periods):
    plans, obs = times.shape
    nper = periods.shape[0]
    pf = periods.astype(jnp.float32)
    w = (TWO_PI / pf).reshape(1, nper)
    inv = (1.0 / pf).reshape(1, nper)
    pf = pf.reshape(1, nper)
    tf = times.astype(jnp.float32).reshape(plans, obs, 1)
    row = pl.BlockSpec((1, nper), lambda g: (0, 0))
    basis, nc, ns = pl.pallas_call(
        basis_kernel,
        grid=(plans,),
        in_specs=[pl.BlockSpec((None, obs, 1), lambda g: (g, 0, 0)), row, row, row],
        out_specs=[
            pl.BlockSpec((None, obs, 2 * nper), lambda g: (g, 0, 0)),
            pl.BlockSpec((None, 1, nper), lambda g: (g, 0, 0)),
            pl.BlockSpec((None, 1, nper), lambda g: (g, 0, 0)),
        ],
        out_shape=[
            jax.ShapeDtypeStruct((plans, obs, 2 * nper), jnp.bfloat16),
            jax.ShapeDtypeStruct((plans, 1, nper), jnp.float32),
            jax.ShapeDtypeStruct((plans, 1, nper), jnp.float32),
        ],
        cost_estimate=pl.CostEstimate(
            flops=60 * plans * obs * nper, transcendentals=0,
            bytes_accessed=plans * obs * 2 * nper * 2),
    )(tf, pf, w, inv)
    return basis, nc.reshape(plans, nper), ns.reshape(plans, nper)


def gather_kernel(idx_ref, src_ref, *rest):
    out_ref = rest[-2]
    stage_ref = rest[-1]
    block = stage_ref.shape[0]

    def body(b, carry):
        r0 = pl.multiple_of(b * block, block)
        for j in range(block):
            stage_ref[pl.ds(j, 1), :] = src_ref[pl.ds(idx_ref[r0 + j], 1), :]
        out_ref[pl.ds(r0, block), :] = stage_ref[...].astype(out_ref.dtype)
        return carry

    lax.fori_loop(0, out_ref.shape[0] // block, body, 0)


def row_gather(src, idx, out_dtype, *after):
    rows, width = idx.shape[0], src.shape[1]
    return pl.pallas_call(
        gather_kernel,
        in_specs=[pl.BlockSpec(memory_space=pltpu.SMEM), pl.BlockSpec(memory_space=pltpu.VMEM)]
        + [pl.BlockSpec(memory_space=pltpu.VMEM) for _ in after],
        out_specs=pl.BlockSpec(memory_space=pltpu.VMEM),
        out_shape=jax.ShapeDtypeStruct((rows, width), out_dtype),
        scratch_shapes=[pltpu.VMEM((32, width), src.dtype)],
        cost_estimate=pl.CostEstimate(
            flops=0, transcendentals=0, bytes_accessed=2 * rows * width * src.dtype.itemsize),
    )(idx, src, *after)


def with_zero_rows(flat):
    return jnp.concatenate([flat, jnp.zeros((8, flat.shape[1]), flat.dtype)], axis=0)


def a2a_kernel(x_ref, out_ref, held, send_sem, recv_sem, own_sem):
    n = x_ref.shape[0]
    me = lax.axis_index("tm")
    sky = lax.axis_index("sky")
    barrier = pltpu.get_barrier_semaphore()

    def greet(k, carry):
        peer = lax.rem(me + k, n)
        pl.semaphore_signal(barrier, inc=1, device_id=(peer, sky), device_id_type=pl.DeviceIdType.MESH)
        return carry

    lax.fori_loop(1, n, greet, 0)
    pl.semaphore_wait(barrier, n - 1)

    def copy(k):
        peer = lax.rem(me + k, n)
        return pltpu.make_async_remote_copy(
            src_ref=x_ref.at[peer],
            dst_ref=held.at[me],
            send_sem=send_sem.at[k],
            recv_sem=recv_sem.at[k],
            device_id=(peer, sky),
            device_id_type=pl.DeviceIdType.MESH,
        )

    def start(j, carry):
        odd = j % 2
        copy((1 - odd) * (j // 2 + 1) + odd * (n - 1 - j // 2)).start()
        return carry

    lax.fori_loop(0, n - 1, start, 0)
    own = pltpu.make_async_copy(x_ref.at[me], held.at[me], own_sem.at[0])
    own.start()

    def finish(k, carry):
        copy(k).wait()
        return carry

    lax.fori_loop(1, n, finish, 0)
    own.wait()
    out_ref[...] = held[...].astype(out_ref.dtype)


def tm_all_to_all(x, out_dtype, collective_id):
    n, rows, width = x.shape
    return pl.pallas_call(
        a2a_kernel,
        in_specs=[pl.BlockSpec(memory_space=pl.ANY)],
        out_specs=pl.BlockSpec(memory_space=pltpu.VMEM),
        out_shape=jax.ShapeDtypeStruct((n, rows, width), out_dtype),
        scratch_shapes=[
            pltpu.VMEM((n, rows, width), x.dtype),
            pltpu.SemaphoreType.DMA((n,)),
            pltpu.SemaphoreType.DMA((n,)),
            pltpu.SemaphoreType.DMA((1,)),
        ],
        compiler_params=pltpu.CompilerParams(collective_id=collective_id, has_side_effects=True),
    )(x)


STREAMS = 4
SUNROLL = 2

def scatter_add_kernel(idx_ref, src_ref, out_ref, acc_ref):
    rows = src_ref.shape[0]
    streams = acc_ref.shape[0]
    acc_ref[...] = jnp.zeros_like(acc_ref)

    def body(step, carry):
        base = step * streams
        for s in range(streams):
            r = base + s
            i = idx_ref[r]
            acc_ref[s, pl.ds(i, 1), :] = acc_ref[s, pl.ds(i, 1), :] + src_ref[pl.ds(r, 1), :]
        return carry

    lax.fori_loop(0, rows // streams, body, 0, unroll=SUNROLL)
    total = acc_ref[0]
    for s in range(1, streams):
        total = total + acc_ref[s]
    out_ref[...] = total[: out_ref.shape[0]]


def scatter_add(src, idx, out_rows):
    rows, width = src.shape
    pad = out_rows + 8
    return pl.pallas_call(
        scatter_add_kernel,
        in_specs=[pl.BlockSpec(memory_space=pltpu.SMEM), pl.BlockSpec(memory_space=pltpu.VMEM)],
        out_specs=pl.BlockSpec(memory_space=pltpu.VMEM),
        out_shape=jax.ShapeDtypeStruct((out_rows, width), jnp.float32),
        scratch_shapes=[pltpu.VMEM((STREAMS, pad, width), jnp.float32)],
        cost_estimate=pl.CostEstimate(flops=rows * width, transcendentals=0, bytes_accessed=(rows + out_rows) * width * 4),
    )(idx, src)


def fit_kernel(slot_ref, basis_ref, arrived_in, inc_ref, ins_ref, model_ref, ev_ref, stage_ref, arrived_ref):
    nper = inc_ref.shape[1]
    obs = stage_ref.shape[0]
    base = pl.program_id(0) * obs

    @pl.when(pl.program_id(0) == 0)
    def _():
        arrived_ref[...] = arrived_in[...].astype(jnp.float32)

    def pick(b, carry):
        r0 = pl.multiple_of(b * 32, 32)
        for j in range(32):
            stage_ref[pl.ds(r0 + j, 1), :] = arrived_ref[pl.ds(slot_ref[base + r0 + j], 1), :]
        return carry

    lax.fori_loop(0, obs // 32, pick, 0)
    basis = basis_ref[...]
    obs_t = stage_ref[...].T.astype(jnp.bfloat16)
    corr = jnp.dot(obs_t, basis, preferred_element_type=jnp.float32)
    cosine = corr[:, :nper]
    sine = corr[:, nper:]
    amp_c = cosine * inc_ref[...]
    amp_s = sine * ins_ref[...]
    logits = BETA * (cosine * amp_c + sine * amp_s)
    highest = jnp.max(logits, axis=1, keepdims=True)
    expo = jnp.exp(logits - highest)
    total = jnp.sum(expo, axis=1, keepdims=True)
    share = expo * (1.0 / total)
    coeff = jnp.concatenate([share * amp_c, share * amp_s], axis=1).astype(jnp.bfloat16)
    model_ref[...] = lax.dot_general(
        basis, coeff, (((1,), (1,)), ((), ())), preferred_element_type=jnp.float32)
    ev_ref[...] = highest + jnp.log(total)


def fit_fused(basis, arrived, slot_of, inv_cos, inv_sin):
    plans, obs, width = basis.shape
    cols = arrived.shape[1]
    nper = width // 2
    row = pl.BlockSpec((None, 1, nper), lambda g, s: (g, 0, 0))
    model, ev = pl.pallas_call(
        fit_kernel,
        grid_spec=pltpu.PrefetchScalarGridSpec(
            num_scalar_prefetch=1,
            grid=(plans,),
            in_specs=[
                pl.BlockSpec((None, obs, width), lambda g, s: (g, 0, 0)),
                pl.BlockSpec(arrived.shape, lambda g, s: (0, 0)),
                row,
                row,
            ],
            out_specs=[
                pl.BlockSpec((None, obs, cols), lambda g, s: (g, 0, 0)),
                pl.BlockSpec((None, cols, 1), lambda g, s: (g, 0, 0)),
            ],
            scratch_shapes=[pltpu.VMEM((obs, cols), jnp.float32), pltpu.VMEM(arrived.shape, jnp.float32)],
        ),
        out_shape=[
            jax.ShapeDtypeStruct((plans, obs, cols), jnp.float32),
            jax.ShapeDtypeStruct((plans, cols, 1), jnp.float32),
        ],
        cost_estimate=pl.CostEstimate(
            flops=4 * plans * obs * width * cols, transcendentals=plans * nper * cols,
            bytes_accessed=plans * obs * width * 2),
    )(slot_of, basis, arrived, inv_cos, inv_sin)
    return model, ev.reshape(plans, cols)


def white_kernel(cnt_ref, cur_hbm, att_hbm, out_ref, cur_ref, att_ref, sems):
    segs, slots, _ = att_ref.shape
    width = out_ref.shape[1]
    blocks = cur_ref.shape[1] // width

    def copies(s):
        rows = pl.ds(s * slots, slots)
        return (
            pltpu.make_async_copy(cur_hbm.at[rows], cur_ref.at[rows], sems.at[0, s]),
            pltpu.make_async_copy(att_hbm.at[s], att_ref.at[s], sems.at[1, s]),
        )

    for s in range(segs):
        for c in copies(s):
            c.start()
    for s in range(segs):
        for c in copies(s):
            c.wait()
        cur = cur_ref[pl.ds(s * slots, slots), :]
        slot = lax.broadcasted_iota(jnp.int32, cur.shape, 0)
        masked = jnp.where(slot < cnt_ref[s], cur, 0.0).astype(jnp.bfloat16)
        white = jnp.dot(att_ref[s], masked, preferred_element_type=jnp.float32)
        for b in range(blocks):
            out_ref[pl.ds(b * segs * slots + s * slots, slots), :] = white[:, b * width:(b + 1) * width]
    out_ref[pl.ds(blocks * segs * slots, 8), :] = jnp.zeros((8, width), jnp.float32)


def whiten_rows(counts, current, attitude_all, width):
    segs, slots, _ = attitude_all.shape
    rows = current.shape[0] * current.shape[1] // width
    return pl.pallas_call(
        white_kernel,
        in_specs=[pl.BlockSpec(memory_space=pltpu.SMEM)] + [pl.BlockSpec(memory_space=pl.ANY)] * 2,
        out_specs=pl.BlockSpec(memory_space=pltpu.VMEM),
        out_shape=jax.ShapeDtypeStruct((rows + 8, width), jnp.float32),
        scratch_shapes=[
            pltpu.VMEM(current.shape, current.dtype),
            pltpu.VMEM(attitude_all.shape, attitude_all.dtype),
            pltpu.SemaphoreType.DMA((2, segs)),
        ],
        cost_estimate=pl.CostEstimate(
            flops=2 * segs * slots * slots * current.shape[1], transcendentals=0,
            bytes_accessed=current.size * 8 + attitude_all.size * 2),
    )(counts, current, attitude_all)


def scatter_sub_kernel(idx_ref, src_in, cur_ref, out_ref, acc_ref, src_ref):
    rows, width = src_ref.shape
    streams = acc_ref.shape[0]
    n = cur_ref.shape[0]
    src_ref[...] = src_in[...].astype(jnp.float32)
    acc_ref[...] = jnp.zeros_like(acc_ref)

    def body(step, carry):
        base = step * streams
        for s in range(streams):
            r = base + s
            i = idx_ref[r]
            acc_ref[s, pl.ds(i, 1), :] = acc_ref[s, pl.ds(i, 1), :] + src_ref[pl.ds(r, 1), :]
        return carry

    lax.fori_loop(0, rows // streams, body, 0, unroll=SUNROLL)
    for b in range(cur_ref.shape[1] // width):
        total = acc_ref[0, pl.ds(b * n, n), :]
        for s in range(1, streams):
            total = total + acc_ref[s, pl.ds(b * n, n), :]
        out_ref[:, b * width:(b + 1) * width] = cur_ref[:, b * width:(b + 1) * width] - total


def scatter_sub(src, idx, current):
    rows, width = src.shape
    blocks = current.shape[1] // width
    return pl.pallas_call(
        scatter_sub_kernel,
        in_specs=[pl.BlockSpec(memory_space=pltpu.SMEM)] + [pl.BlockSpec(memory_space=pltpu.VMEM)] * 2,
        out_specs=pl.BlockSpec(memory_space=pltpu.VMEM),
        out_shape=jax.ShapeDtypeStruct(current.shape, jnp.float32),
        scratch_shapes=[pltpu.VMEM((STREAMS, blocks * current.shape[0] + 8, width), jnp.float32),
                        pltpu.VMEM(src.shape, jnp.float32)],
        cost_estimate=pl.CostEstimate(
            flops=rows * width, transcendentals=0, bytes_accessed=(rows * width + 2 * current.size) * 4),
    )(idx, src, current)

def fit_groups(basis, observed, norm_cos, norm_sin, nper):
    corr = jnp.einsum("fio,fic->foc", basis, observed, preferred_element_type=jnp.float32)
    cosine = corr[:, :nper]
    sine = corr[:, nper:]
    amp_c = cosine / norm_cos[:, :, None]
    amp_s = sine / norm_sin[:, :, None]
    power = cosine * amp_c + sine * amp_s
    logits = BETA * power
    highest = jnp.max(logits, axis=1)
    expo = jnp.exp(logits - highest[:, None, :])
    total = jnp.sum(expo, axis=1)
    share = expo / total[:, None, :]
    coeff = jnp.concatenate([share * amp_c, share * amp_s], axis=1).astype(jnp.bfloat16)
    model = jnp.einsum("fio,foc->fic", basis, coeff, preferred_element_type=jnp.float32)
    return (model, highest + jnp.log(total))


def on_device(residuals, seg_counts, attitude, sched_seg, sched_slot, periods):
    tm_count = lax.axis_size("tm")
    sched_dev, obs = sched_seg.shape
    seg_dev, slots, width = residuals.shape
    nper = periods.shape[0]
    column_blocks = width // SRC_GROUP
    capacity = 2 * sched_dev * obs // tm_count
    requests = sched_dev * obs
    seg_flat = sched_seg.reshape(-1)
    slot_flat = sched_slot.reshape(-1)
    block_of = jnp.repeat(jnp.arange(sched_dev, dtype=jnp.int32) % column_blocks, obs)
    target = seg_flat // seg_dev
    local_row = block_of * (seg_dev * slots) + seg_flat % seg_dev * slots + slot_flat
    onehot = (target[:, None] == jnp.arange(tm_count, dtype=jnp.int32)[None, :]).astype(jnp.int32)
    ones = onehot.astype(jnp.bfloat16).reshape(requests // 128, 128, tm_count)
    tril = (jnp.arange(128)[:, None] >= jnp.arange(128)[None, :]).astype(jnp.bfloat16)
    within = jnp.einsum("ij,bjc->bic", tril, ones, preferred_element_type=jnp.float32)
    totals = within[:, -1, :]
    before = jnp.cumsum(totals, axis=0) - totals
    counts = (within + before[:, None, :]).reshape(requests, tm_count)
    position = jnp.sum(counts * onehot.astype(jnp.float32), axis=1).astype(jnp.int32) - 1
    empty_row = seg_dev * slots * column_blocks
    slot_of = target * capacity + position
    pair = (
        jnp.broadcast_to(jnp.array([empty_row, 0], jnp.int32), (tm_count * capacity, 2))
        .at[slot_of]
        .set(jnp.stack([local_row, jnp.arange(requests, dtype=jnp.int32)], axis=1))
    )
    wanted = pair[:, 0].reshape(tm_count, capacity)
    inverse = pair[:, 1]
    asked = lax.all_to_all(wanted, "tm", split_axis=0, concat_axis=0, tiled=True).reshape(-1)
    basis, norm_cos, norm_sin = basis_and_norms(sched_seg * slots + sched_slot, periods)
    valid = jnp.arange(slots, dtype=jnp.int32)[None, :] < seg_counts[:, None]
    inv_cos = (1.0 / norm_cos).reshape(sched_dev, 1, nper)
    inv_sin = (1.0 / norm_sin).reshape(sched_dev, 1, nper)
    current = residuals.astype(jnp.float32).reshape(seg_dev * slots, width)
    evidence = jnp.zeros((sched_dev, SRC_GROUP), jnp.float32)
    attitude_all = lax.all_gather(attitude, "sky", axis=1, tiled=True)
    for iteration in range(ITERS):
        white = whiten_rows(seg_counts, current, attitude_all, SRC_GROUP)
        picked = row_gather(white, asked, jnp.bfloat16, norm_cos)
        outbound = picked.reshape(tm_count, capacity, SRC_GROUP)
        arrived = tm_all_to_all(outbound, jnp.bfloat16, 1 + 2 * iteration)
        model, evidence = fit_fused(
            basis, arrived.reshape(-1, SRC_GROUP), slot_of, inv_cos, inv_sin)
        outgoing = row_gather(model.reshape(requests, SRC_GROUP), inverse, jnp.bfloat16)
        returned = tm_all_to_all(
            outgoing.reshape(tm_count, capacity, SRC_GROUP),
            jnp.bfloat16, 2 + 2 * iteration)
        current = scatter_sub(returned.reshape(-1, SRC_GROUP), asked, current)
    current = current.reshape(seg_dev, slots, width)
    return (current, evidence)


def solution(mesh):
    in_specs = (
        P("tm", None, "sky"),
        P("tm"),
        P("tm", "sky", None),
        P(("tm", "sky"), None),
        P(("tm", "sky"), None),
        P(),
    )
    out_specs = (P("tm", None, "sky"), P(("tm", "sky"), None))
    return jax.shard_map(
        on_device, mesh=mesh, in_specs=in_specs, out_specs=out_specs, check_vma=False
    )
```

```python
import jax
import jax.numpy as jnp
from jax import lax
from jax.experimental import pallas as pl
from jax.experimental.pallas import tpu as pltpu
from jax.sharding import PartitionSpec as P

SRC_GROUP = 128
ITERS = 2


TWO_PI = 6.283185307179586
BETA = 2.0
RIDGE = 1.0


PIO2_1 = 1.5703125
PIO2_2 = 4.837512969970703125e-4
PIO2_3 = 7.549789954891e-8
ROWS = 16
LANES = 512
UNROLL = 2


def basis_kernel(t_ref, p_ref, w_ref, inv_ref, basis_ref, nc_ref, ns_ref):
    obs = t_ref.shape[0]
    nper = p_ref.shape[1]

    def lane_block(j, carry):
        c0 = pl.multiple_of(j * LANES, LANES)
        pf = p_ref[:, pl.ds(c0, LANES)]
        w = w_ref[:, pl.ds(c0, LANES)]
        inv = inv_ref[:, pl.ds(c0, LANES)]

        def row_block(i, acc):
            acc_c, acc_s = acc
            r0 = pl.multiple_of(i * ROWS, ROWS)
            tf = jnp.broadcast_to(t_ref[pl.ds(r0, ROWS), :], (ROWS, LANES))
            q = jnp.floor(tf * inv)
            r = tf - q * pf
            r = jnp.where(r < 0.0, r + pf, r)
            r = jnp.where(r >= pf, r - pf, r)
            phase = r * w
            k = jnp.floor(phase * 0.6366197723675814 + 0.5)
            y = ((phase - k * PIO2_1) - k * PIO2_2) - k * PIO2_3
            z = y * y
            s = y + y * z * (-1.6666654611e-1 + z * (8.3321608736e-3 + z * -1.9515295891e-4))
            c = 1.0 - 0.5 * z + z * z * (4.166664568298827e-2 + z * (-1.388731625493765e-3 + z * 2.443315711809948e-5))
            odd = (k == 1.0) | (k == 3.0)
            cs = jnp.where(odd, s, c)
            sn = jnp.where(odd, c, s)
            cos_v = jnp.where((k == 1.0) | (k == 2.0), -cs, cs).astype(jnp.bfloat16)
            sin_v = jnp.where((k == 2.0) | (k == 3.0), -sn, sn).astype(jnp.bfloat16)
            basis_ref[pl.ds(r0, ROWS), pl.ds(c0, LANES)] = cos_v
            basis_ref[pl.ds(r0, ROWS), pl.ds(nper + c0, LANES)] = sin_v
            cf = cos_v.astype(jnp.float32)
            sf = sin_v.astype(jnp.float32)
            return acc_c + cf * cf, acc_s + sf * sf

        zero = jnp.zeros((ROWS, LANES), jnp.float32)
        acc_c, acc_s = lax.fori_loop(0, obs // ROWS, row_block, (zero, zero), unroll=UNROLL)
        nc_ref[:, pl.ds(c0, LANES)] = jnp.sum(acc_c, axis=0, keepdims=True) + RIDGE
        ns_ref[:, pl.ds(c0, LANES)] = jnp.sum(acc_s, axis=0, keepdims=True) + RIDGE
        return carry

    lax.fori_loop(0, nper // LANES, lane_block, 0)


def basis_and_norms(times, periods):
    plans, obs = times.shape
    nper = periods.shape[0]
    pf = periods.astype(jnp.float32)
    w = (TWO_PI / pf).reshape(1, nper)
    inv = (1.0 / pf).reshape(1, nper)
    pf = pf.reshape(1, nper)
    tf = times.astype(jnp.float32).reshape(plans, obs, 1)
    row = pl.BlockSpec((1, nper), lambda g: (0, 0))
    basis, nc, ns = pl.pallas_call(
        basis_kernel,
        grid=(plans,),
        in_specs=[pl.BlockSpec((None, obs, 1), lambda g: (g, 0, 0)), row, row, row],
        out_specs=[
            pl.BlockSpec((None, obs, 2 * nper), lambda g: (g, 0, 0)),
            pl.BlockSpec((None, 1, nper), lambda g: (g, 0, 0)),
            pl.BlockSpec((None, 1, nper), lambda g: (g, 0, 0)),
        ],
        out_shape=[
            jax.ShapeDtypeStruct((plans, obs, 2 * nper), jnp.bfloat16),
            jax.ShapeDtypeStruct((plans, 1, nper), jnp.float32),
            jax.ShapeDtypeStruct((plans, 1, nper), jnp.float32),
        ],
        cost_estimate=pl.CostEstimate(
            flops=60 * plans * obs * nper, transcendentals=0,
            bytes_accessed=plans * obs * 2 * nper * 2),
    )(tf, pf, w, inv)
    return basis, nc.reshape(plans, nper), ns.reshape(plans, nper)


def gather_kernel(idx_ref, src_ref, *rest):
    out_ref = rest[-2]
    stage_ref = rest[-1]
    block = stage_ref.shape[0]

    def body(b, carry):
        r0 = pl.multiple_of(b * block, block)
        for j in range(block):
            stage_ref[pl.ds(j, 1), :] = src_ref[pl.ds(idx_ref[r0 + j], 1), :]
        out_ref[pl.ds(r0, block), :] = stage_ref[...].astype(out_ref.dtype)
        return carry

    lax.fori_loop(0, out_ref.shape[0] // block, body, 0)


def row_gather(src, idx, out_dtype, *after):
    rows, width = idx.shape[0], src.shape[1]
    return pl.pallas_call(
        gather_kernel,
        in_specs=[pl.BlockSpec(memory_space=pltpu.SMEM), pl.BlockSpec(memory_space=pltpu.VMEM)]
        + [pl.BlockSpec(memory_space=pltpu.VMEM) for _ in after],
        out_specs=pl.BlockSpec(memory_space=pltpu.VMEM),
        out_shape=jax.ShapeDtypeStruct((rows, width), out_dtype),
        scratch_shapes=[pltpu.VMEM((32, width), src.dtype)],
        cost_estimate=pl.CostEstimate(
            flops=0, transcendentals=0, bytes_accessed=2 * rows * width * src.dtype.itemsize),
    )(idx, src, *after)


def with_zero_rows(flat):
    return jnp.concatenate([flat, jnp.zeros((8, flat.shape[1]), flat.dtype)], axis=0)


def a2a_kernel(x_ref, out_ref, held, send_sem, recv_sem, own_sem):
    n = x_ref.shape[0]
    me = lax.axis_index("tm")
    sky = lax.axis_index("sky")
    barrier = pltpu.get_barrier_semaphore()

    def greet(k, carry):
        peer = lax.rem(me + k, n)
        pl.semaphore_signal(barrier, inc=1, device_id=(peer, sky), device_id_type=pl.DeviceIdType.MESH)
        return carry

    lax.fori_loop(1, n, greet, 0)
    pl.semaphore_wait(barrier, n - 1)

    def copy(k):
        peer = lax.rem(me + k, n)
        return pltpu.make_async_remote_copy(
            src_ref=x_ref.at[peer],
            dst_ref=held.at[me],
            send_sem=send_sem.at[k],
            recv_sem=recv_sem.at[k],
            device_id=(peer, sky),
            device_id_type=pl.DeviceIdType.MESH,
        )

    def start(j, carry):
        odd = j % 2
        copy((1 - odd) * (j // 2 + 1) + odd * (n - 1 - j // 2)).start()
        return carry

    lax.fori_loop(0, n - 1, start, 0)
    own = pltpu.make_async_copy(x_ref.at[me], held.at[me], own_sem.at[0])
    own.start()

    def finish(k, carry):
        copy(k).wait()
        return carry

    lax.fori_loop(1, n, finish, 0)
    own.wait()
    out_ref[...] = held[...].astype(out_ref.dtype)


def tm_all_to_all(x, out_dtype, collective_id):
    n, rows, width = x.shape
    return pl.pallas_call(
        a2a_kernel,
        in_specs=[pl.BlockSpec(memory_space=pl.ANY)],
        out_specs=pl.BlockSpec(memory_space=pltpu.VMEM),
        out_shape=jax.ShapeDtypeStruct((n, rows, width), out_dtype),
        scratch_shapes=[
            pltpu.VMEM((n, rows, width), x.dtype),
            pltpu.SemaphoreType.DMA((n,)),
            pltpu.SemaphoreType.DMA((n,)),
            pltpu.SemaphoreType.DMA((1,)),
        ],
        compiler_params=pltpu.CompilerParams(collective_id=collective_id, has_side_effects=True),
    )(x)


STREAMS = 4
SUNROLL = 2

def scatter_add_kernel(idx_ref, src_ref, out_ref, acc_ref):
    rows = src_ref.shape[0]
    streams = acc_ref.shape[0]
    acc_ref[...] = jnp.zeros_like(acc_ref)

    def body(step, carry):
        base = step * streams
        for s in range(streams):
            r = base + s
            i = idx_ref[r]
            acc_ref[s, pl.ds(i, 1), :] = acc_ref[s, pl.ds(i, 1), :] + src_ref[pl.ds(r, 1), :]
        return carry

    lax.fori_loop(0, rows // streams, body, 0, unroll=SUNROLL)
    total = acc_ref[0]
    for s in range(1, streams):
        total = total + acc_ref[s]
    out_ref[...] = total[: out_ref.shape[0]]


def scatter_add(src, idx, out_rows):
    rows, width = src.shape
    pad = out_rows + 8
    return pl.pallas_call(
        scatter_add_kernel,
        in_specs=[pl.BlockSpec(memory_space=pltpu.SMEM), pl.BlockSpec(memory_space=pltpu.VMEM)],
        out_specs=pl.BlockSpec(memory_space=pltpu.VMEM),
        out_shape=jax.ShapeDtypeStruct((out_rows, width), jnp.float32),
        scratch_shapes=[pltpu.VMEM((STREAMS, pad, width), jnp.float32)],
        cost_estimate=pl.CostEstimate(flops=rows * width, transcendentals=0, bytes_accessed=(rows + out_rows) * width * 4),
    )(idx, src)


def fit_kernel(slot_ref, basis_ref, arrived_in, inc_ref, ins_ref, model_ref, ev_ref, stage_ref, arrived_ref):
    nper = inc_ref.shape[1]
    obs = stage_ref.shape[0]
    base = pl.program_id(0) * obs

    @pl.when(pl.program_id(0) == 0)
    def _():
        arrived_ref[...] = arrived_in[...].astype(jnp.float32)

    def pick(b, carry):
        r0 = pl.multiple_of(b * 32, 32)
        for j in range(32):
            stage_ref[pl.ds(r0 + j, 1), :] = arrived_ref[pl.ds(slot_ref[base + r0 + j], 1), :]
        return carry

    lax.fori_loop(0, obs // 32, pick, 0)
    basis = basis_ref[...]
    obs_t = stage_ref[...].T.astype(jnp.bfloat16)
    corr = jnp.dot(obs_t, basis, preferred_element_type=jnp.float32)
    cosine = corr[:, :nper]
    sine = corr[:, nper:]
    amp_c = cosine * inc_ref[...]
    amp_s = sine * ins_ref[...]
    logits = BETA * (cosine * amp_c + sine * amp_s)
    highest = jnp.max(logits, axis=1, keepdims=True)
    expo = jnp.exp(logits - highest)
    total = jnp.sum(expo, axis=1, keepdims=True)
    share = expo * (1.0 / total)
    coeff = jnp.concatenate([share * amp_c, share * amp_s], axis=1).astype(jnp.bfloat16)
    model_ref[...] = lax.dot_general(
        basis, coeff, (((1,), (1,)), ((), ())), preferred_element_type=jnp.float32)
    ev_ref[...] = highest + jnp.log(total)


def fit_fused(basis, arrived, slot_of, inv_cos, inv_sin):
    plans, obs, width = basis.shape
    cols = arrived.shape[1]
    nper = width // 2
    row = pl.BlockSpec((None, 1, nper), lambda g, s: (g, 0, 0))
    model, ev = pl.pallas_call(
        fit_kernel,
        grid_spec=pltpu.PrefetchScalarGridSpec(
            num_scalar_prefetch=1,
            grid=(plans,),
            in_specs=[
                pl.BlockSpec((None, obs, width), lambda g, s: (g, 0, 0)),
                pl.BlockSpec(arrived.shape, lambda g, s: (0, 0)),
                row,
                row,
            ],
            out_specs=[
                pl.BlockSpec((None, obs, cols), lambda g, s: (g, 0, 0)),
                pl.BlockSpec((None, cols, 1), lambda g, s: (g, 0, 0)),
            ],
            scratch_shapes=[pltpu.VMEM((obs, cols), jnp.float32), pltpu.VMEM(arrived.shape, jnp.float32)],
        ),
        out_shape=[
            jax.ShapeDtypeStruct((plans, obs, cols), jnp.float32),
            jax.ShapeDtypeStruct((plans, cols, 1), jnp.float32),
        ],
        cost_estimate=pl.CostEstimate(
            flops=4 * plans * obs * width * cols, transcendentals=plans * nper * cols,
            bytes_accessed=plans * obs * width * 2),
    )(slot_of, basis, arrived, inv_cos, inv_sin)
    return model, ev.reshape(plans, cols)


def white_kernel(cnt_ref, cur_ref, att_ref, out_ref):
    segs, slots, _ = att_ref.shape
    width = out_ref.shape[1]
    blocks = cur_ref.shape[1] // width
    for s in range(segs):
        cur = cur_ref[pl.ds(s * slots, slots), :]
        slot = lax.broadcasted_iota(jnp.int32, cur.shape, 0)
        masked = jnp.where(slot < cnt_ref[s], cur, 0.0).astype(jnp.bfloat16)
        white = jnp.dot(att_ref[s], masked, preferred_element_type=jnp.float32)
        for b in range(blocks):
            out_ref[pl.ds(b * segs * slots + s * slots, slots), :] = white[:, b * width:(b + 1) * width]
    out_ref[pl.ds(blocks * segs * slots, 8), :] = jnp.zeros((8, width), jnp.float32)


def whiten_rows(counts, current, attitude_all, width):
    segs, slots, _ = attitude_all.shape
    rows = current.shape[0] * current.shape[1] // width
    return pl.pallas_call(
        white_kernel,
        in_specs=[pl.BlockSpec(memory_space=pltpu.SMEM)] + [pl.BlockSpec(memory_space=pltpu.VMEM)] * 2,
        out_specs=pl.BlockSpec(memory_space=pltpu.VMEM),
        out_shape=jax.ShapeDtypeStruct((rows + 8, width), jnp.float32),
        cost_estimate=pl.CostEstimate(
            flops=2 * segs * slots * slots * current.shape[1], transcendentals=0,
            bytes_accessed=current.size * 8 + attitude_all.size * 2),
    )(counts, current, attitude_all)


def scatter_sub_kernel(idx_ref, src_hbm, cur_hbm, out_ref, acc_ref, src_ref, src_in, cur_ref, sems):
    rows, width = src_ref.shape
    streams = acc_ref.shape[0]
    n = cur_ref.shape[0]
    src_copy = pltpu.make_async_copy(src_hbm, src_in, sems.at[0])
    cur_copy = pltpu.make_async_copy(cur_hbm, cur_ref, sems.at[1])
    src_copy.start()
    cur_copy.start()
    acc_ref[...] = jnp.zeros_like(acc_ref)
    src_copy.wait()
    src_ref[...] = src_in[...].astype(jnp.float32)

    def body(step, carry):
        base = step * streams
        for s in range(streams):
            r = base + s
            i = idx_ref[r]
            acc_ref[s, pl.ds(i, 1), :] = acc_ref[s, pl.ds(i, 1), :] + src_ref[pl.ds(r, 1), :]
        return carry

    lax.fori_loop(0, rows // streams, body, 0, unroll=SUNROLL)
    cur_copy.wait()
    for b in range(cur_ref.shape[1] // width):
        total = acc_ref[0, pl.ds(b * n, n), :]
        for s in range(1, streams):
            total = total + acc_ref[s, pl.ds(b * n, n), :]
        out_ref[:, b * width:(b + 1) * width] = cur_ref[:, b * width:(b + 1) * width] - total


def scatter_sub(src, idx, current):
    rows, width = src.shape
    blocks = current.shape[1] // width
    return pl.pallas_call(
        scatter_sub_kernel,
        in_specs=[pl.BlockSpec(memory_space=pltpu.SMEM)] + [pl.BlockSpec(memory_space=pl.ANY)] * 2,
        out_specs=pl.BlockSpec(memory_space=pltpu.VMEM),
        out_shape=jax.ShapeDtypeStruct(current.shape, jnp.float32),
        scratch_shapes=[pltpu.VMEM((STREAMS, blocks * current.shape[0] + 8, width), jnp.float32),
                        pltpu.VMEM(src.shape, jnp.float32), pltpu.VMEM(src.shape, src.dtype),
                        pltpu.VMEM(current.shape, current.dtype), pltpu.SemaphoreType.DMA((2,))],
        cost_estimate=pl.CostEstimate(
            flops=rows * width, transcendentals=0, bytes_accessed=(rows * width + 2 * current.size) * 4),
    )(idx, src, current)

def fit_groups(basis, observed, norm_cos, norm_sin, nper):
    corr = jnp.einsum("fio,fic->foc", basis, observed, preferred_element_type=jnp.float32)
    cosine = corr[:, :nper]
    sine = corr[:, nper:]
    amp_c = cosine / norm_cos[:, :, None]
    amp_s = sine / norm_sin[:, :, None]
    power = cosine * amp_c + sine * amp_s
    logits = BETA * power
    highest = jnp.max(logits, axis=1)
    expo = jnp.exp(logits - highest[:, None, :])
    total = jnp.sum(expo, axis=1)
    share = expo / total[:, None, :]
    coeff = jnp.concatenate([share * amp_c, share * amp_s], axis=1).astype(jnp.bfloat16)
    model = jnp.einsum("fio,foc->fic", basis, coeff, preferred_element_type=jnp.float32)
    return (model, highest + jnp.log(total))


def on_device(residuals, seg_counts, attitude, sched_seg, sched_slot, periods):
    tm_count = lax.axis_size("tm")
    sched_dev, obs = sched_seg.shape
    seg_dev, slots, width = residuals.shape
    nper = periods.shape[0]
    column_blocks = width // SRC_GROUP
    capacity = 2 * sched_dev * obs // tm_count
    requests = sched_dev * obs
    seg_flat = sched_seg.reshape(-1)
    slot_flat = sched_slot.reshape(-1)
    block_of = jnp.repeat(jnp.arange(sched_dev, dtype=jnp.int32) % column_blocks, obs)
    target = seg_flat // seg_dev
    local_row = block_of * (seg_dev * slots) + seg_flat % seg_dev * slots + slot_flat
    onehot = (target[:, None] == jnp.arange(tm_count, dtype=jnp.int32)[None, :]).astype(jnp.int32)
    ones = onehot.astype(jnp.bfloat16).reshape(requests // 128, 128, tm_count)
    tril = (jnp.arange(128)[:, None] >= jnp.arange(128)[None, :]).astype(jnp.bfloat16)
    within = jnp.einsum("ij,bjc->bic", tril, ones, preferred_element_type=jnp.float32)
    totals = within[:, -1, :]
    before = jnp.cumsum(totals, axis=0) - totals
    counts = (within + before[:, None, :]).reshape(requests, tm_count)
    position = jnp.sum(counts * onehot.astype(jnp.float32), axis=1).astype(jnp.int32) - 1
    empty_row = seg_dev * slots * column_blocks
    slot_of = target * capacity + position
    pair = (
        jnp.broadcast_to(jnp.array([empty_row, 0], jnp.int32), (tm_count * capacity, 2))
        .at[slot_of]
        .set(jnp.stack([local_row, jnp.arange(requests, dtype=jnp.int32)], axis=1))
    )
    wanted = pair[:, 0].reshape(tm_count, capacity)
    inverse = pair[:, 1]
    asked = lax.all_to_all(wanted, "tm", split_axis=0, concat_axis=0, tiled=True).reshape(-1)
    basis, norm_cos, norm_sin = basis_and_norms(sched_seg * slots + sched_slot, periods)
    valid = jnp.arange(slots, dtype=jnp.int32)[None, :] < seg_counts[:, None]
    inv_cos = (1.0 / norm_cos).reshape(sched_dev, 1, nper)
    inv_sin = (1.0 / norm_sin).reshape(sched_dev, 1, nper)
    current = residuals.astype(jnp.float32).reshape(seg_dev * slots, width)
    evidence = jnp.zeros((sched_dev, SRC_GROUP), jnp.float32)
    attitude_all = lax.all_gather(attitude, "sky", axis=1, tiled=True)
    for iteration in range(ITERS):
        white = whiten_rows(seg_counts, current, attitude_all, SRC_GROUP)
        picked = row_gather(white, asked, jnp.bfloat16, norm_cos)
        outbound = picked.reshape(tm_count, capacity, SRC_GROUP)
        arrived = tm_all_to_all(outbound, jnp.bfloat16, 1 + 2 * iteration)
        model, evidence = fit_fused(
            basis, arrived.reshape(-1, SRC_GROUP), slot_of, inv_cos, inv_sin)
        outgoing = row_gather(model.reshape(requests, SRC_GROUP), inverse, jnp.bfloat16)
        returned = tm_all_to_all(
            outgoing.reshape(tm_count, capacity, SRC_GROUP),
            jnp.bfloat16, 2 + 2 * iteration)
        current = scatter_sub(returned.reshape(-1, SRC_GROUP), asked, current)
    current = current.reshape(seg_dev, slots, width)
    return (current, evidence)


def solution(mesh):
    in_specs = (
        P("tm", None, "sky"),
        P("tm"),
        P("tm", "sky", None),
        P(("tm", "sky"), None),
        P(("tm", "sky"), None),
        P(),
    )
    out_specs = (P("tm", None, "sky"), P(("tm", "sky"), None))
    return jax.shard_map(
        on_device, mesh=mesh, in_specs=in_specs, out_specs=out_specs, check_vma=False
    )
```
